256 devices in a mesh: dp: 32 (over x, z), expert: 8 (over y, core).
Axes of the slice: x: 4, y: 4, z: 8, core: 2. Of those that a mesh axis runs over, the one named last changes fastest.
Arguments:
- text_embed: bfloat16 [16384, 2048], P(('dp', 'expert')), may hold values from -6 to 6
- image_feats: bfloat16 [8192, 4608], P(('dp', 'expert')), may hold values from -6 to 6
- tile_pos: int32 [8192], P(('dp', 'expert')), may hold values from 0 to 16383, as said below
- proj_in: bfloat16 [4608, 2048], P(None, 'expert'), may hold values from -0.09375 to 0.09375
- proj_out: bfloat16 [2048, 2048], P('expert'), may hold values from -0.125 to 0.125
- norm_gain: float32 [2048], replicated, may hold values from 0.1 to 1.9
- shared_gate: bfloat16 [2048, 2816], P(None, 'expert'), may hold values from -0.125 to 0.125
- shared_up: bfloat16 [2048, 2816], P(None, 'expert'), may hold values from -0.125 to 0.125
- shared_down: bfloat16 [2816, 2048], P('expert'), may hold values from -0.109375 to 0.109375
- expert_gate: bfloat16 [32, 2048, 1408], P('dp', None, 'expert'), may hold values from -0.125 to 0.125
- expert_up: bfloat16 [32, 2048, 1408], P('dp', None, 'expert'), may hold values from -0.125 to 0.125
- expert_down: bfloat16 [32, 1408, 2048], P('dp', 'expert'), may hold values from -0.15625 to 0.15625
- route_ids: int32 [16384, 2], P(('dp', 'expert')), may hold values from 0 to 31, all different within a row; in each aligned block of 512 rows (0 to 511, 512 to 1023, ...) at most 48 rows name the same one
- route_wts: int32 [16384, 2], P(('dp', 'expert')), may hold values from 1 to 65535
Outputs:
- block_out: bfloat16 [16384, 2048], P(('dp', 'expert'))
The draws below stay inside these ranges and needn't reach their ends.
Inputs may be any that keep to these rules, and one draw needn't show every extreme that they name: `tile_pos`: positions are distinct. The 32 image tokens of one device go 1 to each index of dp, always to rows held by the devices with the sender's own index of expert. `route_ids`: in each aligned block of 512 rows no expert is named by more than 48 rows, a bound that some block reaches.
All inputs are finite; a program needn't handle non-finite values.
Results may differ from the reference program's by a relative error of at most 0.018.
Values may be sent and summed in bfloat16 or wider, within the bound.
A program may use at most 128 MiB of HBM per device.

```python
import math
import jax
import jax.numpy as jnp
import numpy as np
from jax import lax

D = 2048
VIS = 4608
FF = 1408
FFS = 2816
TOP = 2
TOK_DEV = 64
IMG_DEV = 32
EXPERTS = 32
GROUP_TOK = 512
CAP = 48
TOKENS = 16384
IMG_TOKENS = 8192
N_DP = 32
N_EXPERT = 8


def draw_tile_pos(key, part):
    peer = IMG_DEV // N_DP
    ndev = N_DP * N_EXPERT
    key_a = jax.random.fold_in(key, 11)
    key_b = jax.random.fold_in(key, 12)
    chosen = jax.vmap(lambda k: jax.random.permutation(k, TOK_DEV))(jax.random.split(key_a, ndev))[:, :IMG_DEV]
    chosen = chosen.astype(jnp.int32).reshape(N_DP, N_EXPERT, N_DP, peer)
    base = (jnp.arange(N_DP, dtype=jnp.int32)[:, None] * N_EXPERT + jnp.arange(N_EXPERT, dtype=jnp.int32)[None, :]) * TOK_DEV
    position = chosen + base[:, :, None, None]
    position = jnp.transpose(position, (2, 1, 0, 3)).reshape(ndev, IMG_DEV)
    shuffle = jax.vmap(lambda k: jax.random.permutation(k, IMG_DEV))(jax.random.split(key_b, ndev))
    position = jnp.take_along_axis(position, shuffle.astype(jnp.int32), axis=1)
    return position.reshape(-1).astype(jnp.int32)


def plant(values, stream_key, low, top_value):
    extent = values.shape
    index_at = [jax.random.randint(jax.random.fold_in(stream_key, axis), (), 0, extent[axis]) for axis in range(len(extent))]
    values = values.at[tuple(index_at)].set(low)
    longest = extent.index(max(extent))
    index_at[longest] = (index_at[longest] + 1) % extent[longest]
    return values.at[tuple(index_at)].set(top_value)


def shard_levels(key, shape, cuts, smallest, high):
    factor_of, own = 1.0, jax.random.fold_in(key, 6)
    for dim, shards_of in cuts:
        heights = jnp.exp(jax.random.uniform(jax.random.fold_in(own, dim), (shards_of,), jnp.float32, smallest / len(cuts), high / len(cuts)))
        factor_of = factor_of * jnp.repeat(heights, shape[dim] // shards_of).reshape([-1 if axis == dim else 1 for axis in range(len(shape))])
    return factor_of


def routed_block(key, own, number, rows, number_of, top, reach, slope):
    sequence = jax.random.permutation(key, number_of)
    crowded, common = load_shares(number_of, rows * top, reach, slope, True), load_shares(number_of, rows * top, reach, slope, False)
    places = jnp.arange(number_of)

    def named(sizes, rotation):
        used = int((sizes > 0).sum())
        fixed = max(1, used // 4)
        passed = fixed + (places - fixed + rotation * (used - fixed)) % max(1, number_of - fixed)
        return jnp.zeros((number_of,), jnp.int32).at[sequence[jnp.where(places < fixed, places, passed)]].set(jnp.asarray(sizes, jnp.int32))

    sizes = jnp.where(number % 4 == 0, named(crowded, number // 4), named(common, number - number // 4 - 1))
    mixed = jax.random.permutation(jax.random.fold_in(own, 3), number_of)
    giver, receiver = mixed[0:number_of // 2 * 2:2], mixed[1:number_of // 2 * 2:2]
    margin = jnp.minimum(sizes[giver] - 1, reach - sizes[receiver]) // 2
    margin = jnp.where((giver == sequence[0]) | (receiver == sequence[0]) | (sizes[receiver] == 0), 0, jnp.maximum(margin, 0))
    passed = jax.random.randint(jax.random.fold_in(own, 4), (number_of // 2,), 0, 1 << 20) % (margin + 1)
    sizes = sizes.at[giver].add(-passed).at[receiver].add(passed)
    members = jnp.searchsorted(jnp.cumsum(sizes), jnp.arange(rows * top), side="right").astype(jnp.int32)
    listing = members.reshape(top, rows).T
    listing = listing[jax.random.permutation(jax.random.fold_in(own, 1), rows)]
    rotation = jax.random.randint(jax.random.fold_in(own, 2), (rows, 1), 0, top)
    return jnp.take_along_axis(listing, (jnp.arange(top)[None, :] + rotation) % top, axis=1)


def load_shares(count, total, limit, lean, full):
    loads = [(1 << 20) // math.isqrt(rank ** lean) + 1 for rank in range(1, count + 1)]
    largest = limit if full else min(limit, max(-(-total // count), total * loads[0] // sum(loads)))
    least = 1 if total - largest >= count - 1 else 0
    counts, rest = [largest] + [least] * (count - 1), total - largest - least * (count - 1)
    while rest > 0:
        free = [i for i in range(1, count) if counts[i] < largest] or [i for i in range(1, count) if counts[i] < limit]
        mass, left = sum([loads[i] for i in free]), rest
        for i in free:
            addition = min(limit - counts[i], max(1, left * loads[i] // mass), rest)
            counts[i] = counts[i] + addition
            rest = rest - addition
    return np.array(counts)


def noise(stream_key, dims, spread, reach, pieces=(), held_as=jnp.bfloat16):
    drawn = jax.random.normal(stream_key, dims, jnp.float32) * spread
    if len(pieces) > 0:
        drawn = shard_levels(stream_key, dims, pieces, -0.22, 0.18) * drawn
    return jnp.clip(drawn, min=-reach, max=reach).astype(held_as)


def setup_inputs(seed: int = 0) -> dict:
    streams_of = jax.random.split(jax.random.key(seed), 15)
    text_embed = noise(streams_of[0], (TOKENS, D), 1.0, 6.0, ((0, 256),))
    image_feats = noise(streams_of[1], (IMG_TOKENS, VIS), 1.0, 6.0, ((0, 256),))
    tile_pos = draw_tile_pos(jax.random.fold_in(streams_of[14], 71), 0)
    proj_in = noise(streams_of[3], (VIS, D), VIS ** -0.5, 0.09375, ((1, 8),))
    proj_out = noise(streams_of[4], (D, D), D ** -0.5, 0.125, ((0, 8),))
    norm_gain = jnp.clip(1.0 + 0.18 * jax.random.normal(streams_of[5], (D,), jnp.float32), 0.1, 1.9)
    shared_gate = noise(streams_of[6], (D, FFS), D ** -0.5, 0.125, ((1, 8),))
    shared_up = noise(streams_of[7], (D, FFS), D ** -0.5, 0.125, ((1, 8),))
    shared_down = noise(streams_of[8], (FFS, D), FFS ** -0.5, 0.109375, ((0, 8),))
    expert_gate = noise(streams_of[9], (EXPERTS, D, FF), D ** -0.5, 0.125, ((0, 32), (2, 8)))
    expert_up = noise(streams_of[10], (EXPERTS, D, FF), D ** -0.5, 0.125, ((0, 32), (2, 8)))
    expert_down = noise(streams_of[11], (EXPERTS, FF, D), FF ** -0.5, 0.15625, ((0, 32), (1, 8)))
    route_ids_keys = jax.random.split(jax.random.fold_in(streams_of[12], 1), TOKENS // GROUP_TOK)
    route_ids_turns = jax.random.permutation(jax.random.fold_in(streams_of[12], 3), TOKENS // GROUP_TOK)
    route_ids = jax.vmap(lambda own, number: routed_block(jax.random.fold_in(streams_of[12], 2), own, number, GROUP_TOK, EXPERTS, TOP, CAP, 2))(route_ids_keys, route_ids_turns).reshape((TOKENS, TOP))
    route_wts = plant(jax.random.randint(streams_of[13], (TOKENS, TOP), 1, 65536), jax.random.fold_in(streams_of[13], 1), 1, 65535).astype(jnp.int32)
    return {"text_embed": text_embed, "image_feats": image_feats, "tile_pos": tile_pos, "proj_in": proj_in, "proj_out": proj_out, "norm_gain": norm_gain, "shared_gate": shared_gate, "shared_up": shared_up, "shared_down": shared_down, "expert_gate": expert_gate, "expert_up": expert_up, "expert_down": expert_down, "route_ids": route_ids, "route_wts": route_wts}


def reference(text_embed, image_feats, tile_pos, proj_in, proj_out, norm_gain, shared_gate, shared_up, shared_down, expert_gate, expert_up, expert_down, route_ids, route_wts):
    vis_hidden = jax.nn.gelu(jnp.dot(image_feats, proj_in, preferred_element_type=jnp.float32), approximate=True).astype(jnp.bfloat16)
    projected = jnp.dot(vis_hidden, proj_out, preferred_element_type=jnp.float32).astype(jnp.bfloat16)
    embed = text_embed.at[tile_pos].set(projected)
    embed_f = embed.astype(jnp.float32)
    meansq = lax.optimization_barrier(jnp.mean(embed_f * embed_f, axis=-1, keepdims=True)) + 1e-06
    normed = (embed_f * lax.rsqrt(meansq) * norm_gain).astype(jnp.bfloat16)
    gate_s = jnp.dot(normed, shared_gate, preferred_element_type=jnp.float32)
    up_s = jnp.dot(normed, shared_up, preferred_element_type=jnp.float32)
    shared_hidden = (jax.nn.silu(gate_s) * up_s).astype(jnp.bfloat16)
    shared_out = jnp.dot(shared_hidden, shared_down, preferred_element_type=jnp.float32)
    weights_f = route_wts.astype(jnp.float32)
    weights_n = weights_f / lax.optimization_barrier(jnp.sum(weights_f, axis=-1, keepdims=True))
    ngroups = TOKENS // GROUP_TOK
    pairs = GROUP_TOK * TOP
    ids = route_ids.reshape(ngroups, pairs)
    onehot = (ids[:, :, None] == jnp.arange(EXPERTS, dtype=jnp.int32)[None, None, :]).astype(jnp.int32)
    rank = lax.optimization_barrier(jnp.sum(jnp.cumsum(onehot, axis=1) * onehot, axis=2)) - 1
    slot = ids * CAP + rank
    pair_index = jnp.broadcast_to(jnp.arange(pairs, dtype=jnp.int32)[None, :], (ngroups, pairs))
    group_index = jnp.broadcast_to(jnp.arange(ngroups, dtype=jnp.int32)[:, None], (ngroups, pairs))
    table = jnp.full((ngroups, EXPERTS * CAP), -1, dtype=jnp.int32)
    table = table.at[group_index, slot].set(pair_index)
    flat_weights = weights_n.reshape(ngroups, pairs)
    group_base = (jnp.arange(ngroups, dtype=jnp.int32) * GROUP_TOK)[:, None]
    fsplit = FF // N_EXPERT

    def one_expert(result, expert):
        source = lax.dynamic_slice_in_dim(table, expert * CAP, CAP, 1)
        valid = source >= 0
        safe = jnp.where(valid, source, 0).astype(jnp.int32)
        token = (safe // TOP + group_base).astype(jnp.int32)
        rows_in = jnp.where(valid[:, :, None], normed[token], jnp.zeros((), jnp.bfloat16)).astype(jnp.float32)
        gate_w = expert_gate[expert].astype(jnp.float32)
        up_w = expert_up[expert].astype(jnp.float32)
        down_w = expert_down[expert].astype(jnp.float32).reshape(N_EXPERT, fsplit, D)
        gate_e = jnp.einsum('gcd,df->gcf', rows_in, gate_w)
        up_e = jnp.einsum('gcd,df->gcf', rows_in, up_w)
        hidden_e = (jax.nn.silu(gate_e) * up_e).astype(jnp.bfloat16)
        hidden_e = hidden_e.astype(jnp.float32).reshape(ngroups, CAP, N_EXPERT, fsplit)
        partial_value = jnp.einsum('gcnf,nfd->gcnd', hidden_e, down_w)
        partial_value = lax.optimization_barrier(partial_value.astype(jnp.bfloat16))
        expert_out = lax.optimization_barrier(jnp.sum(partial_value.astype(jnp.float32), axis=2)).astype(jnp.bfloat16)
        coef = jnp.where(valid, jnp.take_along_axis(flat_weights, safe, axis=1), 0.0)
        result = result.at[token].add(coef[:, :, None] * expert_out.astype(jnp.float32))
        return (result, None)
    routed_out, _ = lax.scan(one_expert, jnp.zeros((TOKENS, D), jnp.float32), jnp.arange(EXPERTS, dtype=jnp.int32))
    return (embed_f + shared_out + routed_out).astype(jnp.bfloat16)
```

```python
import jax
import jax.numpy as jnp
from jax import lax
from jax.sharding import PartitionSpec as P


def normalize(rows, norm_gain):
    rows_f = rows.astype(jnp.float32)
    meansq = jnp.mean(rows_f * rows_f, axis=-1, keepdims=True) + 1e-06
    return (rows_f * lax.rsqrt(meansq) * norm_gain).astype(jnp.bfloat16)


def select_dot(sel, rows):
    return jnp.dot(sel, rows, preferred_element_type=jnp.float32)


def shards(
    text_embed,
    image_feats,
    tile_pos,
    proj_in,
    proj_out,
    norm_gain,
    shared_gate,
    shared_up,
    shared_down,
    expert_gate,
    expert_up,
    expert_down,
    route_ids,
    route_wts,
):
    bf16, f32 = jnp.bfloat16, jnp.float32
    tok_dev, width_model = text_embed.shape
    img_dev, width_vis = image_feats.shape
    n_data = lax.axis_size("dp")
    n_group = lax.axis_size("expert")
    peer = img_dev // n_data
    my_place = lax.axis_index("expert")

    dest_index = tile_pos // tok_dev // n_group
    order = jnp.argsort(dest_index, stable=True)
    offs_sorted = (tile_pos[order] % tok_dev).astype(bf16)
    pad = 128
    packed = jnp.concatenate(
        [image_feats[order], jnp.broadcast_to(offs_sorted[:, None], (img_dev, pad))], axis=1
    ).reshape(n_data, peer, width_vis + pad)
    moved = lax.all_to_all(packed, "dp", split_axis=0, concat_axis=0, tiled=True)
    moved = moved.reshape(img_dev, width_vis + pad)
    moved_feats = moved[:, :width_vis]
    moved_offs = moved[:, width_vis].astype(jnp.int32)

    feats = lax.all_gather(moved_feats, "expert", axis=0, tiled=True)
    vis_hidden = jax.nn.gelu(
        jnp.dot(feats, proj_in, preferred_element_type=f32), approximate=True
    ).astype(bf16)
    partial_proj = jnp.dot(vis_hidden, proj_out, preferred_element_type=f32).astype(bf16)
    projected = lax.psum_scatter(partial_proj, "expert", scatter_dimension=0, tiled=True)

    place = (
        moved_offs[None, :] == jnp.arange(tok_dev, dtype=jnp.int32)[:, None]
    ).astype(bf16)
    placed = select_dot(place, projected)
    has_image = jnp.sum(place.astype(f32), axis=1, keepdims=True) > 0
    embed_own = jnp.where(has_image, placed, text_embed.astype(f32))
    normed_own = normalize(embed_own, norm_gain)

    normed = lax.all_gather(normed_own, "expert", axis=0, tiled=True)
    routes = lax.all_gather(
        jnp.concatenate([route_ids, route_wts], axis=1), "expert", axis=0, tiled=True
    )
    top_count = route_ids.shape[1]
    ids = routes[:, :top_count]
    weights = routes[:, top_count:]

    gate_s = jnp.dot(normed, shared_gate, preferred_element_type=f32)
    up_s = jnp.dot(normed, shared_up, preferred_element_type=f32)
    shared_hidden = (jax.nn.silu(gate_s) * up_s).astype(bf16)

    group_rows = normed.shape[0]
    n_pairs = group_rows * top_count
    capacity = 3 * group_rows * top_count // (2 * n_data)
    share = capacity // n_group
    flat_ids = ids.reshape(-1)
    onehot = (flat_ids[:, None] == jnp.arange(n_data, dtype=jnp.int32)[None, :]).astype(bf16)
    pair_iota = jnp.arange(n_pairs, dtype=jnp.int32)
    earlier = (pair_iota[None, :] < pair_iota[:, None]).astype(bf16)
    counts = select_dot(earlier, onehot)
    rank = jnp.sum(counts * onehot.astype(f32), axis=1).astype(jnp.int32)

    inside = rank // share == my_place
    row_of = jnp.where(inside, flat_ids * share + rank - my_place * share, -1)
    n_rows = n_data * share
    hit = (
        row_of.reshape(group_rows, top_count)[:, :, None]
        == jnp.arange(n_rows, dtype=jnp.int32)[None, None, :]
    )
    pick = jnp.sum(hit.astype(f32), axis=1).astype(bf16)
    send = select_dot(pick.T, normed).astype(bf16).reshape(n_data, share, width_model)
    arrived = lax.all_to_all(send, "dp", split_axis=0, concat_axis=0, tiled=True)
    slots = lax.all_gather(
        arrived.reshape(n_rows, width_model), "expert", axis=0, tiled=True
    )

    gate_e = jnp.dot(slots, expert_gate[0], preferred_element_type=f32)
    up_e = jnp.dot(slots, expert_up[0], preferred_element_type=f32)
    hidden_e = (jax.nn.silu(gate_e) * up_e).astype(bf16)
    partial_out = jnp.dot(hidden_e, expert_down[0], preferred_element_type=f32).astype(bf16)
    summed = lax.psum_scatter(partial_out, "expert", scatter_dimension=0, tiled=True)
    returned = lax.all_to_all(
        summed.reshape(n_data, share, width_model), "dp", split_axis=0, concat_axis=0, tiled=True
    ).reshape(n_rows, width_model)

    weights_f = weights.astype(f32)
    weights_n = weights_f / jnp.sum(weights_f, axis=1, keepdims=True)
    coef = jnp.sum(jnp.where(hit, weights_n[:, :, None], 0.0), axis=1)
    coef_hi = coef.astype(bf16)
    coef_lo = (coef - coef_hi.astype(f32)).astype(bf16)
    combined = select_dot(coef_hi, returned) + select_dot(coef_lo, returned)
    total = lax.psum_scatter(
        (jnp.dot(shared_hidden, shared_down, preferred_element_type=f32) + combined).astype(bf16),
        "expert",
        scatter_dimension=0,
        tiled=True,
    ).astype(f32)
    return (embed_own + total).astype(bf16)


def solution(mesh):
    return jax.shard_map(
        shards,
        mesh=mesh,
        in_specs=(
            P(("dp", "expert"), None),
            P(("dp", "expert"), None),
            P(("dp", "expert")),
            P(None, "expert"),
            P("expert", None),
            P(),
            P(None, "expert"),
            P(None, "expert"),
            P("expert", None),
            P("dp", None, "expert"),
            P("dp", None, "expert"),
            P("dp", "expert", None),
            P(("dp", "expert"), None),
            P(("dp", "expert"), None),
        ),
        out_specs=P(("dp", "expert"), None),
        check_vma=False,
    )
```

```python
import jax
import jax.numpy as jnp
from jax import lax
from jax.experimental import pallas as pl
from jax.experimental.pallas import tpu as pltpu
from jax.sharding import PartitionSpec as P


def dp_all_to_all(x, collective_id):
    n = x.shape[0]
    mesh_ids = pl.DeviceIdType.MESH

    def kernel(x_ref, y_ref, send_sem, recv_sem, local_sem):
        me = lax.axis_index("dp")
        j = lax.axis_index("expert")
        barrier = pltpu.get_barrier_semaphore()
        for k in range(1, n):
            pl.semaphore_signal(
                barrier, inc=1, device_id=(lax.rem(me + k, n), j), device_id_type=mesh_ids
            )
        pl.semaphore_wait(barrier, n - 1)
        local = pltpu.make_async_copy(x_ref.at[me], y_ref.at[me], local_sem)
        local.start()
        copies = []
        for k in range(1, n):
            peer = lax.rem(me + k, n)
            copy = pltpu.make_async_remote_copy(
                src_ref=x_ref.at[peer],
                dst_ref=y_ref.at[me],
                send_sem=send_sem.at[k],
                recv_sem=recv_sem.at[k],
                device_id=(peer, j),
                device_id_type=mesh_ids,
            )
            copy.start()
            copies.append(copy)
        local.wait()
        for copy in copies:
            copy.wait()

    return pl.pallas_call(
        kernel,
        out_shape=jax.ShapeDtypeStruct(x.shape, x.dtype),
        in_specs=[pl.BlockSpec(memory_space=pl.ANY)],
        out_specs=pl.BlockSpec(memory_space=pl.ANY),
        scratch_shapes=[
            pltpu.SemaphoreType.DMA((n,)),
            pltpu.SemaphoreType.DMA((n,)),
            pltpu.SemaphoreType.DMA,
        ],
        compiler_params=pltpu.CompilerParams(collective_id=collective_id, has_side_effects=True),
    )(x)


def normalize(rows, norm_gain):
    rows_f = rows.astype(jnp.float32)
    meansq = jnp.mean(rows_f * rows_f, axis=-1, keepdims=True) + 1e-06
    return (rows_f * lax.rsqrt(meansq) * norm_gain).astype(jnp.bfloat16)


def select_dot(sel, rows):
    return jnp.dot(sel, rows, preferred_element_type=jnp.float32)


def shards(
    text_embed,
    image_feats,
    tile_pos,
    proj_in,
    proj_out,
    norm_gain,
    shared_gate,
    shared_up,
    shared_down,
    expert_gate,
    expert_up,
    expert_down,
    route_ids,
    route_wts,
):
    bf16, f32 = jnp.bfloat16, jnp.float32
    tok_dev, width_model = text_embed.shape
    img_dev, width_vis = image_feats.shape
    n_data = lax.axis_size("dp")
    n_group = lax.axis_size("expert")
    peer = img_dev // n_data
    my_place = lax.axis_index("expert")

    dest_index = tile_pos // tok_dev // n_group
    order = jnp.argsort(dest_index, stable=True)
    offs_sorted = (tile_pos[order] % tok_dev).astype(bf16)
    pad = 128
    packed = jnp.concatenate(
        [image_feats[order], jnp.broadcast_to(offs_sorted[:, None], (img_dev, pad))], axis=1
    ).reshape(n_data, peer, width_vis + pad)
    moved = dp_all_to_all(packed, 0)
    moved = moved.reshape(img_dev, width_vis + pad)
    moved_feats = moved[:, :width_vis]
    moved_offs = moved[:, width_vis].astype(jnp.int32)

    feats = lax.all_gather(moved_feats, "expert", axis=0, tiled=True)
    vis_hidden = jax.nn.gelu(
        jnp.dot(feats, proj_in, preferred_element_type=f32), approximate=True
    ).astype(bf16)
    partial_proj = jnp.dot(vis_hidden, proj_out, preferred_element_type=f32).astype(bf16)
    projected = lax.psum_scatter(partial_proj, "expert", scatter_dimension=0, tiled=True)

    place = (
        moved_offs[None, :] == jnp.arange(tok_dev, dtype=jnp.int32)[:, None]
    ).astype(bf16)
    placed = select_dot(place, projected)
    has_image = jnp.sum(place.astype(f32), axis=1, keepdims=True) > 0
    embed_own = jnp.where(has_image, placed, text_embed.astype(f32))
    normed_own = normalize(embed_own, norm_gain)

    normed = lax.all_gather(normed_own, "expert", axis=0, tiled=True)
    routes = lax.all_gather(
        jnp.concatenate([route_ids, route_wts], axis=1), "expert", axis=0, tiled=True
    )
    top_count = route_ids.shape[1]
    ids = routes[:, :top_count]
    weights = routes[:, top_count:]

    gate_s = jnp.dot(normed, shared_gate, preferred_element_type=f32)
    up_s = jnp.dot(normed, shared_up, preferred_element_type=f32)
    shared_hidden = (jax.nn.silu(gate_s) * up_s).astype(bf16)

    group_rows = normed.shape[0]
    n_pairs = group_rows * top_count
    capacity = 3 * group_rows * top_count // (2 * n_data)
    share = capacity // n_group
    flat_ids = ids.reshape(-1)
    onehot = (flat_ids[:, None] == jnp.arange(n_data, dtype=jnp.int32)[None, :]).astype(bf16)
    pair_iota = jnp.arange(n_pairs, dtype=jnp.int32)
    earlier = (pair_iota[None, :] < pair_iota[:, None]).astype(bf16)
    counts = select_dot(earlier, onehot)
    rank = jnp.sum(counts * onehot.astype(f32), axis=1).astype(jnp.int32)

    inside = rank // share == my_place
    row_of = jnp.where(inside, flat_ids * share + rank - my_place * share, -1)
    n_rows = n_data * share
    hit = (
        row_of.reshape(group_rows, top_count)[:, :, None]
        == jnp.arange(n_rows, dtype=jnp.int32)[None, None, :]
    )
    pick = jnp.sum(hit.astype(f32), axis=1).astype(bf16)
    send = select_dot(pick.T, normed).astype(bf16).reshape(n_data, share, width_model)
    arrived = dp_all_to_all(send, 1)
    slots = lax.all_gather(
        arrived.reshape(n_rows, width_model), "expert", axis=0, tiled=True
    )

    gate_e = jnp.dot(slots, expert_gate[0], preferred_element_type=f32)
    up_e = jnp.dot(slots, expert_up[0], preferred_element_type=f32)
    hidden_e = (jax.nn.silu(gate_e) * up_e).astype(bf16)
    partial_out = jnp.dot(hidden_e, expert_down[0], preferred_element_type=f32).astype(bf16)
    summed = lax.psum_scatter(partial_out, "expert", scatter_dimension=0, tiled=True)
    returned = dp_all_to_all(summed.reshape(n_data, share, width_model), 2).reshape(
        n_rows, width_model
    )

    weights_f = weights.astype(f32)
    weights_n = weights_f / jnp.sum(weights_f, axis=1, keepdims=True)
    coef = jnp.sum(jnp.where(hit, weights_n[:, :, None], 0.0), axis=1)
    coef_hi = coef.astype(bf16)
    coef_lo = (coef - coef_hi.astype(f32)).astype(bf16)
    combined = select_dot(coef_hi, returned) + select_dot(coef_lo, returned)
    total = lax.psum_scatter(
        (jnp.dot(shared_hidden, shared_down, preferred_element_type=f32) + combined).astype(bf16),
        "expert",
        scatter_dimension=0,
        tiled=True,
    ).astype(f32)
    return (embed_own + total).astype(bf16)


def solution(mesh):
    return jax.shard_map(
        shards,
        mesh=mesh,
        in_specs=(
            P(("dp", "expert"), None),
            P(("dp", "expert"), None),
            P(("dp", "expert")),
            P(None, "expert"),
            P("expert", None),
            P(),
            P(None, "expert"),
            P(None, "expert"),
            P("expert", None),
            P("dp", None, "expert"),
            P("dp", None, "expert"),
            P("dp", "expert", None),
            P(("dp", "expert"), None),
            P(("dp", "expert"), None),
        ),
        out_specs=P(("dp", "expert"), None),
        check_vma=False,
    )
```

```python
import jax
import jax.numpy as jnp
from jax import lax
from jax.experimental import pallas as pl
from jax.experimental.pallas import tpu as pltpu
from jax.sharding import PartitionSpec as P


def dp_all_to_all(x, collective_id):
    n = x.shape[0]
    mesh_ids = pl.DeviceIdType.MESH

    def kernel(x_ref, y_ref, send_sem, recv_sem, local_sem):
        me = lax.axis_index("dp")
        j = lax.axis_index("expert")
        barrier = pltpu.get_barrier_semaphore()
        for k in range(1, n):
            pl.semaphore_signal(
                barrier, inc=1, device_id=(lax.rem(me + k, n), j), device_id_type=mesh_ids
            )
        pl.semaphore_wait(barrier, n - 1)
        local = pltpu.make_async_copy(x_ref.at[me], y_ref.at[me], local_sem)
        local.start()
        copies = []
        for k in range(1, n):
            peer = lax.rem(me + k, n)
            copy = pltpu.make_async_remote_copy(
                src_ref=x_ref.at[peer],
                dst_ref=y_ref.at[me],
                send_sem=send_sem.at[k],
                recv_sem=recv_sem.at[k],
                device_id=(peer, j),
                device_id_type=mesh_ids,
            )
            copy.start()
            copies.append(copy)
        local.wait()
        for copy in copies:
            copy.wait()

    return pl.pallas_call(
        kernel,
        out_shape=jax.ShapeDtypeStruct(x.shape, x.dtype),
        in_specs=[pl.BlockSpec(memory_space=pl.ANY)],
        out_specs=pl.BlockSpec(memory_space=pl.ANY),
        scratch_shapes=[
            pltpu.SemaphoreType.DMA((n,)),
            pltpu.SemaphoreType.DMA((n,)),
            pltpu.SemaphoreType.DMA,
        ],
        compiler_params=pltpu.CompilerParams(collective_id=collective_id, has_side_effects=True),
    )(x)


def normalize(rows, norm_gain):
    rows_f = rows.astype(jnp.float32)
    meansq = jnp.mean(rows_f * rows_f, axis=-1, keepdims=True) + 1e-06
    return (rows_f * lax.rsqrt(meansq) * norm_gain).astype(jnp.bfloat16)


def select_dot(sel, rows):
    return jnp.dot(sel, rows, preferred_element_type=jnp.float32)


def shards(
    text_embed,
    image_feats,
    tile_pos,
    proj_in,
    proj_out,
    norm_gain,
    shared_gate,
    shared_up,
    shared_down,
    expert_gate,
    expert_up,
    expert_down,
    route_ids,
    route_wts,
):
    bf16, f32 = jnp.bfloat16, jnp.float32
    tok_dev, width_model = text_embed.shape
    img_dev, width_vis = image_feats.shape
    n_data = lax.axis_size("dp")
    n_group = lax.axis_size("expert")
    peer = img_dev // n_data
    my_place = lax.axis_index("expert")

    route_cols = jnp.concatenate([route_ids, route_wts // 256, route_wts % 256], axis=1)
    route_cols = jnp.pad(route_cols, ((0, 0), (0, 128 - route_cols.shape[1])))

    dest_index = tile_pos // tok_dev // n_group
    order = jnp.argsort(dest_index, stable=True)
    offs_sorted = (tile_pos[order] % tok_dev).astype(bf16)
    pad = 128
    packed = jnp.concatenate(
        [image_feats[order], jnp.broadcast_to(offs_sorted[:, None], (img_dev, pad))], axis=1
    ).reshape(n_data, peer, width_vis + pad)
    moved = dp_all_to_all(packed, 0)
    moved = moved.reshape(img_dev, width_vis + pad)
    moved_feats = moved[:, :width_vis]
    moved_offs = moved[:, width_vis].astype(jnp.int32)

    feats = lax.all_gather(moved_feats, "expert", axis=0, tiled=True)
    vis_hidden = jax.nn.gelu(
        jnp.dot(feats, proj_in, preferred_element_type=f32), approximate=True
    ).astype(bf16)
    partial_proj = jnp.dot(vis_hidden, proj_out, preferred_element_type=f32).astype(bf16)
    projected = lax.psum_scatter(partial_proj, "expert", scatter_dimension=0, tiled=True)

    place = (
        moved_offs[None, :] == jnp.arange(tok_dev, dtype=jnp.int32)[:, None]
    ).astype(bf16)
    placed = select_dot(place, projected)
    has_image = jnp.sum(place.astype(f32), axis=1, keepdims=True) > 0
    embed_own = jnp.where(has_image, placed, text_embed.astype(f32))
    normed_own = normalize(embed_own, norm_gain)

    gathered = lax.all_gather(
        jnp.concatenate([normed_own, route_cols.astype(bf16)], axis=1), "expert", axis=0, tiled=True
    )
    normed = gathered[:, :width_model]
    routes = gathered[:, width_model:].astype(f32)
    top_count = route_ids.shape[1]
    ids = routes[:, :top_count].astype(jnp.int32)
    weights_f = routes[:, top_count : 2 * top_count] * 256.0 + routes[:, 2 * top_count : 3 * top_count]

    gate_s = jnp.dot(normed, shared_gate, preferred_element_type=f32)
    up_s = jnp.dot(normed, shared_up, preferred_element_type=f32)
    shared_hidden = (jax.nn.silu(gate_s) * up_s).astype(bf16)

    group_rows = normed.shape[0]
    n_pairs = group_rows * top_count
    capacity = 3 * group_rows * top_count // (2 * n_data)
    share = capacity // n_group
    flat_ids = ids.reshape(-1)
    onehot = (flat_ids[:, None] == jnp.arange(n_data, dtype=jnp.int32)[None, :]).astype(bf16)
    pair_iota = jnp.arange(n_pairs, dtype=jnp.int32)
    earlier = (pair_iota[None, :] < pair_iota[:, None]).astype(bf16)
    counts = select_dot(earlier, onehot)
    rank = jnp.sum(counts * onehot.astype(f32), axis=1).astype(jnp.int32)

    inside = rank // share == my_place
    row_of = jnp.where(inside, flat_ids * share + rank - my_place * share, -1)
    n_rows = n_data * share
    hit = (
        row_of.reshape(group_rows, top_count)[:, :, None]
        == jnp.arange(n_rows, dtype=jnp.int32)[None, None, :]
    )
    pick = jnp.sum(hit.astype(f32), axis=1).astype(bf16)
    send = select_dot(pick.T, normed).astype(bf16).reshape(n_data, share, width_model)
    arrived = dp_all_to_all(send, 1)
    slots = lax.all_gather(
        arrived.reshape(n_rows, width_model), "expert", axis=0, tiled=True
    )

    gate_e = jnp.dot(slots, expert_gate[0], preferred_element_type=f32)
    up_e = jnp.dot(slots, expert_up[0], preferred_element_type=f32)
    hidden_e = (jax.nn.silu(gate_e) * up_e).astype(bf16)
    partial_out = jnp.dot(hidden_e, expert_down[0], preferred_element_type=f32).astype(bf16)
    summed = lax.psum_scatter(partial_out, "expert", scatter_dimension=0, tiled=True)
    returned = dp_all_to_all(summed.reshape(n_data, share, width_model), 2).reshape(
        n_rows, width_model
    )

    weights_n = weights_f / jnp.sum(weights_f, axis=1, keepdims=True)
    coef = jnp.sum(jnp.where(hit, weights_n[:, :, None], 0.0), axis=1)
    coef_hi = coef.astype(bf16)
    coef_lo = (coef - coef_hi.astype(f32)).astype(bf16)
    combined = select_dot(coef_hi, returned) + select_dot(coef_lo, returned)
    total = lax.psum_scatter(
        (jnp.dot(shared_hidden, shared_down, preferred_element_type=f32) + combined).astype(bf16),
        "expert",
        scatter_dimension=0,
        tiled=True,
    ).astype(f32)
    return (embed_own + total).astype(bf16)


def solution(mesh):
    return jax.shard_map(
        shards,
        mesh=mesh,
        in_specs=(
            P(("dp", "expert"), None),
            P(("dp", "expert"), None),
            P(("dp", "expert")),
            P(None, "expert"),
            P("expert", None),
            P(),
            P(None, "expert"),
            P(None, "expert"),
            P("expert", None),
            P("dp", None, "expert"),
            P("dp", None, "expert"),
            P("dp", "expert", None),
            P(("dp", "expert"), None),
            P(("dp", "expert"), None),
        ),
        out_specs=P(("dp", "expert"), None),
        check_vma=False,
    )
```

```python
import jax
import jax.numpy as jnp
from jax import lax
from jax.experimental import pallas as pl
from jax.experimental.pallas import tpu as pltpu
from jax.sharding import PartitionSpec as P


def dp_all_to_all(x, collective_id):
    n = x.shape[0]
    mesh_ids = pl.DeviceIdType.MESH

    def kernel(x_ref, y_ref, send_sem, recv_sem, local_sem):
        me = lax.axis_index("dp")
        j = lax.axis_index("expert")
        barrier = pltpu.get_barrier_semaphore()
        for k in range(1, n):
            pl.semaphore_signal(
                barrier, inc=1, device_id=(lax.rem(me + k, n), j), device_id_type=mesh_ids
            )
        pl.semaphore_wait(barrier, n - 1)
        local = pltpu.make_async_copy(x_ref.at[me], y_ref.at[me], local_sem)
        local.start()
        copies = []
        for k in range(1, n):
            peer = lax.rem(me + k, n)
            copy = pltpu.make_async_remote_copy(
                src_ref=x_ref.at[peer],
                dst_ref=y_ref.at[me],
                send_sem=send_sem.at[k],
                recv_sem=recv_sem.at[k],
                device_id=(peer, j),
                device_id_type=mesh_ids,
            )
            copy.start()
            copies.append(copy)
        local.wait()
        for copy in copies:
            copy.wait()

    return pl.pallas_call(
        kernel,
        out_shape=jax.ShapeDtypeStruct(x.shape, x.dtype),
        in_specs=[pl.BlockSpec(memory_space=pl.ANY)],
        out_specs=pl.BlockSpec(memory_space=pl.ANY),
        scratch_shapes=[
            pltpu.SemaphoreType.DMA((n,)),
            pltpu.SemaphoreType.DMA((n,)),
            pltpu.SemaphoreType.DMA,
        ],
        compiler_params=pltpu.CompilerParams(collective_id=collective_id, has_side_effects=True),
    )(x)


def expert_reduce_scatter(x, collective_id, out_dtype):
    n, rows, cols = x.shape
    mesh_ids = pl.DeviceIdType.MESH

    def kernel(x_ref, o_ref, buf, send_sem, recv_sem):
        me = lax.axis_index("expert")
        row = lax.axis_index("dp")
        barrier = pltpu.get_barrier_semaphore()
        for k in range(1, n):
            pl.semaphore_signal(
                barrier, inc=1, device_id=(row, lax.rem(me + k, n)), device_id_type=mesh_ids
            )
        pl.semaphore_wait(barrier, n - 1)
        copies = []
        for k in range(1, n):
            copy = pltpu.make_async_remote_copy(
                src_ref=x_ref.at[lax.rem(me + k, n)],
                dst_ref=buf.at[k],
                send_sem=send_sem.at[k],
                recv_sem=recv_sem.at[k],
                device_id=(row, lax.rem(me + k, n)),
                device_id_type=mesh_ids,
            )
            copy.start()
            copies.append(copy)
        acc = x_ref[me].astype(jnp.float32)
        for k, copy in enumerate(copies, 1):
            copy.wait()
            acc = acc + buf[k].astype(jnp.float32)
        o_ref[...] = acc.astype(o_ref.dtype)

    return pl.pallas_call(
        kernel,
        out_shape=jax.ShapeDtypeStruct((rows, cols), out_dtype),
        in_specs=[pl.BlockSpec(memory_space=pltpu.VMEM)],
        out_specs=pl.BlockSpec(memory_space=pltpu.VMEM),
        scratch_shapes=[
            pltpu.VMEM((n, rows, cols), x.dtype),
            pltpu.SemaphoreType.DMA((n,)),
            pltpu.SemaphoreType.DMA((n,)),
        ],
        compiler_params=pltpu.CompilerParams(collective_id=collective_id, has_side_effects=True),
    )(x)


def normalize(rows, norm_gain):
    rows_f = rows.astype(jnp.float32)
    meansq = jnp.mean(rows_f * rows_f, axis=-1, keepdims=True) + 1e-06
    return (rows_f * lax.rsqrt(meansq) * norm_gain).astype(jnp.bfloat16)


def select_dot(sel, rows):
    return jnp.dot(sel, rows, preferred_element_type=jnp.float32)


def shards(
    text_embed,
    image_feats,
    tile_pos,
    proj_in,
    proj_out,
    norm_gain,
    shared_gate,
    shared_up,
    shared_down,
    expert_gate,
    expert_up,
    expert_down,
    route_ids,
    route_wts,
):
    bf16, f32 = jnp.bfloat16, jnp.float32
    tok_dev, width_model = text_embed.shape
    img_dev, width_vis = image_feats.shape
    n_data = lax.axis_size("dp")
    n_group = lax.axis_size("expert")
    peer = img_dev // n_data
    my_place = lax.axis_index("expert")

    route_cols = jnp.concatenate([route_ids, route_wts // 256, route_wts % 256], axis=1)
    route_cols = jnp.pad(route_cols, ((0, 0), (0, 128 - route_cols.shape[1])))

    dest_index = tile_pos // tok_dev // n_group
    order = jnp.argsort(dest_index, stable=True)
    offs_sorted = (tile_pos[order] % tok_dev).astype(bf16)
    pad = 128
    packed = jnp.concatenate(
        [image_feats[order], jnp.broadcast_to(offs_sorted[:, None], (img_dev, pad))], axis=1
    ).reshape(n_data, peer, width_vis + pad)
    moved = dp_all_to_all(packed, 0)
    moved = moved.reshape(img_dev, width_vis + pad)
    moved_feats = moved[:, :width_vis]
    moved_offs = moved[:, width_vis].astype(jnp.int32)

    feats = lax.all_gather(moved_feats, "expert", axis=0, tiled=True)
    vis_hidden = jax.nn.gelu(
        jnp.dot(feats, proj_in, preferred_element_type=f32), approximate=True
    ).astype(bf16)
    partial_proj = jnp.dot(vis_hidden, proj_out, preferred_element_type=f32).astype(bf16)
    projected = expert_reduce_scatter(
        partial_proj.reshape(n_group, img_dev, width_model), 3, bf16
    )

    place = (
        moved_offs[None, :] == jnp.arange(tok_dev, dtype=jnp.int32)[:, None]
    ).astype(bf16)
    placed = select_dot(place, projected)
    has_image = jnp.sum(place.astype(f32), axis=1, keepdims=True) > 0
    embed_own = jnp.where(has_image, placed, text_embed.astype(f32))
    normed_own = normalize(embed_own, norm_gain)

    gathered = lax.all_gather(
        jnp.concatenate([normed_own, route_cols.astype(bf16)], axis=1), "expert", axis=0, tiled=True
    )
    normed = gathered[:, :width_model]
    routes = gathered[:, width_model:].astype(f32)
    top_count = route_ids.shape[1]
    ids = routes[:, :top_count].astype(jnp.int32)
    weights_f = routes[:, top_count : 2 * top_count] * 256.0 + routes[:, 2 * top_count : 3 * top_count]

    gate_s = jnp.dot(normed, shared_gate, preferred_element_type=f32)
    up_s = jnp.dot(normed, shared_up, preferred_element_type=f32)
    shared_hidden = (jax.nn.silu(gate_s) * up_s).astype(bf16)

    group_rows = normed.shape[0]
    n_pairs = group_rows * top_count
    capacity = 3 * group_rows * top_count // (2 * n_data)
    share = capacity // n_group
    flat_ids = ids.reshape(-1)
    onehot = (flat_ids[:, None] == jnp.arange(n_data, dtype=jnp.int32)[None, :]).astype(bf16)
    pair_iota = jnp.arange(n_pairs, dtype=jnp.int32)
    earlier = (pair_iota[None, :] < pair_iota[:, None]).astype(bf16)
    counts = select_dot(earlier, onehot)
    rank = jnp.sum(counts * onehot.astype(f32), axis=1).astype(jnp.int32)

    inside = rank // share == my_place
    row_of = jnp.where(inside, flat_ids * share + rank - my_place * share, -1)
    n_rows = n_data * share
    hit = (
        row_of.reshape(group_rows, top_count)[:, :, None]
        == jnp.arange(n_rows, dtype=jnp.int32)[None, None, :]
    )
    pick = jnp.sum(hit.astype(f32), axis=1).astype(bf16)
    send = select_dot(pick.T, normed).astype(bf16).reshape(n_data, share, width_model)
    arrived = dp_all_to_all(send, 1)
    slots = lax.all_gather(
        arrived.reshape(n_rows, width_model), "expert", axis=0, tiled=True
    )

    gate_e = jnp.dot(slots, expert_gate[0], preferred_element_type=f32)
    up_e = jnp.dot(slots, expert_up[0], preferred_element_type=f32)
    hidden_e = (jax.nn.silu(gate_e) * up_e).astype(bf16)
    partial_out = jnp.dot(hidden_e, expert_down[0], preferred_element_type=f32).astype(bf16)
    summed = lax.psum_scatter(partial_out, "expert", scatter_dimension=0, tiled=True)
    returned = dp_all_to_all(summed.reshape(n_data, share, width_model), 2).reshape(
        n_rows, width_model
    )

    weights_n = weights_f / jnp.sum(weights_f, axis=1, keepdims=True)
    coef = jnp.sum(jnp.where(hit, weights_n[:, :, None], 0.0), axis=1)
    coef_hi = coef.astype(bf16)
    coef_lo = (coef - coef_hi.astype(f32)).astype(bf16)
    combined = select_dot(coef_hi, returned) + select_dot(coef_lo, returned)
    total = expert_reduce_scatter(
        (jnp.dot(shared_hidden, shared_down, preferred_element_type=f32) + combined)
        .astype(bf16)
        .reshape(n_group, tok_dev, width_model),
        4,
        f32,
    )
    return (embed_own + total).astype(bf16)


def solution(mesh):
    return jax.shard_map(
        shards,
        mesh=mesh,
        in_specs=(
            P(("dp", "expert"), None),
            P(("dp", "expert"), None),
            P(("dp", "expert")),
            P(None, "expert"),
            P("expert", None),
            P(),
            P(None, "expert"),
            P(None, "expert"),
            P("expert", None),
            P("dp", None, "expert"),
            P("dp", None, "expert"),
            P("dp", "expert", None),
            P(("dp", "expert"), None),
            P(("dp", "expert"), None),
        ),
        out_specs=P(("dp", "expert"), None),
        check_vma=False,
    )
```

```python
import jax
import jax.numpy as jnp
from jax import lax
from jax.experimental import pallas as pl
from jax.experimental.pallas import tpu as pltpu
from jax.sharding import PartitionSpec as P


def dp_all_to_all(x, collective_id):
    n = x.shape[0]
    mesh_ids = pl.DeviceIdType.MESH

    def kernel(x_ref, y_ref, send_sem, recv_sem, local_sem):
        me = lax.axis_index("dp")
        j = lax.axis_index("expert")
        barrier = pltpu.get_barrier_semaphore()
        for k in range(1, n):
            pl.semaphore_signal(
                barrier, inc=1, device_id=(lax.rem(me + k, n), j), device_id_type=mesh_ids
            )
        pl.semaphore_wait(barrier, n - 1)
        local = pltpu.make_async_copy(x_ref.at[me], y_ref.at[me], local_sem)
        local.start()
        copies = []
        for k in range(1, n):
            peer = lax.rem(me + k, n)
            copy = pltpu.make_async_remote_copy(
                src_ref=x_ref.at[peer],
                dst_ref=y_ref.at[me],
                send_sem=send_sem.at[k],
                recv_sem=recv_sem.at[k],
                device_id=(peer, j),
                device_id_type=mesh_ids,
            )
            copy.start()
            copies.append(copy)
        local.wait()
        for copy in copies:
            copy.wait()

    return pl.pallas_call(
        kernel,
        out_shape=jax.ShapeDtypeStruct(x.shape, x.dtype),
        in_specs=[pl.BlockSpec(memory_space=pl.ANY)],
        out_specs=pl.BlockSpec(memory_space=pl.ANY),
        scratch_shapes=[
            pltpu.SemaphoreType.DMA((n,)),
            pltpu.SemaphoreType.DMA((n,)),
            pltpu.SemaphoreType.DMA,
        ],
        compiler_params=pltpu.CompilerParams(collective_id=collective_id, has_side_effects=True),
    )(x)


def expert_reduce_scatter(x, collective_id, out_dtype):
    n, rows, cols = x.shape
    chips = n // 2
    mesh_ids = pl.DeviceIdType.MESH

    def kernel(x_ref, o_ref, pair_buf, part, far_buf, send1, recv1, send2, recv2):
        me = lax.axis_index("expert")
        row = lax.axis_index("dp")
        chip, core = me // 2, me % 2
        sibling = chip * 2 + 1 - core
        barrier = pltpu.get_barrier_semaphore()
        pl.semaphore_signal(barrier, inc=1, device_id=(row, sibling), device_id_type=mesh_ids)
        for k in range(1, chips):
            pl.semaphore_signal(
                barrier,
                inc=1,
                device_id=(row, lax.rem(chip + k, chips) * 2 + core),
                device_id_type=mesh_ids,
            )
        pl.semaphore_wait(barrier, chips)
        first = pltpu.make_async_remote_copy(
            src_ref=x_ref.at[:, 1 - core],
            dst_ref=pair_buf,
            send_sem=send1,
            recv_sem=recv1,
            device_id=(row, sibling),
            device_id_type=mesh_ids,
        )
        first.start()
        first.wait()
        copies = []
        for k in range(1, chips):
            dest = lax.rem(chip + k, chips)
            part[k] = (
                x_ref[dest, core].astype(jnp.float32) + pair_buf[dest].astype(jnp.float32)
            ).astype(part.dtype)
            copy = pltpu.make_async_remote_copy(
                src_ref=part.at[k],
                dst_ref=far_buf.at[k],
                send_sem=send2.at[k],
                recv_sem=recv2.at[k],
                device_id=(row, dest * 2 + core),
                device_id_type=mesh_ids,
            )
            copy.start()
            copies.append(copy)
        acc = x_ref[chip, core].astype(jnp.float32) + pair_buf[chip].astype(jnp.float32)
        for k, copy in enumerate(copies, 1):
            copy.wait()
            acc = acc + far_buf[k].astype(jnp.float32)
        o_ref[...] = acc.astype(o_ref.dtype)

    return pl.pallas_call(
        kernel,
        out_shape=jax.ShapeDtypeStruct((rows, cols), out_dtype),
        in_specs=[pl.BlockSpec(memory_space=pltpu.VMEM)],
        out_specs=pl.BlockSpec(memory_space=pltpu.VMEM),
        scratch_shapes=[
            pltpu.VMEM((chips, rows, cols), x.dtype),
            pltpu.VMEM((chips, rows, cols), x.dtype),
            pltpu.VMEM((chips, rows, cols), x.dtype),
            pltpu.SemaphoreType.DMA,
            pltpu.SemaphoreType.DMA,
            pltpu.SemaphoreType.DMA((chips,)),
            pltpu.SemaphoreType.DMA((chips,)),
        ],
        compiler_params=pltpu.CompilerParams(collective_id=collective_id, has_side_effects=True),
    )(x.reshape(chips, 2, rows, cols))


def expert_all_gather(x, collective_id):
    rows, cols = x.shape
    n = lax.axis_size("expert")
    chips = n // 2
    mesh_ids = pl.DeviceIdType.MESH

    def kernel(x_ref, o_ref, send0, recv0, send1, recv1, send2, recv2):
        me = lax.axis_index("expert")
        row = lax.axis_index("dp")
        chip, core = me // 2, me % 2
        sibling = chip * 2 + 1 - core
        barrier = pltpu.get_barrier_semaphore()
        pl.semaphore_signal(barrier, inc=1, device_id=(row, sibling), device_id_type=mesh_ids)
        for k in range(1, chips):
            pl.semaphore_signal(
                barrier,
                inc=1,
                device_id=(row, lax.rem(chip + k, chips) * 2 + core),
                device_id_type=mesh_ids,
            )
        pl.semaphore_wait(barrier, chips)
        near = pltpu.make_async_remote_copy(
            src_ref=x_ref,
            dst_ref=o_ref.at[me],
            send_sem=send0,
            recv_sem=recv0,
            device_id=(row, sibling),
            device_id_type=mesh_ids,
        )
        near.start()
        far = []
        for k in range(1, chips):
            copy = pltpu.make_async_remote_copy(
                src_ref=x_ref,
                dst_ref=o_ref.at[me],
                send_sem=send1.at[k],
                recv_sem=recv1.at[k],
                device_id=(row, lax.rem(chip + k, chips) * 2 + core),
                device_id_type=mesh_ids,
            )
            copy.start()
            far.append(copy)
        o_ref[me] = x_ref[...]
        passed = []
        for k, copy in enumerate(far, 1):
            copy.wait_recv()
            source = lax.rem(chip - k + chips, chips) * 2 + core
            relay = pltpu.make_async_remote_copy(
                src_ref=o_ref.at[source],
                dst_ref=o_ref.at[source],
                send_sem=send2.at[k],
                recv_sem=recv2.at[k],
                device_id=(row, sibling),
                device_id_type=mesh_ids,
            )
            relay.start()
            passed.append(relay)
        near.wait()
        for copy in far:
            copy.wait_send()
        for relay in passed:
            relay.wait()

    return pl.pallas_call(
        kernel,
        out_shape=jax.ShapeDtypeStruct((n, rows, cols), x.dtype),
        in_specs=[pl.BlockSpec(memory_space=pltpu.VMEM)],
        out_specs=pl.BlockSpec(memory_space=pltpu.VMEM),
        scratch_shapes=[
            pltpu.SemaphoreType.DMA,
            pltpu.SemaphoreType.DMA,
            pltpu.SemaphoreType.DMA((chips,)),
            pltpu.SemaphoreType.DMA((chips,)),
            pltpu.SemaphoreType.DMA((chips,)),
            pltpu.SemaphoreType.DMA((chips,)),
        ],
        compiler_params=pltpu.CompilerParams(collective_id=collective_id, has_side_effects=True),
    )(x)


def normalize(rows, norm_gain):
    rows_f = rows.astype(jnp.float32)
    meansq = jnp.mean(rows_f * rows_f, axis=-1, keepdims=True) + 1e-06
    return (rows_f * lax.rsqrt(meansq) * norm_gain).astype(jnp.bfloat16)


def select_dot(sel, rows):
    return jnp.dot(sel, rows, preferred_element_type=jnp.float32)


def shards(
    text_embed,
    image_feats,
    tile_pos,
    proj_in,
    proj_out,
    norm_gain,
    shared_gate,
    shared_up,
    shared_down,
    expert_gate,
    expert_up,
    expert_down,
    route_ids,
    route_wts,
):
    bf16, f32 = jnp.bfloat16, jnp.float32
    tok_dev, width_model = text_embed.shape
    img_dev, width_vis = image_feats.shape
    n_data = lax.axis_size("dp")
    n_group = lax.axis_size("expert")
    peer = img_dev // n_data
    my_place = lax.axis_index("expert")

    route_cols = jnp.concatenate([route_ids, route_wts // 256, route_wts % 256], axis=1)
    route_cols = jnp.pad(route_cols, ((0, 0), (0, 128 - route_cols.shape[1])))

    dest_index = tile_pos // tok_dev // n_group
    order = jnp.argsort(dest_index, stable=True)
    offs_sorted = (tile_pos[order] % tok_dev).astype(bf16)
    pad = 128
    packed = jnp.concatenate(
        [image_feats[order], jnp.broadcast_to(offs_sorted[:, None], (img_dev, pad))], axis=1
    ).reshape(n_data, peer, width_vis + pad)
    moved = dp_all_to_all(packed, 0)
    moved = moved.reshape(img_dev, width_vis + pad)
    moved_feats = moved[:, :width_vis]
    moved_offs = moved[:, width_vis].astype(jnp.int32)

    feats = expert_all_gather(moved_feats, 5).reshape(n_group * img_dev, width_vis)
    vis_hidden = jax.nn.gelu(
        jnp.dot(feats, proj_in, preferred_element_type=f32), approximate=True
    ).astype(bf16)
    partial_proj = jnp.dot(vis_hidden, proj_out, preferred_element_type=f32).astype(bf16)
    projected = expert_reduce_scatter(
        partial_proj.reshape(n_group, img_dev, width_model), 3, bf16
    )

    place = (
        moved_offs[None, :] == jnp.arange(tok_dev, dtype=jnp.int32)[:, None]
    ).astype(bf16)
    placed = select_dot(place, projected)
    has_image = jnp.sum(place.astype(f32), axis=1, keepdims=True) > 0
    embed_own = jnp.where(has_image, placed, text_embed.astype(f32))
    normed_own = normalize(embed_own, norm_gain)

    gathered = expert_all_gather(
        jnp.concatenate([normed_own, route_cols.astype(bf16)], axis=1), 6
    ).reshape(n_group * tok_dev, width_model + route_cols.shape[1])
    normed = gathered[:, :width_model]
    routes = gathered[:, width_model:].astype(f32)
    top_count = route_ids.shape[1]
    ids = routes[:, :top_count].astype(jnp.int32)
    weights_f = routes[:, top_count : 2 * top_count] * 256.0 + routes[:, 2 * top_count : 3 * top_count]

    gate_s = jnp.dot(normed, shared_gate, preferred_element_type=f32)
    up_s = jnp.dot(normed, shared_up, preferred_element_type=f32)
    shared_hidden = (jax.nn.silu(gate_s) * up_s).astype(bf16)

    group_rows = normed.shape[0]
    n_pairs = group_rows * top_count
    capacity = 3 * group_rows * top_count // (2 * n_data)
    share = capacity // n_group
    flat_ids = ids.reshape(-1)
    onehot = (flat_ids[:, None] == jnp.arange(n_data, dtype=jnp.int32)[None, :]).astype(bf16)
    pair_iota = jnp.arange(n_pairs, dtype=jnp.int32)
    earlier = (pair_iota[None, :] < pair_iota[:, None]).astype(bf16)
    counts = select_dot(earlier, onehot)
    rank = jnp.sum(counts * onehot.astype(f32), axis=1).astype(jnp.int32)

    inside = rank // share == my_place
    row_of = jnp.where(inside, flat_ids * share + rank - my_place * share, -1)
    n_rows = n_data * share
    hit = (
        row_of.reshape(group_rows, top_count)[:, :, None]
        == jnp.arange(n_rows, dtype=jnp.int32)[None, None, :]
    )
    pick = jnp.sum(hit.astype(f32), axis=1).astype(bf16)
    send = select_dot(pick.T, normed).astype(bf16).reshape(n_data, share, width_model)
    arrived = dp_all_to_all(send, 1)
    slots = expert_all_gather(arrived.reshape(n_rows, width_model), 7).reshape(
        n_group * n_rows, width_model
    )

    gate_e = jnp.dot(slots, expert_gate[0], preferred_element_type=f32)
    up_e = jnp.dot(slots, expert_up[0], preferred_element_type=f32)
    hidden_e = (jax.nn.silu(gate_e) * up_e).astype(bf16)
    partial_out = jnp.dot(hidden_e, expert_down[0], preferred_element_type=f32).astype(bf16)
    summed = expert_reduce_scatter(partial_out.reshape(n_group, n_rows, width_model), 8, bf16)
    returned = dp_all_to_all(summed.reshape(n_data, share, width_model), 2).reshape(
        n_rows, width_model
    )

    weights_n = weights_f / jnp.sum(weights_f, axis=1, keepdims=True)
    coef = jnp.sum(jnp.where(hit, weights_n[:, :, None], 0.0), axis=1)
    coef_hi = coef.astype(bf16)
    coef_lo = (coef - coef_hi.astype(f32)).astype(bf16)
    combined = select_dot(coef_hi, returned) + select_dot(coef_lo, returned)
    total = expert_reduce_scatter(
        (jnp.dot(shared_hidden, shared_down, preferred_element_type=f32) + combined)
        .astype(bf16)
        .reshape(n_group, tok_dev, width_model),
        4,
        f32,
    )
    return (embed_own + total).astype(bf16)


def solution(mesh):
    return jax.shard_map(
        shards,
        mesh=mesh,
        in_specs=(
            P(("dp", "expert"), None),
            P(("dp", "expert"), None),
            P(("dp", "expert")),
            P(None, "expert"),
            P("expert", None),
            P(),
            P(None, "expert"),
            P(None, "expert"),
            P("expert", None),
            P("dp", None, "expert"),
            P("dp", None, "expert"),
            P("dp", "expert", None),
            P(("dp", "expert"), None),
            P(("dp", "expert"), None),
        ),
        out_specs=P(("dp", "expert"), None),
        check_vma=False,
    )
```

```python
import jax
import jax.numpy as jnp
from jax import lax
from jax.experimental import pallas as pl
from jax.experimental.pallas import tpu as pltpu
from jax.sharding import PartitionSpec as P


def dp_all_to_all(x, collective_id):
    n = x.shape[0]
    mesh_ids = pl.DeviceIdType.MESH

    def kernel(x_ref, y_ref, send_sem, recv_sem, local_sem):
        me = lax.axis_index("dp")
        j = lax.axis_index("expert")
        barrier = pltpu.get_barrier_semaphore()
        for k in range(1, n):
            pl.semaphore_signal(
                barrier, inc=1, device_id=(lax.rem(me + k, n), j), device_id_type=mesh_ids
            )
        pl.semaphore_wait(barrier, n - 1)
        local = pltpu.make_async_copy(x_ref.at[me], y_ref.at[me], local_sem)
        local.start()
        copies = []
        for k in range(1, n):
            peer = lax.rem(me + k, n)
            copy = pltpu.make_async_remote_copy(
                src_ref=x_ref.at[peer],
                dst_ref=y_ref.at[me],
                send_sem=send_sem.at[k],
                recv_sem=recv_sem.at[k],
                device_id=(peer, j),
                device_id_type=mesh_ids,
            )
            copy.start()
            copies.append(copy)
        local.wait()
        for copy in copies:
            copy.wait()

    return pl.pallas_call(
        kernel,
        out_shape=jax.ShapeDtypeStruct(x.shape, x.dtype),
        in_specs=[pl.BlockSpec(memory_space=pl.ANY)],
        out_specs=pl.BlockSpec(memory_space=pl.ANY),
        scratch_shapes=[
            pltpu.SemaphoreType.DMA((n,)),
            pltpu.SemaphoreType.DMA((n,)),
            pltpu.SemaphoreType.DMA,
        ],
        compiler_params=pltpu.CompilerParams(collective_id=collective_id, has_side_effects=True),
    )(x)


def expert_reduce_scatter(x, collective_id, out_dtype):
    n, rows, cols = x.shape
    chips = n // 2
    mesh_ids = pl.DeviceIdType.MESH

    def kernel(x_ref, o_ref, pair_buf, part, far_buf, send1, recv1, send2, recv2):
        me = lax.axis_index("expert")
        row = lax.axis_index("dp")
        chip, core = me // 2, me % 2
        sibling = chip * 2 + 1 - core
        barrier = pltpu.get_barrier_semaphore()
        pl.semaphore_signal(barrier, inc=1, device_id=(row, sibling), device_id_type=mesh_ids)
        for k in range(1, chips):
            pl.semaphore_signal(
                barrier,
                inc=1,
                device_id=(row, lax.rem(chip + k, chips) * 2 + core),
                device_id_type=mesh_ids,
            )
        pl.semaphore_wait(barrier, chips)
        first = pltpu.make_async_remote_copy(
            src_ref=x_ref.at[:, 1 - core],
            dst_ref=pair_buf,
            send_sem=send1,
            recv_sem=recv1,
            device_id=(row, sibling),
            device_id_type=mesh_ids,
        )
        first.start()
        first.wait()
        copies = []
        for k in range(1, chips):
            dest = lax.rem(chip + k, chips)
            part[k] = (
                x_ref[dest, core].astype(jnp.float32) + pair_buf[dest].astype(jnp.float32)
            ).astype(part.dtype)
            copy = pltpu.make_async_remote_copy(
                src_ref=part.at[k],
                dst_ref=far_buf.at[k],
                send_sem=send2.at[k],
                recv_sem=recv2.at[k],
                device_id=(row, dest * 2 + core),
                device_id_type=mesh_ids,
            )
            copy.start()
            copies.append(copy)
        acc = x_ref[chip, core].astype(jnp.float32) + pair_buf[chip].astype(jnp.float32)
        for k, copy in enumerate(copies, 1):
            copy.wait()
            acc = acc + far_buf[k].astype(jnp.float32)
        o_ref[...] = acc.astype(o_ref.dtype)

    return pl.pallas_call(
        kernel,
        out_shape=jax.ShapeDtypeStruct((rows, cols), out_dtype),
        in_specs=[pl.BlockSpec(memory_space=pltpu.VMEM)],
        out_specs=pl.BlockSpec(memory_space=pltpu.VMEM),
        scratch_shapes=[
            pltpu.VMEM((chips, rows, cols), x.dtype),
            pltpu.VMEM((chips, rows, cols), x.dtype),
            pltpu.VMEM((chips, rows, cols), x.dtype),
            pltpu.SemaphoreType.DMA,
            pltpu.SemaphoreType.DMA,
            pltpu.SemaphoreType.DMA((chips,)),
            pltpu.SemaphoreType.DMA((chips,)),
        ],
        compiler_params=pltpu.CompilerParams(collective_id=collective_id, has_side_effects=True),
    )(x.reshape(chips, 2, rows, cols))


def expert_all_gather(x, collective_id):
    rows, cols = x.shape
    n = lax.axis_size("expert")
    chips = n // 2
    mesh_ids = pl.DeviceIdType.MESH

    def kernel(x_ref, o_ref, send0, recv0, send1, recv1, send2, recv2):
        me = lax.axis_index("expert")
        row = lax.axis_index("dp")
        chip, core = me // 2, me % 2
        sibling = chip * 2 + 1 - core
        barrier = pltpu.get_barrier_semaphore()
        pl.semaphore_signal(barrier, inc=1, device_id=(row, sibling), device_id_type=mesh_ids)
        for k in range(1, chips):
            pl.semaphore_signal(
                barrier,
                inc=1,
                device_id=(row, lax.rem(chip + k, chips) * 2 + core),
                device_id_type=mesh_ids,
            )
        pl.semaphore_wait(barrier, chips)
        near = pltpu.make_async_remote_copy(
            src_ref=x_ref,
            dst_ref=o_ref.at[me],
            send_sem=send0,
            recv_sem=recv0,
            device_id=(row, sibling),
            device_id_type=mesh_ids,
        )
        near.start()
        far = []
        for k in range(1, chips):
            copy = pltpu.make_async_remote_copy(
                src_ref=x_ref,
                dst_ref=o_ref.at[me],
                send_sem=send1.at[k],
                recv_sem=recv1.at[k],
                device_id=(row, lax.rem(chip + k, chips) * 2 + core),
                device_id_type=mesh_ids,
            )
            copy.start()
            far.append(copy)
        o_ref[me] = x_ref[...]
        passed = []
        for k, copy in enumerate(far, 1):
            copy.wait_recv()
            source = lax.rem(chip - k + chips, chips) * 2 + core
            relay = pltpu.make_async_remote_copy(
                src_ref=o_ref.at[source],
                dst_ref=o_ref.at[source],
                send_sem=send2.at[k],
                recv_sem=recv2.at[k],
                device_id=(row, sibling),
                device_id_type=mesh_ids,
            )
            relay.start()
            passed.append(relay)
        near.wait()
        for copy in far:
            copy.wait_send()
        for relay in passed:
            relay.wait()

    return pl.pallas_call(
        kernel,
        out_shape=jax.ShapeDtypeStruct((n, rows, cols), x.dtype),
        in_specs=[pl.BlockSpec(memory_space=pltpu.VMEM)],
        out_specs=pl.BlockSpec(memory_space=pltpu.VMEM),
        scratch_shapes=[
            pltpu.SemaphoreType.DMA,
            pltpu.SemaphoreType.DMA,
            pltpu.SemaphoreType.DMA((chips,)),
            pltpu.SemaphoreType.DMA((chips,)),
            pltpu.SemaphoreType.DMA((chips,)),
            pltpu.SemaphoreType.DMA((chips,)),
        ],
        compiler_params=pltpu.CompilerParams(collective_id=collective_id, has_side_effects=True),
    )(x)


def normalize(rows, norm_gain):
    rows_f = rows.astype(jnp.float32)
    meansq = jnp.mean(rows_f * rows_f, axis=-1, keepdims=True) + 1e-06
    return (rows_f * lax.rsqrt(meansq) * norm_gain).astype(jnp.bfloat16)


def select_dot(sel, rows):
    return jnp.dot(sel, rows, preferred_element_type=jnp.float32)


def shards(
    text_embed,
    image_feats,
    tile_pos,
    proj_in,
    proj_out,
    norm_gain,
    shared_gate,
    shared_up,
    shared_down,
    expert_gate,
    expert_up,
    expert_down,
    route_ids,
    route_wts,
):
    bf16, f32 = jnp.bfloat16, jnp.float32
    tok_dev, width_model = text_embed.shape
    img_dev, width_vis = image_feats.shape
    n_data = lax.axis_size("dp")
    n_group = lax.axis_size("expert")
    peer = img_dev // n_data
    my_place = lax.axis_index("expert")

    route_cols = jnp.concatenate([route_ids, route_wts // 256, route_wts % 256], axis=1)
    route_cols = jnp.pad(route_cols, ((0, 0), (0, 128 - route_cols.shape[1])))

    dest_index = tile_pos // tok_dev // n_group
    order = jnp.argsort(dest_index, stable=True)
    offs_sorted = (tile_pos[order] % tok_dev).astype(bf16)
    pad = 128
    packed = jnp.concatenate(
        [image_feats[order], jnp.broadcast_to(offs_sorted[:, None], (img_dev, pad))], axis=1
    ).reshape(n_data, peer, width_vis + pad)
    moved = dp_all_to_all(packed, 0)
    moved = moved.reshape(img_dev, width_vis + pad)
    moved_feats = moved[:, :width_vis]
    moved_offs = moved[:, width_vis].astype(jnp.int32)

    feats = expert_all_gather(moved_feats, 5).reshape(n_group * img_dev, width_vis)
    vis_hidden = jax.nn.gelu(
        jnp.dot(feats, proj_in, preferred_element_type=f32), approximate=True
    ).astype(bf16)
    partial_proj = jnp.dot(vis_hidden, proj_out, preferred_element_type=f32).astype(bf16)
    projected = expert_reduce_scatter(
        partial_proj.reshape(n_group, img_dev, width_model), 3, bf16
    )

    place = (
        moved_offs[None, :] == jnp.arange(tok_dev, dtype=jnp.int32)[:, None]
    ).astype(bf16)
    placed = select_dot(place, projected)
    has_image = jnp.sum(place.astype(f32), axis=1, keepdims=True) > 0
    embed_own = jnp.where(has_image, placed, text_embed.astype(f32))
    normed_own = normalize(embed_own, norm_gain)

    gathered = expert_all_gather(
        jnp.concatenate([normed_own, route_cols.astype(bf16)], axis=1), 6
    ).reshape(n_group * tok_dev, width_model + route_cols.shape[1])
    normed = gathered[:, :width_model]
    routes = gathered[:, width_model:].astype(f32)
    top_count = route_ids.shape[1]
    ids = routes[:, :top_count].astype(jnp.int32)
    weights_f = routes[:, top_count : 2 * top_count] * 256.0 + routes[:, 2 * top_count : 3 * top_count]

    gate_s = jnp.dot(normed, shared_gate, preferred_element_type=f32)
    up_s = jnp.dot(normed, shared_up, preferred_element_type=f32)
    shared_hidden = (jax.nn.silu(gate_s) * up_s).astype(bf16)

    group_rows = normed.shape[0]
    n_pairs = group_rows * top_count
    capacity = 3 * group_rows * top_count // (2 * n_data)
    share = capacity // n_group
    flat_ids = ids.reshape(-1)
    onehot = (flat_ids[:, None] == jnp.arange(n_data, dtype=jnp.int32)[None, :]).astype(bf16)
    pair_iota = jnp.arange(n_pairs, dtype=jnp.int32)
    earlier = (pair_iota[None, :] < pair_iota[:, None]).astype(bf16)
    counts = select_dot(earlier, onehot)
    rank = jnp.sum(counts * onehot.astype(f32), axis=1).astype(jnp.int32)

    inside = rank // share == my_place
    row_of = jnp.where(inside, flat_ids * share + rank - my_place * share, -1)
    n_rows = n_data * share
    hit = (
        row_of.reshape(group_rows, top_count)[:, :, None]
        == jnp.arange(n_rows, dtype=jnp.int32)[None, None, :]
    )
    pick = jnp.sum(hit.astype(f32), axis=1).astype(bf16)
    send = select_dot(pick.T, normed).astype(bf16).reshape(n_data, share, width_model)
    arrived = dp_all_to_all(send, 1)
    slots = lax.all_gather(arrived.reshape(n_rows, width_model), "expert", axis=0, tiled=True)

    width_e = expert_gate.shape[2]
    gate_up = jnp.dot(
        slots, jnp.concatenate([expert_gate[0], expert_up[0]], axis=1), preferred_element_type=f32
    )
    gate_e, up_e = gate_up[:, :width_e], gate_up[:, width_e:]
    hidden_e = (jax.nn.silu(gate_e) * up_e).astype(bf16)
    partial_out = jnp.dot(hidden_e, expert_down[0], preferred_element_type=f32).astype(bf16)
    summed = lax.psum_scatter(partial_out, "expert", scatter_dimension=0, tiled=True)
    returned = dp_all_to_all(summed.reshape(n_data, share, width_model), 2).reshape(
        n_rows, width_model
    )

    weights_n = weights_f / jnp.sum(weights_f, axis=1, keepdims=True)
    coef = jnp.sum(jnp.where(hit, weights_n[:, :, None], 0.0), axis=1)
    coef_hi = coef.astype(bf16)
    coef_lo = (coef - coef_hi.astype(f32)).astype(bf16)
    terms = jnp.dot(
        jnp.concatenate([shared_hidden, coef_hi, coef_lo], axis=1),
        jnp.concatenate([shared_down, returned, returned], axis=0),
        preferred_element_type=f32,
    )
    total = expert_reduce_scatter(
        terms.astype(bf16)
        .reshape(n_group, tok_dev, width_model),
        4,
        f32,
    )
    return (embed_own + total).astype(bf16)


def solution(mesh):
    return jax.shard_map(
        shards,
        mesh=mesh,
        in_specs=(
            P(("dp", "expert"), None),
            P(("dp", "expert"), None),
            P(("dp", "expert")),
            P(None, "expert"),
            P("expert", None),
            P(),
            P(None, "expert"),
            P(None, "expert"),
            P("expert", None),
            P("dp", None, "expert"),
            P("dp", None, "expert"),
            P("dp", "expert", None),
            P(("dp", "expert"), None),
            P(("dp", "expert"), None),
        ),
        out_specs=P(("dp", "expert"), None),
        check_vma=False,
    )
```

```python
import jax
import jax.numpy as jnp
from jax import lax
from jax.experimental import pallas as pl
from jax.experimental.pallas import tpu as pltpu
from jax.sharding import PartitionSpec as P


def dp_all_to_all(x, collective_id):
    n = x.shape[0]
    mesh_ids = pl.DeviceIdType.MESH

    def kernel(x_ref, y_ref, send_sem, recv_sem, local_sem):
        me = lax.axis_index("dp")
        j = lax.axis_index("expert")
        barrier = pltpu.get_barrier_semaphore()
        for k in range(1, n):
            pl.semaphore_signal(
                barrier, inc=1, device_id=(lax.rem(me + k, n), j), device_id_type=mesh_ids
            )
        pl.semaphore_wait(barrier, n - 1)
        local = pltpu.make_async_copy(x_ref.at[me], y_ref.at[me], local_sem)
        local.start()
        copies = []
        for k in range(1, n):
            peer = lax.rem(me + k, n)
            copy = pltpu.make_async_remote_copy(
                src_ref=x_ref.at[peer],
                dst_ref=y_ref.at[me],
                send_sem=send_sem.at[k],
                recv_sem=recv_sem.at[k],
                device_id=(peer, j),
                device_id_type=mesh_ids,
            )
            copy.start()
            copies.append(copy)
        local.wait()
        for copy in copies:
            copy.wait()

    return pl.pallas_call(
        kernel,
        out_shape=jax.ShapeDtypeStruct(x.shape, x.dtype),
        in_specs=[pl.BlockSpec(memory_space=pl.ANY)],
        out_specs=pl.BlockSpec(memory_space=pl.ANY),
        scratch_shapes=[
            pltpu.SemaphoreType.DMA((n,)),
            pltpu.SemaphoreType.DMA((n,)),
            pltpu.SemaphoreType.DMA,
        ],
        compiler_params=pltpu.CompilerParams(collective_id=collective_id, has_side_effects=True),
    )(x)


def expert_reduce_scatter(x, collective_id, out_dtype):
    n, rows, cols = x.shape
    chips = n // 2
    mesh_ids = pl.DeviceIdType.MESH

    def kernel(x_ref, o_ref, pair_buf, part, far_buf, send1, recv1, send2, recv2):
        me = lax.axis_index("expert")
        row = lax.axis_index("dp")
        chip, core = me // 2, me % 2
        sibling = chip * 2 + 1 - core
        barrier = pltpu.get_barrier_semaphore()
        pl.semaphore_signal(barrier, inc=1, device_id=(row, sibling), device_id_type=mesh_ids)
        for k in range(1, chips):
            pl.semaphore_signal(
                barrier,
                inc=1,
                device_id=(row, lax.rem(chip + k, chips) * 2 + core),
                device_id_type=mesh_ids,
            )
        pl.semaphore_wait(barrier, chips)
        first = pltpu.make_async_remote_copy(
            src_ref=x_ref.at[:, 1 - core],
            dst_ref=pair_buf,
            send_sem=send1,
            recv_sem=recv1,
            device_id=(row, sibling),
            device_id_type=mesh_ids,
        )
        first.start()
        first.wait()
        copies = []
        for k in range(1, chips):
            dest = lax.rem(chip + k, chips)
            part[k] = (
                x_ref[dest, core].astype(jnp.float32) + pair_buf[dest].astype(jnp.float32)
            ).astype(part.dtype)
            copy = pltpu.make_async_remote_copy(
                src_ref=part.at[k],
                dst_ref=far_buf.at[k],
                send_sem=send2.at[k],
                recv_sem=recv2.at[k],
                device_id=(row, dest * 2 + core),
                device_id_type=mesh_ids,
            )
            copy.start()
            copies.append(copy)
        acc = x_ref[chip, core].astype(jnp.float32) + pair_buf[chip].astype(jnp.float32)
        for k, copy in enumerate(copies, 1):
            copy.wait()
            acc = acc + far_buf[k].astype(jnp.float32)
        o_ref[...] = acc.astype(o_ref.dtype)

    return pl.pallas_call(
        kernel,
        out_shape=jax.ShapeDtypeStruct((rows, cols), out_dtype),
        in_specs=[pl.BlockSpec(memory_space=pltpu.VMEM)],
        out_specs=pl.BlockSpec(memory_space=pltpu.VMEM),
        scratch_shapes=[
            pltpu.VMEM((chips, rows, cols), x.dtype),
            pltpu.VMEM((chips, rows, cols), x.dtype),
            pltpu.VMEM((chips, rows, cols), x.dtype),
            pltpu.SemaphoreType.DMA,
            pltpu.SemaphoreType.DMA,
            pltpu.SemaphoreType.DMA((chips,)),
            pltpu.SemaphoreType.DMA((chips,)),
        ],
        compiler_params=pltpu.CompilerParams(collective_id=collective_id, has_side_effects=True),
    )(x.reshape(chips, 2, rows, cols))


def expert_all_gather(x, collective_id):
    rows, cols = x.shape
    n = lax.axis_size("expert")
    chips = n // 2
    mesh_ids = pl.DeviceIdType.MESH

    def kernel(x_ref, o_ref, send0, recv0, send1, recv1, send2, recv2):
        me = lax.axis_index("expert")
        row = lax.axis_index("dp")
        chip, core = me // 2, me % 2
        sibling = chip * 2 + 1 - core
        barrier = pltpu.get_barrier_semaphore()
        pl.semaphore_signal(barrier, inc=1, device_id=(row, sibling), device_id_type=mesh_ids)
        for k in range(1, chips):
            pl.semaphore_signal(
                barrier,
                inc=1,
                device_id=(row, lax.rem(chip + k, chips) * 2 + core),
                device_id_type=mesh_ids,
            )
        pl.semaphore_wait(barrier, chips)
        near = pltpu.make_async_remote_copy(
            src_ref=x_ref,
            dst_ref=o_ref.at[me],
            send_sem=send0,
            recv_sem=recv0,
            device_id=(row, sibling),
            device_id_type=mesh_ids,
        )
        near.start()
        far = []
        for k in range(1, chips):
            copy = pltpu.make_async_remote_copy(
                src_ref=x_ref,
                dst_ref=o_ref.at[me],
                send_sem=send1.at[k],
                recv_sem=recv1.at[k],
                device_id=(row, lax.rem(chip + k, chips) * 2 + core),
                device_id_type=mesh_ids,
            )
            copy.start()
            far.append(copy)
        o_ref[me] = x_ref[...]
        passed = []
        for k, copy in enumerate(far, 1):
            copy.wait_recv()
            source = lax.rem(chip - k + chips, chips) * 2 + core
            relay = pltpu.make_async_remote_copy(
                src_ref=o_ref.at[source],
                dst_ref=o_ref.at[source],
                send_sem=send2.at[k],
                recv_sem=recv2.at[k],
                device_id=(row, sibling),
                device_id_type=mesh_ids,
            )
            relay.start()
            passed.append(relay)
        near.wait()
        for copy in far:
            copy.wait_send()
        for relay in passed:
            relay.wait()

    return pl.pallas_call(
        kernel,
        out_shape=jax.ShapeDtypeStruct((n, rows, cols), x.dtype),
        in_specs=[pl.BlockSpec(memory_space=pltpu.VMEM)],
        out_specs=pl.BlockSpec(memory_space=pltpu.VMEM),
        scratch_shapes=[
            pltpu.SemaphoreType.DMA,
            pltpu.SemaphoreType.DMA,
            pltpu.SemaphoreType.DMA((chips,)),
            pltpu.SemaphoreType.DMA((chips,)),
            pltpu.SemaphoreType.DMA((chips,)),
            pltpu.SemaphoreType.DMA((chips,)),
        ],
        compiler_params=pltpu.CompilerParams(collective_id=collective_id, has_side_effects=True),
    )(x)


def normalize(rows, norm_gain):
    rows_f = rows.astype(jnp.float32)
    meansq = jnp.mean(rows_f * rows_f, axis=-1, keepdims=True) + 1e-06
    return (rows_f * lax.rsqrt(meansq) * norm_gain).astype(jnp.bfloat16)


def select_dot(sel, rows):
    return jnp.dot(sel, rows, preferred_element_type=jnp.float32)


def shards(
    text_embed,
    image_feats,
    tile_pos,
    proj_in,
    proj_out,
    norm_gain,
    shared_gate,
    shared_up,
    shared_down,
    expert_gate,
    expert_up,
    expert_down,
    route_ids,
    route_wts,
):
    bf16, f32 = jnp.bfloat16, jnp.float32
    tok_dev, width_model = text_embed.shape
    img_dev, width_vis = image_feats.shape
    n_data = lax.axis_size("dp")
    n_group = lax.axis_size("expert")
    peer = img_dev // n_data
    my_place = lax.axis_index("expert")

    route_cols = jnp.concatenate([route_ids, route_wts // 256, route_wts % 256], axis=1)
    route_cols = jnp.pad(route_cols, ((0, 0), (0, 128 - route_cols.shape[1])))

    dest_index = tile_pos // tok_dev // n_group
    order = jnp.argsort(dest_index, stable=True)
    offs_sorted = (tile_pos[order] % tok_dev).astype(bf16)
    pad = 128
    packed = jnp.concatenate(
        [image_feats[order], jnp.broadcast_to(offs_sorted[:, None], (img_dev, pad))], axis=1
    ).reshape(n_data, peer, width_vis + pad)
    moved = dp_all_to_all(packed, 0)
    moved = moved.reshape(img_dev, width_vis + pad)
    moved_feats = moved[:, :width_vis]
    moved_offs = moved[:, width_vis].astype(jnp.int32)

    feats = expert_all_gather(moved_feats, 5).reshape(n_group * img_dev, width_vis)
    vis_hidden = jax.nn.gelu(
        jnp.dot(feats, proj_in, preferred_element_type=f32), approximate=True
    ).astype(bf16)
    partial_proj = jnp.dot(vis_hidden, proj_out, preferred_element_type=f32).astype(bf16)
    projected = expert_reduce_scatter(
        partial_proj.reshape(n_group, img_dev, width_model), 3, bf16
    )

    place = (
        moved_offs[None, :] == jnp.arange(tok_dev, dtype=jnp.int32)[:, None]
    ).astype(bf16)
    placed = select_dot(place, projected)
    has_image = jnp.sum(place.astype(f32), axis=1, keepdims=True) > 0
    embed_own = jnp.where(has_image, placed, text_embed.astype(f32))
    normed_own = normalize(embed_own, norm_gain)

    gathered = expert_all_gather(
        jnp.concatenate([normed_own, route_cols.astype(bf16)], axis=1), 6
    ).reshape(n_group * tok_dev, width_model + route_cols.shape[1])
    normed = gathered[:, :width_model]
    routes = gathered[:, width_model:].astype(f32)
    top_count = route_ids.shape[1]
    ids = routes[:, :top_count].astype(jnp.int32)
    weights_f = routes[:, top_count : 2 * top_count] * 256.0 + routes[:, 2 * top_count : 3 * top_count]

    gate_s = jnp.dot(normed, shared_gate, preferred_element_type=f32)
    up_s = jnp.dot(normed, shared_up, preferred_element_type=f32)
    shared_hidden = (jax.nn.silu(gate_s) * up_s).astype(bf16)

    group_rows = normed.shape[0]
    n_pairs = group_rows * top_count
    capacity = 3 * group_rows * top_count // (2 * n_data)
    share = capacity // n_group
    flat_ids = ids.reshape(-1)
    onehot = (flat_ids[:, None] == jnp.arange(n_data, dtype=jnp.int32)[None, :]).astype(bf16)
    pair_iota = jnp.arange(n_pairs, dtype=jnp.int32)
    earlier = (pair_iota[None, :] < pair_iota[:, None]).astype(bf16)
    counts = select_dot(earlier, onehot)
    rank = jnp.sum(counts * onehot.astype(f32), axis=1).astype(jnp.int32)

    inside = rank // share == my_place
    row_of = jnp.where(inside, flat_ids * share + rank - my_place * share, -1)
    n_rows = n_data * share
    hit = (
        row_of.reshape(group_rows, top_count)[:, :, None]
        == jnp.arange(n_rows, dtype=jnp.int32)[None, None, :]
    )
    pick = jnp.sum(hit.astype(f32), axis=1).astype(bf16)
    lanes = 128
    block = (n_data, share * width_model // lanes, lanes)
    send = select_dot(pick.T, normed).astype(bf16).reshape(block)
    arrived = lax.all_to_all(send, "dp", split_axis=0, concat_axis=0, tiled=True)
    slots = lax.all_gather(arrived.reshape(n_rows, width_model), "expert", axis=0, tiled=True)

    width_e = expert_gate.shape[2]
    gate_up = jnp.dot(
        slots, jnp.concatenate([expert_gate[0], expert_up[0]], axis=1), preferred_element_type=f32
    )
    gate_e, up_e = gate_up[:, :width_e], gate_up[:, width_e:]
    hidden_e = (jax.nn.silu(gate_e) * up_e).astype(bf16)
    partial_out = jnp.dot(hidden_e, expert_down[0], preferred_element_type=f32).astype(bf16)
    summed = lax.psum_scatter(partial_out, "expert", scatter_dimension=0, tiled=True)
    returned = lax.all_to_all(
        summed.reshape(block), "dp", split_axis=0, concat_axis=0, tiled=True
    ).reshape(n_rows, width_model)

    weights_n = weights_f / jnp.sum(weights_f, axis=1, keepdims=True)
    coef = jnp.sum(jnp.where(hit, weights_n[:, :, None], 0.0), axis=1)
    coef_hi = coef.astype(bf16)
    coef_lo = (coef - coef_hi.astype(f32)).astype(bf16)
    terms = jnp.dot(
        jnp.concatenate([shared_hidden, coef_hi, coef_lo], axis=1),
        jnp.concatenate([shared_down, returned, returned], axis=0),
        preferred_element_type=f32,
    )
    total = expert_reduce_scatter(
        terms.astype(bf16)
        .reshape(n_group, tok_dev, width_model),
        4,
        f32,
    )
    return (embed_own + total).astype(bf16)


def solution(mesh):
    return jax.shard_map(
        shards,
        mesh=mesh,
        in_specs=(
            P(("dp", "expert"), None),
            P(("dp", "expert"), None),
            P(("dp", "expert")),
            P(None, "expert"),
            P("expert", None),
            P(),
            P(None, "expert"),
            P(None, "expert"),
            P("expert", None),
            P("dp", None, "expert"),
            P("dp", None, "expert"),
            P("dp", "expert", None),
            P(("dp", "expert"), None),
            P(("dp", "expert"), None),
        ),
        out_specs=P(("dp", "expert"), None),
        check_vma=False,
    )
```

```python
import jax
import jax.numpy as jnp
from jax import lax
from jax.experimental import pallas as pl
from jax.experimental.pallas import tpu as pltpu
from jax.sharding import PartitionSpec as P


def dp_all_to_all(x, collective_id):
    n = x.shape[0]
    mesh_ids = pl.DeviceIdType.MESH

    def kernel(x_ref, y_ref, send_sem, recv_sem, local_sem):
        me = lax.axis_index("dp")
        j = lax.axis_index("expert")
        barrier = pltpu.get_barrier_semaphore()
        for k in range(1, n):
            pl.semaphore_signal(
                barrier, inc=1, device_id=(lax.rem(me + k, n), j), device_id_type=mesh_ids
            )
        pl.semaphore_wait(barrier, n - 1)
        local = pltpu.make_async_copy(x_ref.at[me], y_ref.at[me], local_sem)
        local.start()
        copies = []
        for k in range(1, n):
            peer = lax.rem(me + k, n)
            copy = pltpu.make_async_remote_copy(
                src_ref=x_ref.at[peer],
                dst_ref=y_ref.at[me],
                send_sem=send_sem.at[k],
                recv_sem=recv_sem.at[k],
                device_id=(peer, j),
                device_id_type=mesh_ids,
            )
            copy.start()
            copies.append(copy)
        local.wait()
        for copy in copies:
            copy.wait()

    return pl.pallas_call(
        kernel,
        out_shape=jax.ShapeDtypeStruct(x.shape, x.dtype),
        in_specs=[pl.BlockSpec(memory_space=pl.ANY)],
        out_specs=pl.BlockSpec(memory_space=pl.ANY),
        scratch_shapes=[
            pltpu.SemaphoreType.DMA((n,)),
            pltpu.SemaphoreType.DMA((n,)),
            pltpu.SemaphoreType.DMA,
        ],
        compiler_params=pltpu.CompilerParams(collective_id=collective_id, has_side_effects=True),
    )(x)


def expert_reduce_scatter(x, collective_id, out_dtype):
    n, rows, cols = x.shape
    chips = n // 2
    mesh_ids = pl.DeviceIdType.MESH

    def kernel(x_ref, o_ref, pair_buf, part, far_buf, send1, recv1, send2, recv2):
        me = lax.axis_index("expert")
        row = lax.axis_index("dp")
        chip, core = me // 2, me % 2
        sibling = chip * 2 + 1 - core
        barrier = pltpu.get_barrier_semaphore()
        pl.semaphore_signal(barrier, inc=1, device_id=(row, sibling), device_id_type=mesh_ids)
        for k in range(1, chips):
            pl.semaphore_signal(
                barrier,
                inc=1,
                device_id=(row, lax.rem(chip + k, chips) * 2 + core),
                device_id_type=mesh_ids,
            )
        pl.semaphore_wait(barrier, chips)
        first = pltpu.make_async_remote_copy(
            src_ref=x_ref.at[:, 1 - core],
            dst_ref=pair_buf,
            send_sem=send1,
            recv_sem=recv1,
            device_id=(row, sibling),
            device_id_type=mesh_ids,
        )
        first.start()
        first.wait()
        copies = []
        for k in range(1, chips):
            dest = lax.rem(chip + k, chips)
            part[k] = (
                x_ref[dest, core].astype(jnp.float32) + pair_buf[dest].astype(jnp.float32)
            ).astype(part.dtype)
            copy = pltpu.make_async_remote_copy(
                src_ref=part.at[k],
                dst_ref=far_buf.at[k],
                send_sem=send2.at[k],
                recv_sem=recv2.at[k],
                device_id=(row, dest * 2 + core),
                device_id_type=mesh_ids,
            )
            copy.start()
            copies.append(copy)
        acc = x_ref[chip, core].astype(jnp.float32) + pair_buf[chip].astype(jnp.float32)
        for k, copy in enumerate(copies, 1):
            copy.wait()
            acc = acc + far_buf[k].astype(jnp.float32)
        o_ref[...] = acc.astype(o_ref.dtype)

    return pl.pallas_call(
        kernel,
        out_shape=jax.ShapeDtypeStruct((rows, cols), out_dtype),
        in_specs=[pl.BlockSpec(memory_space=pltpu.VMEM)],
        out_specs=pl.BlockSpec(memory_space=pltpu.VMEM),
        scratch_shapes=[
            pltpu.VMEM((chips, rows, cols), x.dtype),
            pltpu.VMEM((chips, rows, cols), x.dtype),
            pltpu.VMEM((chips, rows, cols), x.dtype),
            pltpu.SemaphoreType.DMA,
            pltpu.SemaphoreType.DMA,
            pltpu.SemaphoreType.DMA((chips,)),
            pltpu.SemaphoreType.DMA((chips,)),
        ],
        compiler_params=pltpu.CompilerParams(collective_id=collective_id, has_side_effects=True),
    )(x.reshape(chips, 2, rows, cols))


def expert_all_gather(x, collective_id):
    rows, cols = x.shape
    n = lax.axis_size("expert")
    chips = n // 2
    mesh_ids = pl.DeviceIdType.MESH

    def kernel(x_ref, o_ref, send0, recv0, send1, recv1, send2, recv2):
        me = lax.axis_index("expert")
        row = lax.axis_index("dp")
        chip, core = me // 2, me % 2
        sibling = chip * 2 + 1 - core
        barrier = pltpu.get_barrier_semaphore()
        pl.semaphore_signal(barrier, inc=1, device_id=(row, sibling), device_id_type=mesh_ids)
        for k in range(1, chips):
            pl.semaphore_signal(
                barrier,
                inc=1,
                device_id=(row, lax.rem(chip + k, chips) * 2 + core),
                device_id_type=mesh_ids,
            )
        pl.semaphore_wait(barrier, chips)
        near = pltpu.make_async_remote_copy(
            src_ref=x_ref,
            dst_ref=o_ref.at[me],
            send_sem=send0,
            recv_sem=recv0,
            device_id=(row, sibling),
            device_id_type=mesh_ids,
        )
        near.start()
        far = []
        for k in range(1, chips):
            copy = pltpu.make_async_remote_copy(
                src_ref=x_ref,
                dst_ref=o_ref.at[me],
                send_sem=send1.at[k],
                recv_sem=recv1.at[k],
                device_id=(row, lax.rem(chip + k, chips) * 2 + core),
                device_id_type=mesh_ids,
            )
            copy.start()
            far.append(copy)
        o_ref[me] = x_ref[...]
        passed = []
        for k, copy in enumerate(far, 1):
            copy.wait_recv()
            source = lax.rem(chip - k + chips, chips) * 2 + core
            relay = pltpu.make_async_remote_copy(
                src_ref=o_ref.at[source],
                dst_ref=o_ref.at[source],
                send_sem=send2.at[k],
                recv_sem=recv2.at[k],
                device_id=(row, sibling),
                device_id_type=mesh_ids,
            )
            relay.start()
            passed.append(relay)
        near.wait()
        for copy in far:
            copy.wait_send()
        for relay in passed:
            relay.wait()

    return pl.pallas_call(
        kernel,
        out_shape=jax.ShapeDtypeStruct((n, rows, cols), x.dtype),
        in_specs=[pl.BlockSpec(memory_space=pltpu.VMEM)],
        out_specs=pl.BlockSpec(memory_space=pltpu.VMEM),
        scratch_shapes=[
            pltpu.SemaphoreType.DMA,
            pltpu.SemaphoreType.DMA,
            pltpu.SemaphoreType.DMA((chips,)),
            pltpu.SemaphoreType.DMA((chips,)),
            pltpu.SemaphoreType.DMA((chips,)),
            pltpu.SemaphoreType.DMA((chips,)),
        ],
        compiler_params=pltpu.CompilerParams(collective_id=collective_id, has_side_effects=True),
    )(x)


def fused_projector(feats, proj_in, proj_out, collective_id):
    rows, width_vis = feats.shape
    n = lax.axis_size("expert")
    width_model = proj_out.shape[1]
    mesh_ids = pl.DeviceIdType.MESH
    f32, bf16 = jnp.float32, jnp.bfloat16

    def kernel(f_ref, wi_ref, wo_ref, o_ref, fbuf, psend, pbuf, send_f, recv_f, send_p, recv_p):
        me = lax.axis_index("expert")
        row = lax.axis_index("dp")
        barrier = pltpu.get_barrier_semaphore()
        for k in range(1, n):
            pl.semaphore_signal(
                barrier, inc=1, device_id=(row, lax.rem(me + k, n)), device_id_type=mesh_ids
            )
        pl.semaphore_wait(barrier, n - 1)
        feat_copies = []
        for k in range(1, n):
            copy = pltpu.make_async_remote_copy(
                src_ref=f_ref,
                dst_ref=fbuf.at[me],
                send_sem=send_f.at[k],
                recv_sem=recv_f.at[k],
                device_id=(row, lax.rem(me + k, n)),
                device_id_type=mesh_ids,
            )
            copy.start()
            feat_copies.append(copy)

        def partial(x):
            hidden = jnp.dot(x, wi_ref[...], preferred_element_type=f32)
            hidden = jax.nn.gelu(hidden, approximate=True).astype(bf16)
            return jnp.dot(hidden, wo_ref[...], preferred_element_type=f32)

        acc = partial(f_ref[...])
        part_copies = []
        for k, copy in enumerate(feat_copies, 1):
            copy.wait_recv()
            source = lax.rem(me - k + n, n)
            psend[k] = partial(fbuf[source]).astype(bf16)
            back = pltpu.make_async_remote_copy(
                src_ref=psend.at[k],
                dst_ref=pbuf.at[k],
                send_sem=send_p.at[k],
                recv_sem=recv_p.at[k],
                device_id=(row, source),
                device_id_type=mesh_ids,
            )
            back.start()
            part_copies.append(back)
        for k, back in enumerate(part_copies, 1):
            back.wait_recv()
            acc = acc + pbuf[k].astype(f32)
        o_ref[...] = acc.astype(o_ref.dtype)
        for copy in feat_copies:
            copy.wait_send()
        for back in part_copies:
            back.wait_send()

    return pl.pallas_call(
        kernel,
        out_shape=jax.ShapeDtypeStruct((rows, width_model), bf16),
        in_specs=[pl.BlockSpec(memory_space=pltpu.VMEM)] * 3,
        out_specs=pl.BlockSpec(memory_space=pltpu.VMEM),
        scratch_shapes=[
            pltpu.VMEM((n, rows, width_vis), feats.dtype),
            pltpu.VMEM((n, rows, width_model), bf16),
            pltpu.VMEM((n, rows, width_model), bf16),
            pltpu.SemaphoreType.DMA((n,)),
            pltpu.SemaphoreType.DMA((n,)),
            pltpu.SemaphoreType.DMA((n,)),
            pltpu.SemaphoreType.DMA((n,)),
        ],
        compiler_params=pltpu.CompilerParams(
            collective_id=collective_id, has_side_effects=True, vmem_limit_bytes=48 * 1024 * 1024
        ),
    )(feats, proj_in, proj_out)


def normalize(rows, norm_gain):
    rows_f = rows.astype(jnp.float32)
    meansq = jnp.mean(rows_f * rows_f, axis=-1, keepdims=True) + 1e-06
    return (rows_f * lax.rsqrt(meansq) * norm_gain).astype(jnp.bfloat16)


def select_dot(sel, rows):
    return jnp.dot(sel, rows, preferred_element_type=jnp.float32)


def shards(
    text_embed,
    image_feats,
    tile_pos,
    proj_in,
    proj_out,
    norm_gain,
    shared_gate,
    shared_up,
    shared_down,
    expert_gate,
    expert_up,
    expert_down,
    route_ids,
    route_wts,
):
    bf16, f32 = jnp.bfloat16, jnp.float32
    tok_dev, width_model = text_embed.shape
    img_dev, width_vis = image_feats.shape
    n_data = lax.axis_size("dp")
    n_group = lax.axis_size("expert")
    peer = img_dev // n_data
    my_place = lax.axis_index("expert")

    route_cols = jnp.concatenate([route_ids, route_wts // 256, route_wts % 256], axis=1)
    route_cols = jnp.pad(route_cols, ((0, 0), (0, 128 - route_cols.shape[1])))

    dest_index = tile_pos // tok_dev // n_group
    order = jnp.argsort(dest_index, stable=True)
    offs_sorted = (tile_pos[order] % tok_dev).astype(bf16)
    pad = 128
    packed = jnp.concatenate(
        [image_feats[order], jnp.broadcast_to(offs_sorted[:, None], (img_dev, pad))], axis=1
    ).reshape(n_data, peer, width_vis + pad)
    moved = dp_all_to_all(packed, 0)
    moved = moved.reshape(img_dev, width_vis + pad)
    moved_feats = moved[:, :width_vis]
    moved_offs = moved[:, width_vis].astype(jnp.int32)

    projected = fused_projector(moved_feats, proj_in, proj_out, 5)

    place = (
        moved_offs[None, :] == jnp.arange(tok_dev, dtype=jnp.int32)[:, None]
    ).astype(bf16)
    placed = select_dot(place, projected)
    has_image = jnp.sum(place.astype(f32), axis=1, keepdims=True) > 0
    embed_own = jnp.where(has_image, placed, text_embed.astype(f32))
    normed_own = normalize(embed_own, norm_gain)

    gathered = expert_all_gather(
        jnp.concatenate([normed_own, route_cols.astype(bf16)], axis=1), 6
    ).reshape(n_group * tok_dev, width_model + route_cols.shape[1])
    normed = gathered[:, :width_model]
    routes = gathered[:, width_model:].astype(f32)
    top_count = route_ids.shape[1]
    ids = routes[:, :top_count].astype(jnp.int32)
    weights_f = routes[:, top_count : 2 * top_count] * 256.0 + routes[:, 2 * top_count : 3 * top_count]

    gate_s = jnp.dot(normed, shared_gate, preferred_element_type=f32)
    up_s = jnp.dot(normed, shared_up, preferred_element_type=f32)
    shared_hidden = (jax.nn.silu(gate_s) * up_s).astype(bf16)

    group_rows = normed.shape[0]
    n_pairs = group_rows * top_count
    capacity = 3 * group_rows * top_count // (2 * n_data)
    share = capacity // n_group
    flat_ids = ids.reshape(-1)
    onehot = (flat_ids[:, None] == jnp.arange(n_data, dtype=jnp.int32)[None, :]).astype(bf16)
    pair_iota = jnp.arange(n_pairs, dtype=jnp.int32)
    earlier = (pair_iota[None, :] < pair_iota[:, None]).astype(bf16)
    counts = select_dot(earlier, onehot)
    rank = jnp.sum(counts * onehot.astype(f32), axis=1).astype(jnp.int32)

    inside = rank // share == my_place
    row_of = jnp.where(inside, flat_ids * share + rank - my_place * share, -1)
    n_rows = n_data * share
    hit = (
        row_of.reshape(group_rows, top_count)[:, :, None]
        == jnp.arange(n_rows, dtype=jnp.int32)[None, None, :]
    )
    pick = jnp.sum(hit.astype(f32), axis=1).astype(bf16)
    lanes = 128
    block = (n_data, share * width_model // lanes, lanes)
    send = select_dot(pick.T, normed).astype(bf16).reshape(block)
    arrived = lax.all_to_all(send, "dp", split_axis=0, concat_axis=0, tiled=True)
    slots = lax.all_gather(arrived.reshape(n_rows, width_model), "expert", axis=0, tiled=True)

    width_e = expert_gate.shape[2]
    gate_up = jnp.dot(
        slots, jnp.concatenate([expert_gate[0], expert_up[0]], axis=1), preferred_element_type=f32
    )
    gate_e, up_e = gate_up[:, :width_e], gate_up[:, width_e:]
    hidden_e = (jax.nn.silu(gate_e) * up_e).astype(bf16)
    partial_out = jnp.dot(hidden_e, expert_down[0], preferred_element_type=f32).astype(bf16)
    summed = lax.psum_scatter(partial_out, "expert", scatter_dimension=0, tiled=True)
    returned = lax.all_to_all(
        summed.reshape(block), "dp", split_axis=0, concat_axis=0, tiled=True
    ).reshape(n_rows, width_model)

    weights_n = weights_f / jnp.sum(weights_f, axis=1, keepdims=True)
    coef = jnp.sum(jnp.where(hit, weights_n[:, :, None], 0.0), axis=1)
    coef_hi = coef.astype(bf16)
    coef_lo = (coef - coef_hi.astype(f32)).astype(bf16)
    terms = jnp.dot(
        jnp.concatenate([shared_hidden, coef_hi, coef_lo], axis=1),
        jnp.concatenate([shared_down, returned, returned], axis=0),
        preferred_element_type=f32,
    )
    total = expert_reduce_scatter(
        terms.astype(bf16)
        .reshape(n_group, tok_dev, width_model),
        4,
        f32,
    )
    return (embed_own + total).astype(bf16)


def solution(mesh):
    return jax.shard_map(
        shards,
        mesh=mesh,
        in_specs=(
            P(("dp", "expert"), None),
            P(("dp", "expert"), None),
            P(("dp", "expert")),
            P(None, "expert"),
            P("expert", None),
            P(),
            P(None, "expert"),
            P(None, "expert"),
            P("expert", None),
            P("dp", None, "expert"),
            P("dp", None, "expert"),
            P("dp", "expert", None),
            P(("dp", "expert"), None),
            P(("dp", "expert"), None),
        ),
        out_specs=P(("dp", "expert"), None),
        check_vma=False,
    )
```

```python
import jax
import jax.numpy as jnp
from jax import lax
from jax.experimental import pallas as pl
from jax.experimental.pallas import tpu as pltpu
from jax.sharding import PartitionSpec as P


def dp_all_to_all(x, collective_id):
    n = x.shape[0]
    mesh_ids = pl.DeviceIdType.MESH

    def kernel(x_ref, y_ref, send_sem, recv_sem, local_sem):
        me = lax.axis_index("dp")
        j = lax.axis_index("expert")
        barrier = pltpu.get_barrier_semaphore()
        for k in range(1, n):
            pl.semaphore_signal(
                barrier, inc=1, device_id=(lax.rem(me + k, n), j), device_id_type=mesh_ids
            )
        pl.semaphore_wait(barrier, n - 1)
        local = pltpu.make_async_copy(x_ref.at[me], y_ref.at[me], local_sem)
        local.start()
        copies = []
        for k in range(1, n):
            peer = lax.rem(me + k, n)
            copy = pltpu.make_async_remote_copy(
                src_ref=x_ref.at[peer],
                dst_ref=y_ref.at[me],
                send_sem=send_sem.at[k],
                recv_sem=recv_sem.at[k],
                device_id=(peer, j),
                device_id_type=mesh_ids,
            )
            copy.start()
            copies.append(copy)
        local.wait()
        for copy in copies:
            copy.wait()

    return pl.pallas_call(
        kernel,
        out_shape=jax.ShapeDtypeStruct(x.shape, x.dtype),
        in_specs=[pl.BlockSpec(memory_space=pl.ANY)],
        out_specs=pl.BlockSpec(memory_space=pl.ANY),
        scratch_shapes=[
            pltpu.SemaphoreType.DMA((n,)),
            pltpu.SemaphoreType.DMA((n,)),
            pltpu.SemaphoreType.DMA,
        ],
        compiler_params=pltpu.CompilerParams(collective_id=collective_id, has_side_effects=True),
    )(x)


def expert_reduce_scatter(x, collective_id, out_dtype, base):
    n, rows, cols = x.shape
    chips = n // 2
    mesh_ids = pl.DeviceIdType.MESH

    def kernel(x_ref, b_ref, o_ref, pair_buf, part, far_buf, send1, recv1, send2, recv2):
        me = lax.axis_index("expert")
        row = lax.axis_index("dp")
        chip, core = me // 2, me % 2
        sibling = chip * 2 + 1 - core
        barrier = pltpu.get_barrier_semaphore()
        pl.semaphore_signal(barrier, inc=1, device_id=(row, sibling), device_id_type=mesh_ids)
        for k in range(1, chips):
            pl.semaphore_signal(
                barrier,
                inc=1,
                device_id=(row, lax.rem(chip + k, chips) * 2 + core),
                device_id_type=mesh_ids,
            )
        pl.semaphore_wait(barrier, chips)
        first = pltpu.make_async_remote_copy(
            src_ref=x_ref.at[:, 1 - core],
            dst_ref=pair_buf,
            send_sem=send1,
            recv_sem=recv1,
            device_id=(row, sibling),
            device_id_type=mesh_ids,
        )
        first.start()
        first.wait()
        copies = []
        for k in range(1, chips):
            dest = lax.rem(chip + k, chips)
            part[k] = (
                x_ref[dest, core].astype(jnp.float32) + pair_buf[dest].astype(jnp.float32)
            ).astype(part.dtype)
            copy = pltpu.make_async_remote_copy(
                src_ref=part.at[k],
                dst_ref=far_buf.at[k],
                send_sem=send2.at[k],
                recv_sem=recv2.at[k],
                device_id=(row, dest * 2 + core),
                device_id_type=mesh_ids,
            )
            copy.start()
            copies.append(copy)
        acc = x_ref[chip, core].astype(jnp.float32) + pair_buf[chip].astype(jnp.float32)
        acc = acc + b_ref[...].astype(jnp.float32)
        for k, copy in enumerate(copies, 1):
            copy.wait()
            acc = acc + far_buf[k].astype(jnp.float32)
        o_ref[...] = acc.astype(o_ref.dtype)

    return pl.pallas_call(
        kernel,
        out_shape=jax.ShapeDtypeStruct((rows, cols), out_dtype),
        in_specs=[pl.BlockSpec(memory_space=pltpu.VMEM)] * 2,
        out_specs=pl.BlockSpec(memory_space=pltpu.VMEM),
        scratch_shapes=[
            pltpu.VMEM((chips, rows, cols), x.dtype),
            pltpu.VMEM((chips, rows, cols), x.dtype),
            pltpu.VMEM((chips, rows, cols), x.dtype),
            pltpu.SemaphoreType.DMA,
            pltpu.SemaphoreType.DMA,
            pltpu.SemaphoreType.DMA((chips,)),
            pltpu.SemaphoreType.DMA((chips,)),
        ],
        compiler_params=pltpu.CompilerParams(collective_id=collective_id, has_side_effects=True),
    )(x.reshape(chips, 2, rows, cols), base)


def expert_all_gather(x, collective_id):
    rows, cols = x.shape
    n = lax.axis_size("expert")
    chips = n // 2
    mesh_ids = pl.DeviceIdType.MESH

    def kernel(x_ref, o_ref, send0, recv0, send1, recv1, send2, recv2):
        me = lax.axis_index("expert")
        row = lax.axis_index("dp")
        chip, core = me // 2, me % 2
        sibling = chip * 2 + 1 - core
        barrier = pltpu.get_barrier_semaphore()
        pl.semaphore_signal(barrier, inc=1, device_id=(row, sibling), device_id_type=mesh_ids)
        for k in range(1, chips):
            pl.semaphore_signal(
                barrier,
                inc=1,
                device_id=(row, lax.rem(chip + k, chips) * 2 + core),
                device_id_type=mesh_ids,
            )
        pl.semaphore_wait(barrier, chips)
        near = pltpu.make_async_remote_copy(
            src_ref=x_ref,
            dst_ref=o_ref.at[me],
            send_sem=send0,
            recv_sem=recv0,
            device_id=(row, sibling),
            device_id_type=mesh_ids,
        )
        near.start()
        far = []
        for k in range(1, chips):
            copy = pltpu.make_async_remote_copy(
                src_ref=x_ref,
                dst_ref=o_ref.at[me],
                send_sem=send1.at[k],
                recv_sem=recv1.at[k],
                device_id=(row, lax.rem(chip + k, chips) * 2 + core),
                device_id_type=mesh_ids,
            )
            copy.start()
            far.append(copy)
        o_ref[me] = x_ref[...]
        passed = []
        for k, copy in enumerate(far, 1):
            copy.wait_recv()
            source = lax.rem(chip - k + chips, chips) * 2 + core
            relay = pltpu.make_async_remote_copy(
                src_ref=o_ref.at[source],
                dst_ref=o_ref.at[source],
                send_sem=send2.at[k],
                recv_sem=recv2.at[k],
                device_id=(row, sibling),
                device_id_type=mesh_ids,
            )
            relay.start()
            passed.append(relay)
        near.wait()
        for copy in far:
            copy.wait_send()
        for relay in passed:
            relay.wait()

    return pl.pallas_call(
        kernel,
        out_shape=jax.ShapeDtypeStruct((n, rows, cols), x.dtype),
        in_specs=[pl.BlockSpec(memory_space=pltpu.VMEM)],
        out_specs=pl.BlockSpec(memory_space=pltpu.VMEM),
        scratch_shapes=[
            pltpu.SemaphoreType.DMA,
            pltpu.SemaphoreType.DMA,
            pltpu.SemaphoreType.DMA((chips,)),
            pltpu.SemaphoreType.DMA((chips,)),
            pltpu.SemaphoreType.DMA((chips,)),
            pltpu.SemaphoreType.DMA((chips,)),
        ],
        compiler_params=pltpu.CompilerParams(collective_id=collective_id, has_side_effects=True),
    )(x)


def fused_projector(feats, proj_in, proj_out, collective_id):
    rows, width_vis = feats.shape
    n = lax.axis_size("expert")
    width_model = proj_out.shape[1]
    mesh_ids = pl.DeviceIdType.MESH
    f32, bf16 = jnp.float32, jnp.bfloat16

    def kernel(f_ref, wi_ref, wo_ref, o_ref, fbuf, psend, pbuf, send_f, recv_f, send_p, recv_p):
        me = lax.axis_index("expert")
        row = lax.axis_index("dp")
        barrier = pltpu.get_barrier_semaphore()
        for k in range(1, n):
            pl.semaphore_signal(
                barrier, inc=1, device_id=(row, lax.rem(me + k, n)), device_id_type=mesh_ids
            )
        pl.semaphore_wait(barrier, n - 1)
        feat_copies = []
        for k in range(1, n):
            copy = pltpu.make_async_remote_copy(
                src_ref=f_ref,
                dst_ref=fbuf.at[me],
                send_sem=send_f.at[k],
                recv_sem=recv_f.at[k],
                device_id=(row, lax.rem(me + k, n)),
                device_id_type=mesh_ids,
            )
            copy.start()
            feat_copies.append(copy)

        def partial(x):
            hidden = jnp.dot(x, wi_ref[...], preferred_element_type=f32)
            hidden = jax.nn.gelu(hidden, approximate=True).astype(bf16)
            return jnp.dot(hidden, wo_ref[...], preferred_element_type=f32)

        acc = partial(f_ref[...])
        part_copies = []
        for k, copy in enumerate(feat_copies, 1):
            copy.wait_recv()
            source = lax.rem(me - k + n, n)
            psend[k] = partial(fbuf[source]).astype(bf16)
            back = pltpu.make_async_remote_copy(
                src_ref=psend.at[k],
                dst_ref=pbuf.at[k],
                send_sem=send_p.at[k],
                recv_sem=recv_p.at[k],
                device_id=(row, source),
                device_id_type=mesh_ids,
            )
            back.start()
            part_copies.append(back)
        for k, back in enumerate(part_copies, 1):
            back.wait_recv()
            acc = acc + pbuf[k].astype(f32)
        o_ref[...] = acc.astype(o_ref.dtype)
        for copy in feat_copies:
            copy.wait_send()
        for back in part_copies:
            back.wait_send()

    return pl.pallas_call(
        kernel,
        out_shape=jax.ShapeDtypeStruct((rows, width_model), bf16),
        in_specs=[pl.BlockSpec(memory_space=pltpu.VMEM)] * 3,
        out_specs=pl.BlockSpec(memory_space=pltpu.VMEM),
        scratch_shapes=[
            pltpu.VMEM((n, rows, width_vis), feats.dtype),
            pltpu.VMEM((n, rows, width_model), bf16),
            pltpu.VMEM((n, rows, width_model), bf16),
            pltpu.SemaphoreType.DMA((n,)),
            pltpu.SemaphoreType.DMA((n,)),
            pltpu.SemaphoreType.DMA((n,)),
            pltpu.SemaphoreType.DMA((n,)),
        ],
        compiler_params=pltpu.CompilerParams(
            collective_id=collective_id, has_side_effects=True, vmem_limit_bytes=48 * 1024 * 1024
        ),
    )(feats, proj_in, proj_out)


def normalize(rows, norm_gain):
    rows_f = rows.astype(jnp.float32)
    meansq = jnp.mean(rows_f * rows_f, axis=-1, keepdims=True) + 1e-06
    return (rows_f * lax.rsqrt(meansq) * norm_gain).astype(jnp.bfloat16)


def select_dot(sel, rows):
    return jnp.dot(sel, rows, preferred_element_type=jnp.float32)


def shards(
    text_embed,
    image_feats,
    tile_pos,
    proj_in,
    proj_out,
    norm_gain,
    shared_gate,
    shared_up,
    shared_down,
    expert_gate,
    expert_up,
    expert_down,
    route_ids,
    route_wts,
):
    bf16, f32 = jnp.bfloat16, jnp.float32
    tok_dev, width_model = text_embed.shape
    img_dev, width_vis = image_feats.shape
    n_data = lax.axis_size("dp")
    n_group = lax.axis_size("expert")
    peer = img_dev // n_data
    my_place = lax.axis_index("expert")

    route_cols = jnp.concatenate([route_ids, route_wts // 256, route_wts % 256], axis=1)
    route_cols = jnp.pad(route_cols, ((0, 0), (0, 128 - route_cols.shape[1])))

    dest_index = tile_pos // tok_dev // n_group
    order = jnp.argsort(dest_index, stable=True)
    offs_sorted = (tile_pos[order] % tok_dev).astype(bf16)
    pad = 128
    packed = jnp.concatenate(
        [image_feats[order], jnp.broadcast_to(offs_sorted[:, None], (img_dev, pad))], axis=1
    ).reshape(n_data, peer, width_vis + pad)
    moved = dp_all_to_all(packed, 0)
    moved = moved.reshape(img_dev, width_vis + pad)
    moved_feats = moved[:, :width_vis]
    moved_offs = moved[:, width_vis].astype(jnp.int32)

    projected = fused_projector(moved_feats, proj_in, proj_out, 5)

    place = (
        moved_offs[None, :] == jnp.arange(tok_dev, dtype=jnp.int32)[:, None]
    ).astype(bf16)
    placed = select_dot(place, projected)
    has_image = jnp.sum(place.astype(f32), axis=1, keepdims=True) > 0
    embed_own = jnp.where(has_image, placed, text_embed.astype(f32))
    normed_own = normalize(embed_own, norm_gain)

    gathered = expert_all_gather(
        jnp.concatenate([normed_own, route_cols.astype(bf16)], axis=1), 6
    ).reshape(n_group * tok_dev, width_model + route_cols.shape[1])
    normed = gathered[:, :width_model]
    routes = gathered[:, width_model:].astype(f32)
    top_count = route_ids.shape[1]
    ids = routes[:, :top_count].astype(jnp.int32)
    weights_f = routes[:, top_count : 2 * top_count] * 256.0 + routes[:, 2 * top_count : 3 * top_count]

    gate_s = jnp.dot(normed, shared_gate, preferred_element_type=f32)
    up_s = jnp.dot(normed, shared_up, preferred_element_type=f32)
    shared_hidden = (jax.nn.silu(gate_s) * up_s).astype(bf16)

    group_rows = normed.shape[0]
    n_pairs = group_rows * top_count
    capacity = 3 * group_rows * top_count // (2 * n_data)
    share = capacity // n_group
    flat_ids = ids.reshape(-1)
    onehot = (flat_ids[:, None] == jnp.arange(n_data, dtype=jnp.int32)[None, :]).astype(bf16)
    pair_iota = jnp.arange(n_pairs, dtype=jnp.int32)
    earlier = (pair_iota[None, :] < pair_iota[:, None]).astype(bf16)
    counts = select_dot(earlier, onehot)
    rank = jnp.sum(counts * onehot.astype(f32), axis=1).astype(jnp.int32)

    inside = rank // share == my_place
    row_of = jnp.where(inside, flat_ids * share + rank - my_place * share, -1)
    n_rows = n_data * share
    hit = (
        row_of.reshape(group_rows, top_count)[:, :, None]
        == jnp.arange(n_rows, dtype=jnp.int32)[None, None, :]
    )
    pick = jnp.sum(hit.astype(f32), axis=1).astype(bf16)
    lanes = 128
    block = (n_data, share * width_model // lanes, lanes)
    send = select_dot(pick.T, normed).astype(bf16).reshape(block)
    arrived = lax.all_to_all(send, "dp", split_axis=0, concat_axis=0, tiled=True)
    slots = lax.all_gather(arrived.reshape(n_rows, width_model), "expert", axis=0, tiled=True)

    width_e = expert_gate.shape[2]
    gate_up = jnp.dot(
        slots, jnp.concatenate([expert_gate[0], expert_up[0]], axis=1), preferred_element_type=f32
    )
    gate_e, up_e = gate_up[:, :width_e], gate_up[:, width_e:]
    hidden_e = (jax.nn.silu(gate_e) * up_e).astype(bf16)
    partial_out = jnp.dot(hidden_e, expert_down[0], preferred_element_type=f32).astype(bf16)
    summed = lax.psum_scatter(partial_out, "expert", scatter_dimension=0, tiled=True)
    returned = lax.all_to_all(
        summed.reshape(block), "dp", split_axis=0, concat_axis=0, tiled=True
    ).reshape(n_rows, width_model)

    weights_n = weights_f / jnp.sum(weights_f, axis=1, keepdims=True)
    coef = jnp.sum(jnp.where(hit, weights_n[:, :, None], 0.0), axis=1)
    coef_hi = coef.astype(bf16)
    coef_lo = (coef - coef_hi.astype(f32)).astype(bf16)
    terms = jnp.dot(
        jnp.concatenate([shared_hidden, coef_hi, coef_lo], axis=1),
        jnp.concatenate([shared_down, returned, returned], axis=0),
        preferred_element_type=f32,
    )
    return expert_reduce_scatter(
        terms.astype(bf16).reshape(n_group, tok_dev, width_model),
        4,
        bf16,
        embed_own.astype(bf16),
    )


def solution(mesh):
    return jax.shard_map(
        shards,
        mesh=mesh,
        in_specs=(
            P(("dp", "expert"), None),
            P(("dp", "expert"), None),
            P(("dp", "expert")),
            P(None, "expert"),
            P("expert", None),
            P(),
            P(None, "expert"),
            P(None, "expert"),
            P("expert", None),
            P("dp", None, "expert"),
            P("dp", None, "expert"),
            P("dp", "expert", None),
            P(("dp", "expert"), None),
            P(("dp", "expert"), None),
        ),
        out_specs=P(("dp", "expert"), None),
        check_vma=False,
    )
```

```python
import jax
import jax.numpy as jnp
from jax import lax
from jax.experimental import pallas as pl
from jax.experimental.pallas import tpu as pltpu
from jax.sharding import PartitionSpec as P


def dp_all_to_all(x, collective_id):
    n = x.shape[0]
    mesh_ids = pl.DeviceIdType.MESH

    def kernel(x_ref, y_ref, send_sem, recv_sem, local_sem):
        me = lax.axis_index("dp")
        j = lax.axis_index("expert")
        barrier = pltpu.get_barrier_semaphore()
        for k in range(1, n):
            pl.semaphore_signal(
                barrier, inc=1, device_id=(lax.rem(me + k, n), j), device_id_type=mesh_ids
            )
        pl.semaphore_wait(barrier, n - 1)
        local = pltpu.make_async_copy(x_ref.at[me], y_ref.at[me], local_sem)
        local.start()
        copies = []
        for k in range(1, n):
            peer = lax.rem(me + k, n)
            copy = pltpu.make_async_remote_copy(
                src_ref=x_ref.at[peer],
                dst_ref=y_ref.at[me],
                send_sem=send_sem.at[k],
                recv_sem=recv_sem.at[k],
                device_id=(peer, j),
                device_id_type=mesh_ids,
            )
            copy.start()
            copies.append(copy)
        local.wait()
        for copy in copies:
            copy.wait()

    return pl.pallas_call(
        kernel,
        out_shape=jax.ShapeDtypeStruct(x.shape, x.dtype),
        in_specs=[pl.BlockSpec(memory_space=pl.ANY)],
        out_specs=pl.BlockSpec(memory_space=pl.ANY),
        scratch_shapes=[
            pltpu.SemaphoreType.DMA((n,)),
            pltpu.SemaphoreType.DMA((n,)),
            pltpu.SemaphoreType.DMA,
        ],
        compiler_params=pltpu.CompilerParams(collective_id=collective_id, has_side_effects=True),
    )(x)


def expert_reduce_scatter(x, collective_id, out_dtype, base):
    n, rows, cols = x.shape
    chips = n // 2
    mesh_ids = pl.DeviceIdType.MESH

    def kernel(x_ref, b_ref, o_ref, pair_buf, part, far_buf, send1, recv1, send2, recv2):
        me = lax.axis_index("expert")
        row = lax.axis_index("dp")
        chip, core = me // 2, me % 2
        sibling = chip * 2 + 1 - core
        barrier = pltpu.get_barrier_semaphore()
        pl.semaphore_signal(barrier, inc=1, device_id=(row, sibling), device_id_type=mesh_ids)
        for k in range(1, chips):
            pl.semaphore_signal(
                barrier,
                inc=1,
                device_id=(row, lax.rem(chip + k, chips) * 2 + core),
                device_id_type=mesh_ids,
            )
        pl.semaphore_wait(barrier, chips)
        first = pltpu.make_async_remote_copy(
            src_ref=x_ref.at[:, 1 - core],
            dst_ref=pair_buf,
            send_sem=send1,
            recv_sem=recv1,
            device_id=(row, sibling),
            device_id_type=mesh_ids,
        )
        first.start()
        first.wait()
        copies = []
        for k in range(1, chips):
            dest = lax.rem(chip + k, chips)
            part[k] = (
                x_ref[dest, core].astype(jnp.float32) + pair_buf[dest].astype(jnp.float32)
            ).astype(part.dtype)
            copy = pltpu.make_async_remote_copy(
                src_ref=part.at[k],
                dst_ref=far_buf.at[k],
                send_sem=send2.at[k],
                recv_sem=recv2.at[k],
                device_id=(row, dest * 2 + core),
                device_id_type=mesh_ids,
            )
            copy.start()
            copies.append(copy)
        acc = x_ref[chip, core].astype(jnp.float32) + pair_buf[chip].astype(jnp.float32)
        acc = acc + b_ref[...].astype(jnp.float32)
        for k, copy in enumerate(copies, 1):
            copy.wait()
            acc = acc + far_buf[k].astype(jnp.float32)
        o_ref[...] = acc.astype(o_ref.dtype)

    return pl.pallas_call(
        kernel,
        out_shape=jax.ShapeDtypeStruct((rows, cols), out_dtype),
        in_specs=[pl.BlockSpec(memory_space=pltpu.VMEM)] * 2,
        out_specs=pl.BlockSpec(memory_space=pltpu.VMEM),
        scratch_shapes=[
            pltpu.VMEM((chips, rows, cols), x.dtype),
            pltpu.VMEM((chips, rows, cols), x.dtype),
            pltpu.VMEM((chips, rows, cols), x.dtype),
            pltpu.SemaphoreType.DMA,
            pltpu.SemaphoreType.DMA,
            pltpu.SemaphoreType.DMA((chips,)),
            pltpu.SemaphoreType.DMA((chips,)),
        ],
        compiler_params=pltpu.CompilerParams(collective_id=collective_id, has_side_effects=True),
    )(x.reshape(chips, 2, rows, cols), base)


def expert_all_gather(x, collective_id):
    rows, cols = x.shape
    n = lax.axis_size("expert")
    chips = n // 2
    mesh_ids = pl.DeviceIdType.MESH

    def kernel(x_ref, o_ref, send0, recv0, send1, recv1, send2, recv2):
        me = lax.axis_index("expert")
        row = lax.axis_index("dp")
        chip, core = me // 2, me % 2
        sibling = chip * 2 + 1 - core
        barrier = pltpu.get_barrier_semaphore()
        pl.semaphore_signal(barrier, inc=1, device_id=(row, sibling), device_id_type=mesh_ids)
        for k in range(1, chips):
            pl.semaphore_signal(
                barrier,
                inc=1,
                device_id=(row, lax.rem(chip + k, chips) * 2 + core),
                device_id_type=mesh_ids,
            )
        pl.semaphore_wait(barrier, chips)
        near = pltpu.make_async_remote_copy(
            src_ref=x_ref,
            dst_ref=o_ref.at[me],
            send_sem=send0,
            recv_sem=recv0,
            device_id=(row, sibling),
            device_id_type=mesh_ids,
        )
        near.start()
        far = []
        for k in range(1, chips):
            copy = pltpu.make_async_remote_copy(
                src_ref=x_ref,
                dst_ref=o_ref.at[me],
                send_sem=send1.at[k],
                recv_sem=recv1.at[k],
                device_id=(row, lax.rem(chip + k, chips) * 2 + core),
                device_id_type=mesh_ids,
            )
            copy.start()
            far.append(copy)
        o_ref[me] = x_ref[...]
        passed = []
        for k, copy in enumerate(far, 1):
            copy.wait_recv()
            source = lax.rem(chip - k + chips, chips) * 2 + core
            relay = pltpu.make_async_remote_copy(
                src_ref=o_ref.at[source],
                dst_ref=o_ref.at[source],
                send_sem=send2.at[k],
                recv_sem=recv2.at[k],
                device_id=(row, sibling),
                device_id_type=mesh_ids,
            )
            relay.start()
            passed.append(relay)
        near.wait()
        for copy in far:
            copy.wait_send()
        for relay in passed:
            relay.wait()

    return pl.pallas_call(
        kernel,
        out_shape=jax.ShapeDtypeStruct((n, rows, cols), x.dtype),
        in_specs=[pl.BlockSpec(memory_space=pltpu.VMEM)],
        out_specs=pl.BlockSpec(memory_space=pltpu.VMEM),
        scratch_shapes=[
            pltpu.SemaphoreType.DMA,
            pltpu.SemaphoreType.DMA,
            pltpu.SemaphoreType.DMA((chips,)),
            pltpu.SemaphoreType.DMA((chips,)),
            pltpu.SemaphoreType.DMA((chips,)),
            pltpu.SemaphoreType.DMA((chips,)),
        ],
        compiler_params=pltpu.CompilerParams(collective_id=collective_id, has_side_effects=True),
    )(x)


def fused_projector(feats, proj_in, proj_out, collective_id):
    rows, width_vis = feats.shape
    n = lax.axis_size("expert")
    width_model = proj_out.shape[1]
    mesh_ids = pl.DeviceIdType.MESH
    f32, bf16 = jnp.float32, jnp.bfloat16

    def kernel(f_ref, wi_ref, wo_ref, o_ref, fbuf, psend, pbuf, send_f, recv_f, send_p, recv_p):
        me = lax.axis_index("expert")
        row = lax.axis_index("dp")
        barrier = pltpu.get_barrier_semaphore()
        for k in range(1, n):
            pl.semaphore_signal(
                barrier, inc=1, device_id=(row, lax.rem(me + k, n)), device_id_type=mesh_ids
            )
        pl.semaphore_wait(barrier, n - 1)
        feat_copies = []
        for k in range(1, n):
            copy = pltpu.make_async_remote_copy(
                src_ref=f_ref,
                dst_ref=fbuf.at[me],
                send_sem=send_f.at[k],
                recv_sem=recv_f.at[k],
                device_id=(row, lax.rem(me + k, n)),
                device_id_type=mesh_ids,
            )
            copy.start()
            feat_copies.append(copy)

        def partial(x):
            hidden = jnp.dot(x, wi_ref[...], preferred_element_type=f32)
            hidden = jax.nn.gelu(hidden, approximate=True).astype(bf16)
            return jnp.dot(hidden, wo_ref[...], preferred_element_type=f32)

        acc = partial(f_ref[...])
        part_copies = []
        for k, copy in enumerate(feat_copies, 1):
            copy.wait_recv()
            source = lax.rem(me - k + n, n)
            psend[k] = partial(fbuf[source]).astype(bf16)
            back = pltpu.make_async_remote_copy(
                src_ref=psend.at[k],
                dst_ref=pbuf.at[k],
                send_sem=send_p.at[k],
                recv_sem=recv_p.at[k],
                device_id=(row, source),
                device_id_type=mesh_ids,
            )
            back.start()
            part_copies.append(back)
        for k, back in enumerate(part_copies, 1):
            back.wait_recv()
            acc = acc + pbuf[k].astype(f32)
        o_ref[...] = acc.astype(o_ref.dtype)
        for copy in feat_copies:
            copy.wait_send()
        for back in part_copies:
            back.wait_send()

    return pl.pallas_call(
        kernel,
        out_shape=jax.ShapeDtypeStruct((rows, width_model), bf16),
        in_specs=[pl.BlockSpec(memory_space=pltpu.VMEM)] * 3,
        out_specs=pl.BlockSpec(memory_space=pltpu.VMEM),
        scratch_shapes=[
            pltpu.VMEM((n, rows, width_vis), feats.dtype),
            pltpu.VMEM((n, rows, width_model), bf16),
            pltpu.VMEM((n, rows, width_model), bf16),
            pltpu.SemaphoreType.DMA((n,)),
            pltpu.SemaphoreType.DMA((n,)),
            pltpu.SemaphoreType.DMA((n,)),
            pltpu.SemaphoreType.DMA((n,)),
        ],
        compiler_params=pltpu.CompilerParams(
            collective_id=collective_id, has_side_effects=True, vmem_limit_bytes=48 * 1024 * 1024
        ),
    )(feats, proj_in, proj_out)


def normalize(rows, norm_gain):
    rows_f = rows.astype(jnp.float32)
    meansq = jnp.mean(rows_f * rows_f, axis=-1, keepdims=True) + 1e-06
    return (rows_f * lax.rsqrt(meansq) * norm_gain).astype(jnp.bfloat16)


def select_dot(sel, rows):
    return jnp.dot(sel, rows, preferred_element_type=jnp.float32)


def shards(
    text_embed,
    image_feats,
    tile_pos,
    proj_in,
    proj_out,
    norm_gain,
    shared_gate,
    shared_up,
    shared_down,
    expert_gate,
    expert_up,
    expert_down,
    route_ids,
    route_wts,
):
    bf16, f32 = jnp.bfloat16, jnp.float32
    tok_dev, width_model = text_embed.shape
    img_dev, width_vis = image_feats.shape
    n_data = lax.axis_size("dp")
    n_group = lax.axis_size("expert")
    peer = img_dev // n_data
    my_place = lax.axis_index("expert")

    route_cols = jnp.concatenate([route_ids, route_wts // 256, route_wts % 256], axis=1)
    route_cols = jnp.pad(route_cols, ((0, 0), (0, 128 - route_cols.shape[1])))

    dest_index = tile_pos // tok_dev // n_group
    order = jnp.argsort(dest_index, stable=True)
    offs_sorted = (tile_pos[order] % tok_dev).astype(bf16)
    pad = 128
    packed = jnp.concatenate(
        [image_feats[order], jnp.broadcast_to(offs_sorted[:, None], (img_dev, pad))], axis=1
    ).reshape(n_data, peer, width_vis + pad)
    moved = lax.all_to_all(packed, "dp", split_axis=0, concat_axis=0, tiled=True)
    moved = moved.reshape(img_dev, width_vis + pad)
    moved_feats = moved[:, :width_vis]
    moved_offs = moved[:, width_vis].astype(jnp.int32)

    projected = fused_projector(moved_feats, proj_in, proj_out, 5)

    place = (
        moved_offs[None, :] == jnp.arange(tok_dev, dtype=jnp.int32)[:, None]
    ).astype(bf16)
    placed = select_dot(place, projected)
    has_image = jnp.sum(place.astype(f32), axis=1, keepdims=True) > 0
    embed_own = jnp.where(has_image, placed, text_embed.astype(f32))
    normed_own = normalize(embed_own, norm_gain)

    gathered = expert_all_gather(
        jnp.concatenate([normed_own, route_cols.astype(bf16)], axis=1), 6
    ).reshape(n_group * tok_dev, width_model + route_cols.shape[1])
    normed = gathered[:, :width_model]
    routes = gathered[:, width_model:].astype(f32)
    top_count = route_ids.shape[1]
    ids = routes[:, :top_count].astype(jnp.int32)
    weights_f = routes[:, top_count : 2 * top_count] * 256.0 + routes[:, 2 * top_count : 3 * top_count]

    gate_s = jnp.dot(normed, shared_gate, preferred_element_type=f32)
    up_s = jnp.dot(normed, shared_up, preferred_element_type=f32)
    shared_hidden = (jax.nn.silu(gate_s) * up_s).astype(bf16)

    group_rows = normed.shape[0]
    n_pairs = group_rows * top_count
    capacity = 3 * group_rows * top_count // (2 * n_data)
    share = capacity // n_group
    flat_ids = ids.reshape(-1)
    onehot = (flat_ids[:, None] == jnp.arange(n_data, dtype=jnp.int32)[None, :]).astype(bf16)
    pair_iota = jnp.arange(n_pairs, dtype=jnp.int32)
    earlier = (pair_iota[None, :] < pair_iota[:, None]).astype(bf16)
    counts = select_dot(earlier, onehot)
    rank = jnp.sum(counts * onehot.astype(f32), axis=1).astype(jnp.int32)

    inside = rank // share == my_place
    row_of = jnp.where(inside, flat_ids * share + rank - my_place * share, -1)
    n_rows = n_data * share
    hit = (
        row_of.reshape(group_rows, top_count)[:, :, None]
        == jnp.arange(n_rows, dtype=jnp.int32)[None, None, :]
    )
    pick = jnp.sum(hit.astype(f32), axis=1).astype(bf16)
    lanes = 128
    block = (n_data, share * width_model // lanes, lanes)
    send = select_dot(pick.T, normed).astype(bf16).reshape(block)
    arrived = lax.all_to_all(send, "dp", split_axis=0, concat_axis=0, tiled=True)
    slots = lax.all_gather(arrived.reshape(n_rows, width_model), "expert", axis=0, tiled=True)

    width_e = expert_gate.shape[2]
    gate_up = jnp.dot(
        slots, jnp.concatenate([expert_gate[0], expert_up[0]], axis=1), preferred_element_type=f32
    )
    gate_e, up_e = gate_up[:, :width_e], gate_up[:, width_e:]
    hidden_e = (jax.nn.silu(gate_e) * up_e).astype(bf16)
    partial_out = jnp.dot(hidden_e, expert_down[0], preferred_element_type=f32).astype(bf16)
    summed = lax.psum_scatter(partial_out, "expert", scatter_dimension=0, tiled=True)
    returned = lax.all_to_all(
        summed.reshape(block), "dp", split_axis=0, concat_axis=0, tiled=True
    ).reshape(n_rows, width_model)

    weights_n = weights_f / jnp.sum(weights_f, axis=1, keepdims=True)
    coef = jnp.sum(jnp.where(hit, weights_n[:, :, None], 0.0), axis=1)
    coef_hi = coef.astype(bf16)
    coef_lo = (coef - coef_hi.astype(f32)).astype(bf16)
    terms = jnp.dot(
        jnp.concatenate([shared_hidden, coef_hi, coef_lo], axis=1),
        jnp.concatenate([shared_down, returned, returned], axis=0),
        preferred_element_type=f32,
    )
    return expert_reduce_scatter(
        terms.astype(bf16).reshape(n_group, tok_dev, width_model),
        4,
        bf16,
        embed_own.astype(bf16),
    )


def solution(mesh):
    return jax.shard_map(
        shards,
        mesh=mesh,
        in_specs=(
            P(("dp", "expert"), None),
            P(("dp", "expert"), None),
            P(("dp", "expert")),
            P(None, "expert"),
            P("expert", None),
            P(),
            P(None, "expert"),
            P(None, "expert"),
            P("expert", None),
            P("dp", None, "expert"),
            P("dp", None, "expert"),
            P("dp", "expert", None),
            P(("dp", "expert"), None),
            P(("dp", "expert"), None),
        ),
        out_specs=P(("dp", "expert"), None),
        check_vma=False,
    )
```

```python
import jax
import jax.numpy as jnp
from jax import lax
from jax.experimental import pallas as pl
from jax.experimental.pallas import tpu as pltpu
from jax.sharding import PartitionSpec as P


def dp_all_to_all(x, collective_id):
    n = x.shape[0]
    mesh_ids = pl.DeviceIdType.MESH

    def kernel(x_ref, y_ref, send_sem, recv_sem, local_sem):
        me = lax.axis_index("dp")
        j = lax.axis_index("expert")
        barrier = pltpu.get_barrier_semaphore()
        for k in range(1, n):
            pl.semaphore_signal(
                barrier, inc=1, device_id=(lax.rem(me + k, n), j), device_id_type=mesh_ids
            )
        pl.semaphore_wait(barrier, n - 1)
        local = pltpu.make_async_copy(x_ref.at[me], y_ref.at[me], local_sem)
        local.start()
        copies = []
        for k in range(1, n):
            peer = lax.rem(me + k, n)
            copy = pltpu.make_async_remote_copy(
                src_ref=x_ref.at[peer],
                dst_ref=y_ref.at[me],
                send_sem=send_sem.at[k],
                recv_sem=recv_sem.at[k],
                device_id=(peer, j),
                device_id_type=mesh_ids,
            )
            copy.start()
            copies.append(copy)
        local.wait()
        for copy in copies:
            copy.wait()

    return pl.pallas_call(
        kernel,
        out_shape=jax.ShapeDtypeStruct(x.shape, x.dtype),
        in_specs=[pl.BlockSpec(memory_space=pl.ANY)],
        out_specs=pl.BlockSpec(memory_space=pl.ANY),
        scratch_shapes=[
            pltpu.SemaphoreType.DMA((n,)),
            pltpu.SemaphoreType.DMA((n,)),
            pltpu.SemaphoreType.DMA,
        ],
        compiler_params=pltpu.CompilerParams(collective_id=collective_id, has_side_effects=True),
    )(x)


def expert_reduce_scatter(x, collective_id, out_dtype, base):
    n, rows, cols = x.shape
    chips = n // 2
    mesh_ids = pl.DeviceIdType.MESH

    def kernel(x_ref, b_ref, o_ref, pair_buf, part, far_buf, send1, recv1, send2, recv2):
        me = lax.axis_index("expert")
        row = lax.axis_index("dp")
        chip, core = me // 2, me % 2
        sibling = chip * 2 + 1 - core
        barrier = pltpu.get_barrier_semaphore()
        pl.semaphore_signal(barrier, inc=1, device_id=(row, sibling), device_id_type=mesh_ids)
        for k in range(1, chips):
            pl.semaphore_signal(
                barrier,
                inc=1,
                device_id=(row, lax.rem(chip + k, chips) * 2 + core),
                device_id_type=mesh_ids,
            )
        pl.semaphore_wait(barrier, chips)
        first = pltpu.make_async_remote_copy(
            src_ref=x_ref.at[:, 1 - core],
            dst_ref=pair_buf,
            send_sem=send1,
            recv_sem=recv1,
            device_id=(row, sibling),
            device_id_type=mesh_ids,
        )
        first.start()
        first.wait()
        copies = []
        for k in range(1, chips):
            dest = lax.rem(chip + k, chips)
            part[k] = (
                x_ref[dest, core].astype(jnp.float32) + pair_buf[dest].astype(jnp.float32)
            ).astype(part.dtype)
            copy = pltpu.make_async_remote_copy(
                src_ref=part.at[k],
                dst_ref=far_buf.at[k],
                send_sem=send2.at[k],
                recv_sem=recv2.at[k],
                device_id=(row, dest * 2 + core),
                device_id_type=mesh_ids,
            )
            copy.start()
            copies.append(copy)
        acc = x_ref[chip, core].astype(jnp.float32) + pair_buf[chip].astype(jnp.float32)
        acc = acc + b_ref[...].astype(jnp.float32)
        for k, copy in enumerate(copies, 1):
            copy.wait()
            acc = acc + far_buf[k].astype(jnp.float32)
        o_ref[...] = acc.astype(o_ref.dtype)

    return pl.pallas_call(
        kernel,
        out_shape=jax.ShapeDtypeStruct((rows, cols), out_dtype),
        in_specs=[pl.BlockSpec(memory_space=pltpu.VMEM)] * 2,
        out_specs=pl.BlockSpec(memory_space=pltpu.VMEM),
        scratch_shapes=[
            pltpu.VMEM((chips, rows, cols), x.dtype),
            pltpu.VMEM((chips, rows, cols), x.dtype),
            pltpu.VMEM((chips, rows, cols), x.dtype),
            pltpu.SemaphoreType.DMA,
            pltpu.SemaphoreType.DMA,
            pltpu.SemaphoreType.DMA((chips,)),
            pltpu.SemaphoreType.DMA((chips,)),
        ],
        compiler_params=pltpu.CompilerParams(collective_id=collective_id, has_side_effects=True),
    )(x.reshape(chips, 2, rows, cols), base)


def expert_all_gather(x, collective_id):
    rows, cols = x.shape
    n = lax.axis_size("expert")
    chips = n // 2
    mesh_ids = pl.DeviceIdType.MESH

    def kernel(x_ref, o_ref, send0, recv0, send1, recv1, send2, recv2):
        me = lax.axis_index("expert")
        row = lax.axis_index("dp")
        chip, core = me // 2, me % 2
        sibling = chip * 2 + 1 - core
        barrier = pltpu.get_barrier_semaphore()
        pl.semaphore_signal(barrier, inc=1, device_id=(row, sibling), device_id_type=mesh_ids)
        for k in range(1, chips):
            pl.semaphore_signal(
                barrier,
                inc=1,
                device_id=(row, lax.rem(chip + k, chips) * 2 + core),
                device_id_type=mesh_ids,
            )
        pl.semaphore_wait(barrier, chips)
        near = pltpu.make_async_remote_copy(
            src_ref=x_ref,
            dst_ref=o_ref.at[me],
            send_sem=send0,
            recv_sem=recv0,
            device_id=(row, sibling),
            device_id_type=mesh_ids,
        )
        near.start()
        far = []
        for k in range(1, chips):
            copy = pltpu.make_async_remote_copy(
                src_ref=x_ref,
                dst_ref=o_ref.at[me],
                send_sem=send1.at[k],
                recv_sem=recv1.at[k],
                device_id=(row, lax.rem(chip + k, chips) * 2 + core),
                device_id_type=mesh_ids,
            )
            copy.start()
            far.append(copy)
        o_ref[me] = x_ref[...]
        passed = []
        for k, copy in enumerate(far, 1):
            copy.wait_recv()
            source = lax.rem(chip - k + chips, chips) * 2 + core
            relay = pltpu.make_async_remote_copy(
                src_ref=o_ref.at[source],
                dst_ref=o_ref.at[source],
                send_sem=send2.at[k],
                recv_sem=recv2.at[k],
                device_id=(row, sibling),
                device_id_type=mesh_ids,
            )
            relay.start()
            passed.append(relay)
        near.wait()
        for copy in far:
            copy.wait_send()
        for relay in passed:
            relay.wait()

    return pl.pallas_call(
        kernel,
        out_shape=jax.ShapeDtypeStruct((n, rows, cols), x.dtype),
        in_specs=[pl.BlockSpec(memory_space=pltpu.VMEM)],
        out_specs=pl.BlockSpec(memory_space=pltpu.VMEM),
        scratch_shapes=[
            pltpu.SemaphoreType.DMA,
            pltpu.SemaphoreType.DMA,
            pltpu.SemaphoreType.DMA((chips,)),
            pltpu.SemaphoreType.DMA((chips,)),
            pltpu.SemaphoreType.DMA((chips,)),
            pltpu.SemaphoreType.DMA((chips,)),
        ],
        compiler_params=pltpu.CompilerParams(collective_id=collective_id, has_side_effects=True),
    )(x)


def fused_projector(feats, proj_in, proj_out, collective_id):
    rows, width_vis = feats.shape
    n = lax.axis_size("expert")
    chips = n // 2
    width_model = proj_out.shape[1]
    mesh_ids = pl.DeviceIdType.MESH
    f32, bf16 = jnp.float32, jnp.bfloat16

    def kernel(
        f_ref, wi_ref, wo_ref, o_ref, fbuf, psend, pbuf,
        send_n, recv_n, send_f, recv_f, send_r, recv_r, send_p, recv_p,
    ):
        me = lax.axis_index("expert")
        row = lax.axis_index("dp")
        chip, core = me // 2, me % 2
        sibling = chip * 2 + 1 - core
        barrier = pltpu.get_barrier_semaphore()
        for k in range(1, n):
            pl.semaphore_signal(
                barrier, inc=1, device_id=(row, lax.rem(me + k, n)), device_id_type=mesh_ids
            )
        pl.semaphore_wait(barrier, n - 1)
        near = pltpu.make_async_remote_copy(
            src_ref=f_ref,
            dst_ref=fbuf.at[me],
            send_sem=send_n,
            recv_sem=recv_n,
            device_id=(row, sibling),
            device_id_type=mesh_ids,
        )
        near.start()
        far = []
        for k in range(1, chips):
            copy = pltpu.make_async_remote_copy(
                src_ref=f_ref,
                dst_ref=fbuf.at[me],
                send_sem=send_f.at[k],
                recv_sem=recv_f.at[k],
                device_id=(row, lax.rem(chip + k, chips) * 2 + core),
                device_id_type=mesh_ids,
            )
            copy.start()
            far.append(copy)

        def partial(x):
            hidden = jnp.dot(x, wi_ref[...], preferred_element_type=f32)
            hidden = jax.nn.gelu(hidden, approximate=True).astype(bf16)
            return jnp.dot(hidden, wo_ref[...], preferred_element_type=f32)

        backs = []

        def answer(index, source):
            psend[index] = partial(fbuf[source]).astype(bf16)
            back = pltpu.make_async_remote_copy(
                src_ref=psend.at[index],
                dst_ref=pbuf.at[index],
                send_sem=send_p.at[index],
                recv_sem=recv_p.at[index],
                device_id=(row, source),
                device_id_type=mesh_ids,
            )
            back.start()
            backs.append(back)

        acc = partial(f_ref[...])
        near.wait_recv()
        answer(0, sibling)
        relays = []
        for k, copy in enumerate(far, 1):
            copy.wait_recv()
            source = lax.rem(chip - k + chips, chips) * 2 + core
            relay = pltpu.make_async_remote_copy(
                src_ref=fbuf.at[source],
                dst_ref=fbuf.at[source],
                send_sem=send_r.at[k],
                recv_sem=recv_r.at[k],
                device_id=(row, sibling),
                device_id_type=mesh_ids,
            )
            relay.start()
            relays.append(relay)
            answer(k, source)
        for k, relay in enumerate(relays, 1):
            relay.wait_recv()
            answer(chips - 1 + k, lax.rem(chip - k + chips, chips) * 2 + 1 - core)
        for index, back in enumerate(backs):
            back.wait_recv()
            acc = acc + pbuf[index].astype(f32)
        o_ref[...] = acc.astype(o_ref.dtype)
        near.wait_send()
        for copy in far:
            copy.wait_send()
        for relay in relays:
            relay.wait_send()
        for back in backs:
            back.wait_send()

    return pl.pallas_call(
        kernel,
        out_shape=jax.ShapeDtypeStruct((rows, width_model), bf16),
        in_specs=[pl.BlockSpec(memory_space=pltpu.VMEM)] * 3,
        out_specs=pl.BlockSpec(memory_space=pltpu.VMEM),
        scratch_shapes=[
            pltpu.VMEM((n, rows, width_vis), feats.dtype),
            pltpu.VMEM((n, rows, width_model), bf16),
            pltpu.VMEM((n, rows, width_model), bf16),
            pltpu.SemaphoreType.DMA,
            pltpu.SemaphoreType.DMA,
            pltpu.SemaphoreType.DMA((chips,)),
            pltpu.SemaphoreType.DMA((chips,)),
            pltpu.SemaphoreType.DMA((chips,)),
            pltpu.SemaphoreType.DMA((chips,)),
            pltpu.SemaphoreType.DMA((n,)),
            pltpu.SemaphoreType.DMA((n,)),
        ],
        compiler_params=pltpu.CompilerParams(
            collective_id=collective_id, has_side_effects=True, vmem_limit_bytes=48 * 1024 * 1024
        ),
    )(feats, proj_in, proj_out)


def normalize(rows, norm_gain):
    rows_f = rows.astype(jnp.float32)
    meansq = jnp.mean(rows_f * rows_f, axis=-1, keepdims=True) + 1e-06
    return (rows_f * lax.rsqrt(meansq) * norm_gain).astype(jnp.bfloat16)


def select_dot(sel, rows):
    return jnp.dot(sel, rows, preferred_element_type=jnp.float32)


def shards(
    text_embed,
    image_feats,
    tile_pos,
    proj_in,
    proj_out,
    norm_gain,
    shared_gate,
    shared_up,
    shared_down,
    expert_gate,
    expert_up,
    expert_down,
    route_ids,
    route_wts,
):
    bf16, f32 = jnp.bfloat16, jnp.float32
    tok_dev, width_model = text_embed.shape
    img_dev, width_vis = image_feats.shape
    n_data = lax.axis_size("dp")
    n_group = lax.axis_size("expert")
    peer = img_dev // n_data
    my_place = lax.axis_index("expert")

    route_cols = jnp.concatenate([route_ids, route_wts // 256, route_wts % 256], axis=1)
    route_cols = jnp.pad(route_cols, ((0, 0), (0, 128 - route_cols.shape[1])))

    dest_index = tile_pos // tok_dev // n_group
    order = jnp.argsort(dest_index, stable=True)
    offs_sorted = (tile_pos[order] % tok_dev).astype(bf16)
    pad = 128
    packed = jnp.concatenate(
        [image_feats[order], jnp.broadcast_to(offs_sorted[:, None], (img_dev, pad))], axis=1
    ).reshape(n_data, peer, width_vis + pad)
    moved = lax.all_to_all(packed, "dp", split_axis=0, concat_axis=0, tiled=True)
    moved = moved.reshape(img_dev, width_vis + pad)
    moved_feats = moved[:, :width_vis]
    moved_offs = moved[:, width_vis].astype(jnp.int32)

    projected = fused_projector(moved_feats, proj_in, proj_out, 5)

    place = (
        moved_offs[None, :] == jnp.arange(tok_dev, dtype=jnp.int32)[:, None]
    ).astype(bf16)
    placed = select_dot(place, projected)
    has_image = jnp.sum(place.astype(f32), axis=1, keepdims=True) > 0
    embed_own = jnp.where(has_image, placed, text_embed.astype(f32))
    normed_own = normalize(embed_own, norm_gain)

    gathered = expert_all_gather(
        jnp.concatenate([normed_own, route_cols.astype(bf16)], axis=1), 6
    ).reshape(n_group * tok_dev, width_model + route_cols.shape[1])
    normed = gathered[:, :width_model]
    routes = gathered[:, width_model:].astype(f32)
    top_count = route_ids.shape[1]
    ids = routes[:, :top_count].astype(jnp.int32)
    weights_f = routes[:, top_count : 2 * top_count] * 256.0 + routes[:, 2 * top_count : 3 * top_count]

    gate_s = jnp.dot(normed, shared_gate, preferred_element_type=f32)
    up_s = jnp.dot(normed, shared_up, preferred_element_type=f32)
    shared_hidden = (jax.nn.silu(gate_s) * up_s).astype(bf16)

    group_rows = normed.shape[0]
    n_pairs = group_rows * top_count
    capacity = 3 * group_rows * top_count // (2 * n_data)
    share = capacity // n_group
    flat_ids = ids.reshape(-1)
    onehot = (flat_ids[:, None] == jnp.arange(n_data, dtype=jnp.int32)[None, :]).astype(bf16)
    pair_iota = jnp.arange(n_pairs, dtype=jnp.int32)
    earlier = (pair_iota[None, :] < pair_iota[:, None]).astype(bf16)
    counts = select_dot(earlier, onehot)
    rank = jnp.sum(counts * onehot.astype(f32), axis=1).astype(jnp.int32)

    inside = rank // share == my_place
    row_of = jnp.where(inside, flat_ids * share + rank - my_place * share, -1)
    n_rows = n_data * share
    hit = (
        row_of.reshape(group_rows, top_count)[:, :, None]
        == jnp.arange(n_rows, dtype=jnp.int32)[None, None, :]
    )
    pick = jnp.sum(hit.astype(f32), axis=1).astype(bf16)
    lanes = 128
    block = (n_data, share * width_model // lanes, lanes)
    send = select_dot(pick.T, normed).astype(bf16).reshape(block)
    arrived = lax.all_to_all(send, "dp", split_axis=0, concat_axis=0, tiled=True)
    slots = lax.all_gather(arrived.reshape(n_rows, width_model), "expert", axis=0, tiled=True)

    width_e = expert_gate.shape[2]
    gate_up = jnp.dot(
        slots, jnp.concatenate([expert_gate[0], expert_up[0]], axis=1), preferred_element_type=f32
    )
    gate_e, up_e = gate_up[:, :width_e], gate_up[:, width_e:]
    hidden_e = (jax.nn.silu(gate_e) * up_e).astype(bf16)
    partial_out = jnp.dot(hidden_e, expert_down[0], preferred_element_type=f32).astype(bf16)
    summed = lax.psum_scatter(partial_out, "expert", scatter_dimension=0, tiled=True)
    returned = lax.all_to_all(
        summed.reshape(block), "dp", split_axis=0, concat_axis=0, tiled=True
    ).reshape(n_rows, width_model)

    weights_n = weights_f / jnp.sum(weights_f, axis=1, keepdims=True)
    coef = jnp.sum(jnp.where(hit, weights_n[:, :, None], 0.0), axis=1)
    coef_hi = coef.astype(bf16)
    coef_lo = (coef - coef_hi.astype(f32)).astype(bf16)
    terms = jnp.dot(
        jnp.concatenate([shared_hidden, coef_hi, coef_lo], axis=1),
        jnp.concatenate([shared_down, returned, returned], axis=0),
        preferred_element_type=f32,
    )
    return expert_reduce_scatter(
        terms.astype(bf16).reshape(n_group, tok_dev, width_model),
        4,
        bf16,
        embed_own.astype(bf16),
    )


def solution(mesh):
    return jax.shard_map(
        shards,
        mesh=mesh,
        in_specs=(
            P(("dp", "expert"), None),
            P(("dp", "expert"), None),
            P(("dp", "expert")),
            P(None, "expert"),
            P("expert", None),
            P(),
            P(None, "expert"),
            P(None, "expert"),
            P("expert", None),
            P("dp", None, "expert"),
            P("dp", None, "expert"),
            P("dp", "expert", None),
            P(("dp", "expert"), None),
            P(("dp", "expert"), None),
        ),
        out_specs=P(("dp", "expert"), None),
        check_vma=False,
    )
```

```python
import jax
import jax.numpy as jnp
from jax import lax
from jax.experimental import pallas as pl
from jax.experimental.pallas import tpu as pltpu
from jax.sharding import PartitionSpec as P


def dp_all_to_all(x, collective_id):
    n = x.shape[0]
    mesh_ids = pl.DeviceIdType.MESH

    def kernel(x_ref, y_ref, send_sem, recv_sem, local_sem):
        me = lax.axis_index("dp")
        j = lax.axis_index("expert")
        barrier = pltpu.get_barrier_semaphore()
        for k in range(1, n):
            pl.semaphore_signal(
                barrier, inc=1, device_id=(lax.rem(me + k, n), j), device_id_type=mesh_ids
            )
        pl.semaphore_wait(barrier, n - 1)
        local = pltpu.make_async_copy(x_ref.at[me], y_ref.at[me], local_sem)
        local.start()
        copies = []
        for k in range(1, n):
            peer = lax.rem(me + k, n)
            copy = pltpu.make_async_remote_copy(
                src_ref=x_ref.at[peer],
                dst_ref=y_ref.at[me],
                send_sem=send_sem.at[k],
                recv_sem=recv_sem.at[k],
                device_id=(peer, j),
                device_id_type=mesh_ids,
            )
            copy.start()
            copies.append(copy)
        local.wait()
        for copy in copies:
            copy.wait()

    return pl.pallas_call(
        kernel,
        out_shape=jax.ShapeDtypeStruct(x.shape, x.dtype),
        in_specs=[pl.BlockSpec(memory_space=pl.ANY)],
        out_specs=pl.BlockSpec(memory_space=pl.ANY),
        scratch_shapes=[
            pltpu.SemaphoreType.DMA((n,)),
            pltpu.SemaphoreType.DMA((n,)),
            pltpu.SemaphoreType.DMA,
        ],
        compiler_params=pltpu.CompilerParams(collective_id=collective_id, has_side_effects=True),
    )(x)


def expert_reduce_scatter(x, collective_id, out_dtype, base):
    n, rows, cols = x.shape
    chips = n // 2
    mesh_ids = pl.DeviceIdType.MESH

    def kernel(x_ref, b_ref, o_ref, pair_buf, part, far_buf, send1, recv1, send2, recv2):
        me = lax.axis_index("expert")
        row = lax.axis_index("dp")
        chip, core = me // 2, me % 2
        sibling = chip * 2 + 1 - core
        barrier = pltpu.get_barrier_semaphore()
        pl.semaphore_signal(barrier, inc=1, device_id=(row, sibling), device_id_type=mesh_ids)
        for k in range(1, chips):
            pl.semaphore_signal(
                barrier,
                inc=1,
                device_id=(row, lax.rem(chip + k, chips) * 2 + core),
                device_id_type=mesh_ids,
            )
        pl.semaphore_wait(barrier, chips)
        first = pltpu.make_async_remote_copy(
            src_ref=x_ref.at[:, 1 - core],
            dst_ref=pair_buf,
            send_sem=send1,
            recv_sem=recv1,
            device_id=(row, sibling),
            device_id_type=mesh_ids,
        )
        first.start()
        first.wait()
        copies = []
        for k in range(1, chips):
            dest = lax.rem(chip + k, chips)
            part[k] = (
                x_ref[dest, core].astype(jnp.float32) + pair_buf[dest].astype(jnp.float32)
            ).astype(part.dtype)
            copy = pltpu.make_async_remote_copy(
                src_ref=part.at[k],
                dst_ref=far_buf.at[k],
                send_sem=send2.at[k],
                recv_sem=recv2.at[k],
                device_id=(row, dest * 2 + core),
                device_id_type=mesh_ids,
            )
            copy.start()
            copies.append(copy)
        acc = x_ref[chip, core].astype(jnp.float32) + pair_buf[chip].astype(jnp.float32)
        acc = acc + b_ref[...].astype(jnp.float32)
        for k, copy in enumerate(copies, 1):
            copy.wait()
            acc = acc + far_buf[k].astype(jnp.float32)
        o_ref[...] = acc.astype(o_ref.dtype)

    return pl.pallas_call(
        kernel,
        out_shape=jax.ShapeDtypeStruct((rows, cols), out_dtype),
        in_specs=[pl.BlockSpec(memory_space=pltpu.VMEM)] * 2,
        out_specs=pl.BlockSpec(memory_space=pltpu.VMEM),
        scratch_shapes=[
            pltpu.VMEM((chips, rows, cols), x.dtype),
            pltpu.VMEM((chips, rows, cols), x.dtype),
            pltpu.VMEM((chips, rows, cols), x.dtype),
            pltpu.SemaphoreType.DMA,
            pltpu.SemaphoreType.DMA,
            pltpu.SemaphoreType.DMA((chips,)),
            pltpu.SemaphoreType.DMA((chips,)),
        ],
        compiler_params=pltpu.CompilerParams(collective_id=collective_id, has_side_effects=True),
    )(x.reshape(chips, 2, rows, cols), base)


def expert_all_gather(x, collective_id):
    rows, cols = x.shape
    n = lax.axis_size("expert")
    chips = n // 2
    mesh_ids = pl.DeviceIdType.MESH

    def kernel(x_ref, o_ref, send0, recv0, send1, recv1, send2, recv2):
        me = lax.axis_index("expert")
        row = lax.axis_index("dp")
        chip, core = me // 2, me % 2
        sibling = chip * 2 + 1 - core
        barrier = pltpu.get_barrier_semaphore()
        pl.semaphore_signal(barrier, inc=1, device_id=(row, sibling), device_id_type=mesh_ids)
        for k in range(1, chips):
            pl.semaphore_signal(
                barrier,
                inc=1,
                device_id=(row, lax.rem(chip + k, chips) * 2 + core),
                device_id_type=mesh_ids,
            )
        pl.semaphore_wait(barrier, chips)
        near = pltpu.make_async_remote_copy(
            src_ref=x_ref,
            dst_ref=o_ref.at[me],
            send_sem=send0,
            recv_sem=recv0,
            device_id=(row, sibling),
            device_id_type=mesh_ids,
        )
        near.start()
        far = []
        for k in range(1, chips):
            copy = pltpu.make_async_remote_copy(
                src_ref=x_ref,
                dst_ref=o_ref.at[me],
                send_sem=send1.at[k],
                recv_sem=recv1.at[k],
                device_id=(row, lax.rem(chip + k, chips) * 2 + core),
                device_id_type=mesh_ids,
            )
            copy.start()
            far.append(copy)
        o_ref[me] = x_ref[...]
        passed = []
        for k, copy in enumerate(far, 1):
            copy.wait_recv()
            source = lax.rem(chip - k + chips, chips) * 2 + core
            relay = pltpu.make_async_remote_copy(
                src_ref=o_ref.at[source],
                dst_ref=o_ref.at[source],
                send_sem=send2.at[k],
                recv_sem=recv2.at[k],
                device_id=(row, sibling),
                device_id_type=mesh_ids,
            )
            relay.start()
            passed.append(relay)
        near.wait()
        for copy in far:
            copy.wait_send()
        for relay in passed:
            relay.wait()

    return pl.pallas_call(
        kernel,
        out_shape=jax.ShapeDtypeStruct((n, rows, cols), x.dtype),
        in_specs=[pl.BlockSpec(memory_space=pltpu.VMEM)],
        out_specs=pl.BlockSpec(memory_space=pltpu.VMEM),
        scratch_shapes=[
            pltpu.SemaphoreType.DMA,
            pltpu.SemaphoreType.DMA,
            pltpu.SemaphoreType.DMA((chips,)),
            pltpu.SemaphoreType.DMA((chips,)),
            pltpu.SemaphoreType.DMA((chips,)),
            pltpu.SemaphoreType.DMA((chips,)),
        ],
        compiler_params=pltpu.CompilerParams(collective_id=collective_id, has_side_effects=True),
    )(x)


def fused_projector(feats, proj_in, proj_out, collective_id):
    rows, width_vis = feats.shape
    n = lax.axis_size("expert")
    chips = n // 2
    width_model = proj_out.shape[1]
    mesh_ids = pl.DeviceIdType.MESH
    f32, bf16 = jnp.float32, jnp.bfloat16

    def kernel(
        f_ref, wi_ref, wo_ref, o_ref, fbuf, psend, pbuf,
        send_n, recv_n, send_f, recv_f, send_r, recv_r, send_p, recv_p,
    ):
        me = lax.axis_index("expert")
        row = lax.axis_index("dp")
        chip, core = me // 2, me % 2
        sibling = chip * 2 + 1 - core
        barrier = pltpu.get_barrier_semaphore()
        for k in range(1, n):
            pl.semaphore_signal(
                barrier, inc=1, device_id=(row, lax.rem(me + k, n)), device_id_type=mesh_ids
            )
        pl.semaphore_wait(barrier, n - 1)
        near = pltpu.make_async_remote_copy(
            src_ref=f_ref,
            dst_ref=fbuf.at[me],
            send_sem=send_n,
            recv_sem=recv_n,
            device_id=(row, sibling),
            device_id_type=mesh_ids,
        )
        near.start()
        far = []
        for k in range(1, chips):
            copy = pltpu.make_async_remote_copy(
                src_ref=f_ref,
                dst_ref=fbuf.at[me],
                send_sem=send_f.at[k],
                recv_sem=recv_f.at[k],
                device_id=(row, lax.rem(chip + k, chips) * 2 + core),
                device_id_type=mesh_ids,
            )
            copy.start()
            far.append(copy)

        def partial(x):
            hidden = jnp.dot(x, wi_ref[...], preferred_element_type=f32)
            hidden = jax.nn.gelu(hidden, approximate=True).astype(bf16)
            return jnp.dot(hidden, wo_ref[...], preferred_element_type=f32)

        backs = []

        def answer(index, source):
            psend[index] = partial(fbuf[source]).astype(bf16)
            back = pltpu.make_async_remote_copy(
                src_ref=psend.at[index],
                dst_ref=pbuf.at[index],
                send_sem=send_p.at[index],
                recv_sem=recv_p.at[index],
                device_id=(row, source),
                device_id_type=mesh_ids,
            )
            back.start()
            backs.append(back)

        acc = partial(f_ref[...])
        near.wait_recv()
        answer(0, sibling)
        relays = []
        for k, copy in enumerate(far, 1):
            copy.wait_recv()
            source = lax.rem(chip - k + chips, chips) * 2 + core
            relay = pltpu.make_async_remote_copy(
                src_ref=fbuf.at[source],
                dst_ref=fbuf.at[source],
                send_sem=send_r.at[k],
                recv_sem=recv_r.at[k],
                device_id=(row, sibling),
                device_id_type=mesh_ids,
            )
            relay.start()
            relays.append(relay)
            answer(k, source)
        for k, relay in enumerate(relays, 1):
            relay.wait_recv()
            answer(chips - 1 + k, lax.rem(chip - k + chips, chips) * 2 + 1 - core)
        for index, back in enumerate(backs):
            back.wait_recv()
            acc = acc + pbuf[index].astype(f32)
        o_ref[...] = acc.astype(o_ref.dtype)
        near.wait_send()
        for copy in far:
            copy.wait_send()
        for relay in relays:
            relay.wait_send()
        for back in backs:
            back.wait_send()

    return pl.pallas_call(
        kernel,
        out_shape=jax.ShapeDtypeStruct((rows, width_model), bf16),
        in_specs=[pl.BlockSpec(memory_space=pltpu.VMEM)] * 3,
        out_specs=pl.BlockSpec(memory_space=pltpu.VMEM),
        scratch_shapes=[
            pltpu.VMEM((n, rows, width_vis), feats.dtype),
            pltpu.VMEM((n, rows, width_model), bf16),
            pltpu.VMEM((n, rows, width_model), bf16),
            pltpu.SemaphoreType.DMA,
            pltpu.SemaphoreType.DMA,
            pltpu.SemaphoreType.DMA((chips,)),
            pltpu.SemaphoreType.DMA((chips,)),
            pltpu.SemaphoreType.DMA((chips,)),
            pltpu.SemaphoreType.DMA((chips,)),
            pltpu.SemaphoreType.DMA((n,)),
            pltpu.SemaphoreType.DMA((n,)),
        ],
        compiler_params=pltpu.CompilerParams(
            collective_id=collective_id, has_side_effects=True, vmem_limit_bytes=48 * 1024 * 1024
        ),
    )(feats, proj_in, proj_out)


def normalize(rows, norm_gain):
    rows_f = rows.astype(jnp.float32)
    meansq = jnp.mean(rows_f * rows_f, axis=-1, keepdims=True) + 1e-06
    return (rows_f * lax.rsqrt(meansq) * norm_gain).astype(jnp.bfloat16)


def select_dot(sel, rows):
    return jnp.dot(sel, rows, preferred_element_type=jnp.float32)


def shards(
    text_embed,
    image_feats,
    tile_pos,
    proj_in,
    proj_out,
    norm_gain,
    shared_gate,
    shared_up,
    shared_down,
    expert_gate,
    expert_up,
    expert_down,
    route_ids,
    route_wts,
):
    bf16, f32 = jnp.bfloat16, jnp.float32
    tok_dev, width_model = text_embed.shape
    img_dev, width_vis = image_feats.shape
    n_data = lax.axis_size("dp")
    n_group = lax.axis_size("expert")
    peer = img_dev // n_data
    my_place = lax.axis_index("expert")

    route_cols = jnp.concatenate([route_ids, route_wts // 256, route_wts % 256], axis=1)
    route_cols = jnp.pad(route_cols, ((0, 0), (0, 128 - route_cols.shape[1])))

    dest_index = tile_pos // tok_dev // n_group
    order = jnp.argsort(dest_index, stable=True)
    offs_sorted = (tile_pos[order] % tok_dev).astype(bf16)
    pad = 128
    packed = jnp.concatenate(
        [image_feats[order], jnp.broadcast_to(offs_sorted[:, None], (img_dev, pad))], axis=1
    ).reshape(n_data, peer, width_vis + pad)
    moved = lax.all_to_all(packed, "dp", split_axis=0, concat_axis=0, tiled=True)
    moved = moved.reshape(img_dev, width_vis + pad)
    moved_feats = moved[:, :width_vis]
    moved_offs = moved[:, width_vis].astype(jnp.int32)

    projected = fused_projector(moved_feats, proj_in, proj_out, 5)

    place = (
        moved_offs[None, :] == jnp.arange(tok_dev, dtype=jnp.int32)[:, None]
    ).astype(bf16)
    placed = select_dot(place, projected)
    has_image = jnp.sum(place.astype(f32), axis=1, keepdims=True) > 0
    embed_own = jnp.where(has_image, placed, text_embed.astype(f32))

    text_gathered = lax.all_gather(
        jnp.concatenate([normalize(text_embed, norm_gain), route_cols.astype(bf16)], axis=1),
        "expert",
        axis=0,
        tiled=True,
    )
    image_block = jnp.concatenate(
        [
            normalize(projected, norm_gain),
            jnp.broadcast_to(moved_offs.astype(bf16)[:, None], (img_dev, pad)),
        ],
        axis=1,
    )
    image_rows = expert_all_gather(image_block, 6)
    group_offs = image_rows[:, :, width_model].astype(jnp.int32)
    spot = (
        group_offs[:, None, :] == jnp.arange(tok_dev, dtype=jnp.int32)[None, :, None]
    ).astype(bf16)
    image_placed = jnp.einsum(
        "gri,gid->grd", spot, image_rows[:, :, :width_model], preferred_element_type=f32
    ).reshape(n_group * tok_dev, width_model)
    image_here = (jnp.sum(spot.astype(f32), axis=2) > 0).reshape(n_group * tok_dev, 1)
    normed = jnp.where(
        image_here, image_placed, text_gathered[:, :width_model].astype(f32)
    ).astype(bf16)
    routes = text_gathered[:, width_model:].astype(f32)
    top_count = route_ids.shape[1]
    ids = routes[:, :top_count].astype(jnp.int32)
    weights_f = routes[:, top_count : 2 * top_count] * 256.0 + routes[:, 2 * top_count : 3 * top_count]

    gate_s = jnp.dot(normed, shared_gate, preferred_element_type=f32)
    up_s = jnp.dot(normed, shared_up, preferred_element_type=f32)
    shared_hidden = (jax.nn.silu(gate_s) * up_s).astype(bf16)

    group_rows = normed.shape[0]
    n_pairs = group_rows * top_count
    capacity = 3 * group_rows * top_count // (2 * n_data)
    share = capacity // n_group
    flat_ids = ids.reshape(-1)
    onehot = (flat_ids[:, None] == jnp.arange(n_data, dtype=jnp.int32)[None, :]).astype(bf16)
    pair_iota = jnp.arange(n_pairs, dtype=jnp.int32)
    earlier = (pair_iota[None, :] < pair_iota[:, None]).astype(bf16)
    counts = select_dot(earlier, onehot)
    rank = jnp.sum(counts * onehot.astype(f32), axis=1).astype(jnp.int32)

    inside = rank // share == my_place
    row_of = jnp.where(inside, flat_ids * share + rank - my_place * share, -1)
    n_rows = n_data * share
    hit = (
        row_of.reshape(group_rows, top_count)[:, :, None]
        == jnp.arange(n_rows, dtype=jnp.int32)[None, None, :]
    )
    pick = jnp.sum(hit.astype(f32), axis=1).astype(bf16)
    lanes = 128
    block = (n_data, share * width_model // lanes, lanes)
    send = select_dot(pick.T, normed).astype(bf16).reshape(block)
    arrived = lax.all_to_all(send, "dp", split_axis=0, concat_axis=0, tiled=True)
    slots = lax.all_gather(arrived.reshape(n_rows, width_model), "expert", axis=0, tiled=True)

    width_e = expert_gate.shape[2]
    gate_up = jnp.dot(
        slots, jnp.concatenate([expert_gate[0], expert_up[0]], axis=1), preferred_element_type=f32
    )
    gate_e, up_e = gate_up[:, :width_e], gate_up[:, width_e:]
    hidden_e = (jax.nn.silu(gate_e) * up_e).astype(bf16)
    partial_out = jnp.dot(hidden_e, expert_down[0], preferred_element_type=f32).astype(bf16)
    summed = lax.psum_scatter(partial_out, "expert", scatter_dimension=0, tiled=True)
    returned = lax.all_to_all(
        summed.reshape(block), "dp", split_axis=0, concat_axis=0, tiled=True
    ).reshape(n_rows, width_model)

    weights_n = weights_f / jnp.sum(weights_f, axis=1, keepdims=True)
    coef = jnp.sum(jnp.where(hit, weights_n[:, :, None], 0.0), axis=1)
    coef_hi = coef.astype(bf16)
    coef_lo = (coef - coef_hi.astype(f32)).astype(bf16)
    terms = jnp.dot(
        jnp.concatenate([shared_hidden, coef_hi, coef_lo], axis=1),
        jnp.concatenate([shared_down, returned, returned], axis=0),
        preferred_element_type=f32,
    )
    return expert_reduce_scatter(
        terms.astype(bf16).reshape(n_group, tok_dev, width_model),
        4,
        bf16,
        embed_own.astype(bf16),
    )


def solution(mesh):
    return jax.shard_map(
        shards,
        mesh=mesh,
        in_specs=(
            P(("dp", "expert"), None),
            P(("dp", "expert"), None),
            P(("dp", "expert")),
            P(None, "expert"),
            P("expert", None),
            P(),
            P(None, "expert"),
            P(None, "expert"),
            P("expert", None),
            P("dp", None, "expert"),
            P("dp", None, "expert"),
            P("dp", "expert", None),
            P(("dp", "expert"), None),
            P(("dp", "expert"), None),
        ),
        out_specs=P(("dp", "expert"), None),
        check_vma=False,
    )
```

```python
import jax
import jax.numpy as jnp
from jax import lax
from jax.experimental import pallas as pl
from jax.experimental.pallas import tpu as pltpu
from jax.sharding import PartitionSpec as P


def dp_all_to_all(x, collective_id):
    n = x.shape[0]
    mesh_ids = pl.DeviceIdType.MESH

    def kernel(x_ref, y_ref, send_sem, recv_sem, local_sem):
        me = lax.axis_index("dp")
        j = lax.axis_index("expert")
        barrier = pltpu.get_barrier_semaphore()
        for k in range(1, n):
            pl.semaphore_signal(
                barrier, inc=1, device_id=(lax.rem(me + k, n), j), device_id_type=mesh_ids
            )
        pl.semaphore_wait(barrier, n - 1)
        local = pltpu.make_async_copy(x_ref.at[me], y_ref.at[me], local_sem)
        local.start()
        copies = []
        for k in range(1, n):
            peer = lax.rem(me + k, n)
            copy = pltpu.make_async_remote_copy(
                src_ref=x_ref.at[peer],
                dst_ref=y_ref.at[me],
                send_sem=send_sem.at[k],
                recv_sem=recv_sem.at[k],
                device_id=(peer, j),
                device_id_type=mesh_ids,
            )
            copy.start()
            copies.append(copy)
        local.wait()
        for copy in copies:
            copy.wait()

    return pl.pallas_call(
        kernel,
        out_shape=jax.ShapeDtypeStruct(x.shape, x.dtype),
        in_specs=[pl.BlockSpec(memory_space=pl.ANY)],
        out_specs=pl.BlockSpec(memory_space=pl.ANY),
        scratch_shapes=[
            pltpu.SemaphoreType.DMA((n,)),
            pltpu.SemaphoreType.DMA((n,)),
            pltpu.SemaphoreType.DMA,
        ],
        compiler_params=pltpu.CompilerParams(collective_id=collective_id, has_side_effects=True),
    )(x)


def expert_reduce_scatter(x, collective_id, out_dtype, base):
    n, rows, cols = x.shape
    chips = n // 2
    mesh_ids = pl.DeviceIdType.MESH

    def kernel(x_ref, b_ref, o_ref, pair_buf, part, far_buf, send1, recv1, send2, recv2):
        me = lax.axis_index("expert")
        row = lax.axis_index("dp")
        chip, core = me // 2, me % 2
        sibling = chip * 2 + 1 - core
        barrier = pltpu.get_barrier_semaphore()
        pl.semaphore_signal(barrier, inc=1, device_id=(row, sibling), device_id_type=mesh_ids)
        for k in range(1, chips):
            pl.semaphore_signal(
                barrier,
                inc=1,
                device_id=(row, lax.rem(chip + k, chips) * 2 + core),
                device_id_type=mesh_ids,
            )
        pl.semaphore_wait(barrier, chips)
        first = pltpu.make_async_remote_copy(
            src_ref=x_ref.at[:, 1 - core],
            dst_ref=pair_buf,
            send_sem=send1,
            recv_sem=recv1,
            device_id=(row, sibling),
            device_id_type=mesh_ids,
        )
        first.start()
        first.wait()
        copies = []
        for k in range(1, chips):
            dest = lax.rem(chip + k, chips)
            part[k] = (
                x_ref[dest, core].astype(jnp.float32) + pair_buf[dest].astype(jnp.float32)
            ).astype(part.dtype)
            copy = pltpu.make_async_remote_copy(
                src_ref=part.at[k],
                dst_ref=far_buf.at[k],
                send_sem=send2.at[k],
                recv_sem=recv2.at[k],
                device_id=(row, dest * 2 + core),
                device_id_type=mesh_ids,
            )
            copy.start()
            copies.append(copy)
        acc = x_ref[chip, core].astype(jnp.float32) + pair_buf[chip].astype(jnp.float32)
        acc = acc + b_ref[...].astype(jnp.float32)
        for k, copy in enumerate(copies, 1):
            copy.wait()
            acc = acc + far_buf[k].astype(jnp.float32)
        o_ref[...] = acc.astype(o_ref.dtype)

    return pl.pallas_call(
        kernel,
        out_shape=jax.ShapeDtypeStruct((rows, cols), out_dtype),
        in_specs=[pl.BlockSpec(memory_space=pltpu.VMEM)] * 2,
        out_specs=pl.BlockSpec(memory_space=pltpu.VMEM),
        scratch_shapes=[
            pltpu.VMEM((chips, rows, cols), x.dtype),
            pltpu.VMEM((chips, rows, cols), x.dtype),
            pltpu.VMEM((chips, rows, cols), x.dtype),
            pltpu.SemaphoreType.DMA,
            pltpu.SemaphoreType.DMA,
            pltpu.SemaphoreType.DMA((chips,)),
            pltpu.SemaphoreType.DMA((chips,)),
        ],
        compiler_params=pltpu.CompilerParams(collective_id=collective_id, has_side_effects=True),
    )(x.reshape(chips, 2, rows, cols), base)


def expert_all_gather(x, collective_id):
    rows, cols = x.shape
    n = lax.axis_size("expert")
    chips = n // 2
    mesh_ids = pl.DeviceIdType.MESH

    def kernel(x_ref, o_ref, send0, recv0, send1, recv1, send2, recv2):
        me = lax.axis_index("expert")
        row = lax.axis_index("dp")
        chip, core = me // 2, me % 2
        sibling = chip * 2 + 1 - core
        barrier = pltpu.get_barrier_semaphore()
        pl.semaphore_signal(barrier, inc=1, device_id=(row, sibling), device_id_type=mesh_ids)
        for k in range(1, chips):
            pl.semaphore_signal(
                barrier,
                inc=1,
                device_id=(row, lax.rem(chip + k, chips) * 2 + core),
                device_id_type=mesh_ids,
            )
        pl.semaphore_wait(barrier, chips)
        near = pltpu.make_async_remote_copy(
            src_ref=x_ref,
            dst_ref=o_ref.at[me],
            send_sem=send0,
            recv_sem=recv0,
            device_id=(row, sibling),
            device_id_type=mesh_ids,
        )
        near.start()
        far = []
        for k in range(1, chips):
            copy = pltpu.make_async_remote_copy(
                src_ref=x_ref,
                dst_ref=o_ref.at[me],
                send_sem=send1.at[k],
                recv_sem=recv1.at[k],
                device_id=(row, lax.rem(chip + k, chips) * 2 + core),
                device_id_type=mesh_ids,
            )
            copy.start()
            far.append(copy)
        o_ref[me] = x_ref[...]
        passed = []
        for k, copy in enumerate(far, 1):
            copy.wait_recv()
            source = lax.rem(chip - k + chips, chips) * 2 + core
            relay = pltpu.make_async_remote_copy(
                src_ref=o_ref.at[source],
                dst_ref=o_ref.at[source],
                send_sem=send2.at[k],
                recv_sem=recv2.at[k],
                device_id=(row, sibling),
                device_id_type=mesh_ids,
            )
            relay.start()
            passed.append(relay)
        near.wait()
        for copy in far:
            copy.wait_send()
        for relay in passed:
            relay.wait()

    return pl.pallas_call(
        kernel,
        out_shape=jax.ShapeDtypeStruct((n, rows, cols), x.dtype),
        in_specs=[pl.BlockSpec(memory_space=pltpu.VMEM)],
        out_specs=pl.BlockSpec(memory_space=pltpu.VMEM),
        scratch_shapes=[
            pltpu.SemaphoreType.DMA,
            pltpu.SemaphoreType.DMA,
            pltpu.SemaphoreType.DMA((chips,)),
            pltpu.SemaphoreType.DMA((chips,)),
            pltpu.SemaphoreType.DMA((chips,)),
            pltpu.SemaphoreType.DMA((chips,)),
        ],
        compiler_params=pltpu.CompilerParams(collective_id=collective_id, has_side_effects=True),
    )(x)


def fused_projector(feats, proj_in, proj_out, collective_id):
    rows, width_vis = feats.shape
    n = lax.axis_size("expert")
    chips = n // 2
    width_model = proj_out.shape[1]
    mesh_ids = pl.DeviceIdType.MESH
    f32, bf16 = jnp.float32, jnp.bfloat16

    def kernel(
        f_ref, wi_ref, wo_ref, o_ref, fbuf, psend, pbuf,
        send_n, recv_n, send_f, recv_f, send_r, recv_r, send_p, recv_p,
    ):
        me = lax.axis_index("expert")
        row = lax.axis_index("dp")
        chip, core = me // 2, me % 2
        sibling = chip * 2 + 1 - core
        barrier = pltpu.get_barrier_semaphore()
        for k in range(1, n):
            pl.semaphore_signal(
                barrier, inc=1, device_id=(row, lax.rem(me + k, n)), device_id_type=mesh_ids
            )
        pl.semaphore_wait(barrier, n - 1)
        near = pltpu.make_async_remote_copy(
            src_ref=f_ref,
            dst_ref=fbuf.at[me],
            send_sem=send_n,
            recv_sem=recv_n,
            device_id=(row, sibling),
            device_id_type=mesh_ids,
        )
        near.start()
        far = []
        for k in range(1, chips):
            copy = pltpu.make_async_remote_copy(
                src_ref=f_ref,
                dst_ref=fbuf.at[me],
                send_sem=send_f.at[k],
                recv_sem=recv_f.at[k],
                device_id=(row, lax.rem(chip + k, chips) * 2 + core),
                device_id_type=mesh_ids,
            )
            copy.start()
            far.append(copy)

        def partial(x):
            hidden = jnp.dot(x, wi_ref[...], preferred_element_type=f32)
            hidden = jax.nn.gelu(hidden, approximate=True).astype(bf16)
            return jnp.dot(hidden, wo_ref[...], preferred_element_type=f32)

        backs = []

        def answer(index, source):
            psend[index] = partial(fbuf[source]).astype(bf16)
            back = pltpu.make_async_remote_copy(
                src_ref=psend.at[index],
                dst_ref=pbuf.at[index],
                send_sem=send_p.at[index],
                recv_sem=recv_p.at[index],
                device_id=(row, source),
                device_id_type=mesh_ids,
            )
            back.start()
            backs.append(back)

        acc = partial(f_ref[...])
        near.wait_recv()
        answer(0, sibling)
        relays = []
        for k, copy in enumerate(far, 1):
            copy.wait_recv()
            source = lax.rem(chip - k + chips, chips) * 2 + core
            relay = pltpu.make_async_remote_copy(
                src_ref=fbuf.at[source],
                dst_ref=fbuf.at[source],
                send_sem=send_r.at[k],
                recv_sem=recv_r.at[k],
                device_id=(row, sibling),
                device_id_type=mesh_ids,
            )
            relay.start()
            relays.append(relay)
            answer(k, source)
        for k, relay in enumerate(relays, 1):
            relay.wait_recv()
            answer(chips - 1 + k, lax.rem(chip - k + chips, chips) * 2 + 1 - core)
        for index, back in enumerate(backs):
            back.wait_recv()
            acc = acc + pbuf[index].astype(f32)
        o_ref[...] = acc.astype(o_ref.dtype)
        near.wait_send()
        for copy in far:
            copy.wait_send()
        for relay in relays:
            relay.wait_send()
        for back in backs:
            back.wait_send()

    return pl.pallas_call(
        kernel,
        out_shape=jax.ShapeDtypeStruct((rows, width_model), bf16),
        in_specs=[pl.BlockSpec(memory_space=pltpu.VMEM)] * 3,
        out_specs=pl.BlockSpec(memory_space=pltpu.VMEM),
        scratch_shapes=[
            pltpu.VMEM((n, rows, width_vis), feats.dtype),
            pltpu.VMEM((n, rows, width_model), bf16),
            pltpu.VMEM((n, rows, width_model), bf16),
            pltpu.SemaphoreType.DMA,
            pltpu.SemaphoreType.DMA,
            pltpu.SemaphoreType.DMA((chips,)),
            pltpu.SemaphoreType.DMA((chips,)),
            pltpu.SemaphoreType.DMA((chips,)),
            pltpu.SemaphoreType.DMA((chips,)),
            pltpu.SemaphoreType.DMA((n,)),
            pltpu.SemaphoreType.DMA((n,)),
        ],
        compiler_params=pltpu.CompilerParams(
            collective_id=collective_id, has_side_effects=True, vmem_limit_bytes=48 * 1024 * 1024
        ),
    )(feats, proj_in, proj_out)


def normalize(rows, norm_gain):
    rows_f = rows.astype(jnp.float32)
    meansq = jnp.mean(rows_f * rows_f, axis=-1, keepdims=True) + 1e-06
    return (rows_f * lax.rsqrt(meansq) * norm_gain).astype(jnp.bfloat16)


def select_dot(sel, rows):
    return jnp.dot(sel, rows, preferred_element_type=jnp.float32)


def shards(
    text_embed,
    image_feats,
    tile_pos,
    proj_in,
    proj_out,
    norm_gain,
    shared_gate,
    shared_up,
    shared_down,
    expert_gate,
    expert_up,
    expert_down,
    route_ids,
    route_wts,
):
    bf16, f32 = jnp.bfloat16, jnp.float32
    tok_dev, width_model = text_embed.shape
    img_dev, width_vis = image_feats.shape
    n_data = lax.axis_size("dp")
    n_group = lax.axis_size("expert")
    peer = img_dev // n_data
    my_place = lax.axis_index("expert")

    route_cols = jnp.concatenate([route_ids, route_wts // 256, route_wts % 256], axis=1)
    route_cols = jnp.pad(route_cols, ((0, 0), (0, 128 - route_cols.shape[1])))

    dest_index = tile_pos // tok_dev // n_group
    order = jnp.argsort(dest_index, stable=True)
    offs_sorted = (tile_pos[order] % tok_dev).astype(bf16)
    pad = 128
    packed = jnp.concatenate(
        [image_feats[order], jnp.broadcast_to(offs_sorted[:, None], (img_dev, pad))], axis=1
    ).reshape(n_data, peer, width_vis + pad)
    moved = lax.all_to_all(packed, "dp", split_axis=0, concat_axis=0, tiled=True)
    moved = moved.reshape(img_dev, width_vis + pad)
    moved_feats = moved[:, :width_vis]
    moved_offs = moved[:, width_vis].astype(jnp.int32)

    projected = fused_projector(moved_feats, proj_in, proj_out, 5)

    place = (
        moved_offs[None, :] == jnp.arange(tok_dev, dtype=jnp.int32)[:, None]
    ).astype(bf16)
    placed = select_dot(place, projected)
    has_image = jnp.sum(place.astype(f32), axis=1, keepdims=True) > 0
    embed_own = jnp.where(has_image, placed, text_embed.astype(f32))
    normed_own = normalize(embed_own, norm_gain)

    gathered = expert_all_gather(
        jnp.concatenate([normed_own, route_cols.astype(bf16)], axis=1), 6
    ).reshape(n_group * tok_dev, width_model + route_cols.shape[1])
    normed = gathered[:, :width_model]
    routes = gathered[:, width_model:].astype(f32)
    top_count = route_ids.shape[1]
    ids = routes[:, :top_count].astype(jnp.int32)
    weights_f = routes[:, top_count : 2 * top_count] * 256.0 + routes[:, 2 * top_count : 3 * top_count]

    gate_s = jnp.dot(normed, shared_gate, preferred_element_type=f32)
    up_s = jnp.dot(normed, shared_up, preferred_element_type=f32)
    shared_hidden = (jax.nn.silu(gate_s) * up_s).astype(bf16)

    group_rows = normed.shape[0]
    n_pairs = group_rows * top_count
    capacity = 3 * group_rows * top_count // (2 * n_data)
    share = capacity // n_group
    flat_ids = ids.reshape(-1)
    onehot = (flat_ids[:, None] == jnp.arange(n_data, dtype=jnp.int32)[None, :]).astype(bf16)
    pair_iota = jnp.arange(n_pairs, dtype=jnp.int32)
    earlier = (pair_iota[None, :] < pair_iota[:, None]).astype(bf16)
    counts = select_dot(earlier, onehot)
    rank = jnp.sum(counts * onehot.astype(f32), axis=1).astype(jnp.int32)

    inside = rank // share == my_place
    row_of = jnp.where(inside, flat_ids * share + rank - my_place * share, -1)
    n_rows = n_data * share
    hit = (
        row_of.reshape(group_rows, top_count)[:, :, None]
        == jnp.arange(n_rows, dtype=jnp.int32)[None, None, :]
    )
    pick = jnp.sum(hit.astype(f32), axis=1).astype(bf16)
    lanes = 128
    block = (n_data, share * width_model // lanes, lanes)
    send = select_dot(pick.T, normed).astype(bf16).reshape(block)
    arrived = dp_all_to_all(send, 1)
    slots = lax.all_gather(arrived.reshape(n_rows, width_model), "expert", axis=0, tiled=True)

    width_e = expert_gate.shape[2]
    gate_up = jnp.dot(
        slots, jnp.concatenate([expert_gate[0], expert_up[0]], axis=1), preferred_element_type=f32
    )
    gate_e, up_e = gate_up[:, :width_e], gate_up[:, width_e:]
    hidden_e = (jax.nn.silu(gate_e) * up_e).astype(bf16)
    partial_out = jnp.dot(hidden_e, expert_down[0], preferred_element_type=f32).astype(bf16)
    summed = lax.psum_scatter(partial_out, "expert", scatter_dimension=0, tiled=True)
    returned = lax.all_to_all(
        summed.reshape(block), "dp", split_axis=0, concat_axis=0, tiled=True
    ).reshape(n_rows, width_model)

    weights_n = weights_f / jnp.sum(weights_f, axis=1, keepdims=True)
    coef = jnp.sum(jnp.where(hit, weights_n[:, :, None], 0.0), axis=1)
    coef_hi = coef.astype(bf16)
    coef_lo = (coef - coef_hi.astype(f32)).astype(bf16)
    terms = jnp.dot(
        jnp.concatenate([shared_hidden, coef_hi, coef_lo], axis=1),
        jnp.concatenate([shared_down, returned, returned], axis=0),
        preferred_element_type=f32,
    )
    return expert_reduce_scatter(
        terms.astype(bf16).reshape(n_group, tok_dev, width_model),
        4,
        bf16,
        embed_own.astype(bf16),
    )


def solution(mesh):
    return jax.shard_map(
        shards,
        mesh=mesh,
        in_specs=(
            P(("dp", "expert"), None),
            P(("dp", "expert"), None),
            P(("dp", "expert")),
            P(None, "expert"),
            P("expert", None),
            P(),
            P(None, "expert"),
            P(None, "expert"),
            P("expert", None),
            P("dp", None, "expert"),
            P("dp", None, "expert"),
            P("dp", "expert", None),
            P(("dp", "expert"), None),
            P(("dp", "expert"), None),
        ),
        out_specs=P(("dp", "expert"), None),
        check_vma=False,
    )
```

```python
import jax
import jax.numpy as jnp
from jax import lax
from jax.experimental import pallas as pl
from jax.experimental.pallas import tpu as pltpu
from jax.sharding import PartitionSpec as P


def dp_all_to_all(x, collective_id):
    n = x.shape[0]
    mesh_ids = pl.DeviceIdType.MESH

    def kernel(x_ref, y_ref, send_sem, recv_sem, local_sem):
        me = lax.axis_index("dp")
        j = lax.axis_index("expert")
        barrier = pltpu.get_barrier_semaphore()
        for k in range(1, n):
            pl.semaphore_signal(
                barrier, inc=1, device_id=(lax.rem(me + k, n), j), device_id_type=mesh_ids
            )
        pl.semaphore_wait(barrier, n - 1)
        local = pltpu.make_async_copy(x_ref.at[me], y_ref.at[me], local_sem)
        local.start()
        copies = []
        for k in range(1, n):
            peer = lax.rem(me + k, n)
            copy = pltpu.make_async_remote_copy(
                src_ref=x_ref.at[peer],
                dst_ref=y_ref.at[me],
                send_sem=send_sem.at[k],
                recv_sem=recv_sem.at[k],
                device_id=(peer, j),
                device_id_type=mesh_ids,
            )
            copy.start()
            copies.append(copy)
        local.wait()
        for copy in copies:
            copy.wait()

    return pl.pallas_call(
        kernel,
        out_shape=jax.ShapeDtypeStruct(x.shape, x.dtype),
        in_specs=[pl.BlockSpec(memory_space=pl.ANY)],
        out_specs=pl.BlockSpec(memory_space=pl.ANY),
        scratch_shapes=[
            pltpu.SemaphoreType.DMA((n,)),
            pltpu.SemaphoreType.DMA((n,)),
            pltpu.SemaphoreType.DMA,
        ],
        compiler_params=pltpu.CompilerParams(collective_id=collective_id, has_side_effects=True),
    )(x)


def expert_reduce_scatter(x, collective_id, out_dtype, base):
    n, rows, cols = x.shape
    chips = n // 2
    mesh_ids = pl.DeviceIdType.MESH

    def kernel(x_ref, b_ref, o_ref, pair_buf, part, far_buf, send1, recv1, send2, recv2):
        me = lax.axis_index("expert")
        row = lax.axis_index("dp")
        chip, core = me // 2, me % 2
        sibling = chip * 2 + 1 - core
        barrier = pltpu.get_barrier_semaphore()
        pl.semaphore_signal(barrier, inc=1, device_id=(row, sibling), device_id_type=mesh_ids)
        for k in range(1, chips):
            pl.semaphore_signal(
                barrier,
                inc=1,
                device_id=(row, lax.rem(chip + k, chips) * 2 + core),
                device_id_type=mesh_ids,
            )
        pl.semaphore_wait(barrier, chips)
        first = pltpu.make_async_remote_copy(
            src_ref=x_ref.at[:, 1 - core],
            dst_ref=pair_buf,
            send_sem=send1,
            recv_sem=recv1,
            device_id=(row, sibling),
            device_id_type=mesh_ids,
        )
        first.start()
        first.wait()
        copies = []
        for k in range(1, chips):
            dest = lax.rem(chip + k, chips)
            part[k] = (
                x_ref[dest, core].astype(jnp.float32) + pair_buf[dest].astype(jnp.float32)
            ).astype(part.dtype)
            copy = pltpu.make_async_remote_copy(
                src_ref=part.at[k],
                dst_ref=far_buf.at[k],
                send_sem=send2.at[k],
                recv_sem=recv2.at[k],
                device_id=(row, dest * 2 + core),
                device_id_type=mesh_ids,
            )
            copy.start()
            copies.append(copy)
        acc = x_ref[chip, core].astype(jnp.float32) + pair_buf[chip].astype(jnp.float32)
        acc = acc + b_ref[...].astype(jnp.float32)
        for k, copy in enumerate(copies, 1):
            copy.wait()
            acc = acc + far_buf[k].astype(jnp.float32)
        o_ref[...] = acc.astype(o_ref.dtype)

    return pl.pallas_call(
        kernel,
        out_shape=jax.ShapeDtypeStruct((rows, cols), out_dtype),
        in_specs=[pl.BlockSpec(memory_space=pltpu.VMEM)] * 2,
        out_specs=pl.BlockSpec(memory_space=pltpu.VMEM),
        scratch_shapes=[
            pltpu.VMEM((chips, rows, cols), x.dtype),
            pltpu.VMEM((chips, rows, cols), x.dtype),
            pltpu.VMEM((chips, rows, cols), x.dtype),
            pltpu.SemaphoreType.DMA,
            pltpu.SemaphoreType.DMA,
            pltpu.SemaphoreType.DMA((chips,)),
            pltpu.SemaphoreType.DMA((chips,)),
        ],
        compiler_params=pltpu.CompilerParams(collective_id=collective_id, has_side_effects=True),
    )(x.reshape(chips, 2, rows, cols), base)


def expert_all_gather(x, collective_id):
    rows, cols = x.shape
    n = lax.axis_size("expert")
    chips = n // 2
    mesh_ids = pl.DeviceIdType.MESH

    def kernel(x_ref, o_ref, send0, recv0, send1, recv1, send2, recv2):
        me = lax.axis_index("expert")
        row = lax.axis_index("dp")
        chip, core = me // 2, me % 2
        sibling = chip * 2 + 1 - core
        barrier = pltpu.get_barrier_semaphore()
        pl.semaphore_signal(barrier, inc=1, device_id=(row, sibling), device_id_type=mesh_ids)
        for k in range(1, chips):
            pl.semaphore_signal(
                barrier,
                inc=1,
                device_id=(row, lax.rem(chip + k, chips) * 2 + core),
                device_id_type=mesh_ids,
            )
        pl.semaphore_wait(barrier, chips)
        near = pltpu.make_async_remote_copy(
            src_ref=x_ref,
            dst_ref=o_ref.at[me],
            send_sem=send0,
            recv_sem=recv0,
            device_id=(row, sibling),
            device_id_type=mesh_ids,
        )
        near.start()
        far = []
        for k in range(1, chips):
            copy = pltpu.make_async_remote_copy(
                src_ref=x_ref,
                dst_ref=o_ref.at[me],
                send_sem=send1.at[k],
                recv_sem=recv1.at[k],
                device_id=(row, lax.rem(chip + k, chips) * 2 + core),
                device_id_type=mesh_ids,
            )
            copy.start()
            far.append(copy)
        o_ref[me] = x_ref[...]
        passed = []
        for k, copy in enumerate(far, 1):
            copy.wait_recv()
            source = lax.rem(chip - k + chips, chips) * 2 + core
            relay = pltpu.make_async_remote_copy(
                src_ref=o_ref.at[source],
                dst_ref=o_ref.at[source],
                send_sem=send2.at[k],
                recv_sem=recv2.at[k],
                device_id=(row, sibling),
                device_id_type=mesh_ids,
            )
            relay.start()
            passed.append(relay)
        near.wait()
        for copy in far:
            copy.wait_send()
        for relay in passed:
            relay.wait()

    return pl.pallas_call(
        kernel,
        out_shape=jax.ShapeDtypeStruct((n, rows, cols), x.dtype),
        in_specs=[pl.BlockSpec(memory_space=pltpu.VMEM)],
        out_specs=pl.BlockSpec(memory_space=pltpu.VMEM),
        scratch_shapes=[
            pltpu.SemaphoreType.DMA,
            pltpu.SemaphoreType.DMA,
            pltpu.SemaphoreType.DMA((chips,)),
            pltpu.SemaphoreType.DMA((chips,)),
            pltpu.SemaphoreType.DMA((chips,)),
            pltpu.SemaphoreType.DMA((chips,)),
        ],
        compiler_params=pltpu.CompilerParams(collective_id=collective_id, has_side_effects=True),
    )(x)


def fused_projector(feats, proj_in, proj_out, collective_id):
    rows, width_vis = feats.shape
    n = lax.axis_size("expert")
    chips = n // 2
    width_model = proj_out.shape[1]
    mesh_ids = pl.DeviceIdType.MESH
    f32, bf16 = jnp.float32, jnp.bfloat16

    def kernel(
        f_ref, wi_ref, wo_ref, o_ref, fbuf, psend, pbuf,
        send_n, recv_n, send_f, recv_f, send_r, recv_r, send_p, recv_p,
    ):
        me = lax.axis_index("expert")
        row = lax.axis_index("dp")
        chip, core = me // 2, me % 2
        sibling = chip * 2 + 1 - core
        barrier = pltpu.get_barrier_semaphore()
        for k in range(1, n):
            pl.semaphore_signal(
                barrier, inc=1, device_id=(row, lax.rem(me + k, n)), device_id_type=mesh_ids
            )
        pl.semaphore_wait(barrier, n - 1)
        near = pltpu.make_async_remote_copy(
            src_ref=f_ref,
            dst_ref=fbuf.at[me],
            send_sem=send_n,
            recv_sem=recv_n,
            device_id=(row, sibling),
            device_id_type=mesh_ids,
        )
        near.start()
        far = []
        for k in range(1, chips):
            copy = pltpu.make_async_remote_copy(
                src_ref=f_ref,
                dst_ref=fbuf.at[me],
                send_sem=send_f.at[k],
                recv_sem=recv_f.at[k],
                device_id=(row, lax.rem(chip + k, chips) * 2 + core),
                device_id_type=mesh_ids,
            )
            copy.start()
            far.append(copy)

        def partial(x):
            hidden = jnp.dot(x, wi_ref[...], preferred_element_type=f32)
            hidden = jax.nn.gelu(hidden, approximate=True).astype(bf16)
            return jnp.dot(hidden, wo_ref[...], preferred_element_type=f32)

        backs = []

        def answer(index, source):
            psend[index] = partial(fbuf[source]).astype(bf16)
            back = pltpu.make_async_remote_copy(
                src_ref=psend.at[index],
                dst_ref=pbuf.at[index],
                send_sem=send_p.at[index],
                recv_sem=recv_p.at[index],
                device_id=(row, source),
                device_id_type=mesh_ids,
            )
            back.start()
            backs.append(back)

        acc = partial(f_ref[...])
        near.wait_recv()
        answer(0, sibling)
        relays = []
        for k, copy in enumerate(far, 1):
            copy.wait_recv()
            source = lax.rem(chip - k + chips, chips) * 2 + core
            relay = pltpu.make_async_remote_copy(
                src_ref=fbuf.at[source],
                dst_ref=fbuf.at[source],
                send_sem=send_r.at[k],
                recv_sem=recv_r.at[k],
                device_id=(row, sibling),
                device_id_type=mesh_ids,
            )
            relay.start()
            relays.append(relay)
            answer(k, source)
        for k, relay in enumerate(relays, 1):
            relay.wait_recv()
            answer(chips - 1 + k, lax.rem(chip - k + chips, chips) * 2 + 1 - core)
        for index, back in enumerate(backs):
            back.wait_recv()
            acc = acc + pbuf[index].astype(f32)
        o_ref[...] = acc.astype(o_ref.dtype)
        near.wait_send()
        for copy in far:
            copy.wait_send()
        for relay in relays:
            relay.wait_send()
        for back in backs:
            back.wait_send()

    return pl.pallas_call(
        kernel,
        out_shape=jax.ShapeDtypeStruct((rows, width_model), bf16),
        in_specs=[pl.BlockSpec(memory_space=pltpu.VMEM)] * 3,
        out_specs=pl.BlockSpec(memory_space=pltpu.VMEM),
        scratch_shapes=[
            pltpu.VMEM((n, rows, width_vis), feats.dtype),
            pltpu.VMEM((n, rows, width_model), bf16),
            pltpu.VMEM((n, rows, width_model), bf16),
            pltpu.SemaphoreType.DMA,
            pltpu.SemaphoreType.DMA,
            pltpu.SemaphoreType.DMA((chips,)),
            pltpu.SemaphoreType.DMA((chips,)),
            pltpu.SemaphoreType.DMA((chips,)),
            pltpu.SemaphoreType.DMA((chips,)),
            pltpu.SemaphoreType.DMA((n,)),
            pltpu.SemaphoreType.DMA((n,)),
        ],
        compiler_params=pltpu.CompilerParams(
            collective_id=collective_id, has_side_effects=True, vmem_limit_bytes=48 * 1024 * 1024
        ),
    )(feats, proj_in, proj_out)


def normalize(rows, norm_gain):
    rows_f = rows.astype(jnp.float32)
    meansq = jnp.mean(rows_f * rows_f, axis=-1, keepdims=True) + 1e-06
    return (rows_f * lax.rsqrt(meansq) * norm_gain).astype(jnp.bfloat16)


def select_dot(sel, rows):
    return jnp.dot(sel, rows, preferred_element_type=jnp.float32)


def shards(
    text_embed,
    image_feats,
    tile_pos,
    proj_in,
    proj_out,
    norm_gain,
    shared_gate,
    shared_up,
    shared_down,
    expert_gate,
    expert_up,
    expert_down,
    route_ids,
    route_wts,
):
    bf16, f32 = jnp.bfloat16, jnp.float32
    tok_dev, width_model = text_embed.shape
    img_dev, width_vis = image_feats.shape
    n_data = lax.axis_size("dp")
    n_group = lax.axis_size("expert")
    peer = img_dev // n_data
    my_place = lax.axis_index("expert")

    route_cols = jnp.concatenate([route_ids, route_wts // 256, route_wts % 256], axis=1)
    route_cols = jnp.pad(route_cols, ((0, 0), (0, 128 - route_cols.shape[1])))

    dest_index = tile_pos // tok_dev // n_group
    img_iota = jnp.arange(img_dev, dtype=jnp.int32)
    same_before = (dest_index[None, :] == dest_index[:, None]) & (img_iota[None, :] < img_iota[:, None])
    send_slot = dest_index * peer + jnp.sum(same_before.astype(jnp.int32), axis=1)
    reorder = (send_slot[None, :] == img_iota[:, None]).astype(bf16)
    pad = 128
    unordered = jnp.concatenate(
        [image_feats, jnp.broadcast_to((tile_pos % tok_dev).astype(bf16)[:, None], (img_dev, pad))],
        axis=1,
    )
    packed = select_dot(reorder, unordered).astype(bf16).reshape(n_data, peer, width_vis + pad)
    moved = lax.all_to_all(packed, "dp", split_axis=0, concat_axis=0, tiled=True)
    moved = moved.reshape(img_dev, width_vis + pad)
    moved_feats = moved[:, :width_vis]
    moved_offs = moved[:, width_vis].astype(jnp.int32)

    projected = fused_projector(moved_feats, proj_in, proj_out, 5)

    place = (
        moved_offs[None, :] == jnp.arange(tok_dev, dtype=jnp.int32)[:, None]
    ).astype(bf16)
    placed = select_dot(place, projected)
    has_image = jnp.sum(place.astype(f32), axis=1, keepdims=True) > 0
    embed_own = jnp.where(has_image, placed, text_embed.astype(f32))
    normed_own = normalize(embed_own, norm_gain)

    gathered = expert_all_gather(
        jnp.concatenate([normed_own, route_cols.astype(bf16)], axis=1), 6
    ).reshape(n_group * tok_dev, width_model + route_cols.shape[1])
    normed = gathered[:, :width_model]
    routes = gathered[:, width_model:].astype(f32)
    top_count = route_ids.shape[1]
    ids = routes[:, :top_count].astype(jnp.int32)
    weights_f = routes[:, top_count : 2 * top_count] * 256.0 + routes[:, 2 * top_count : 3 * top_count]

    gate_s = jnp.dot(normed, shared_gate, preferred_element_type=f32)
    up_s = jnp.dot(normed, shared_up, preferred_element_type=f32)
    shared_hidden = (jax.nn.silu(gate_s) * up_s).astype(bf16)

    group_rows = normed.shape[0]
    n_pairs = group_rows * top_count
    capacity = 3 * group_rows * top_count // (2 * n_data)
    share = capacity // n_group
    flat_ids = ids.reshape(-1)
    onehot = (flat_ids[:, None] == jnp.arange(n_data, dtype=jnp.int32)[None, :]).astype(bf16)
    pair_iota = jnp.arange(n_pairs, dtype=jnp.int32)
    earlier = (pair_iota[None, :] < pair_iota[:, None]).astype(bf16)
    counts = select_dot(earlier, onehot)
    rank = jnp.sum(counts * onehot.astype(f32), axis=1).astype(jnp.int32)

    inside = rank // share == my_place
    row_of = jnp.where(inside, flat_ids * share + rank - my_place * share, -1)
    n_rows = n_data * share
    hit = (
        row_of.reshape(group_rows, top_count)[:, :, None]
        == jnp.arange(n_rows, dtype=jnp.int32)[None, None, :]
    )
    pick = jnp.sum(hit.astype(f32), axis=1).astype(bf16)
    lanes = 128
    block = (n_data, share * width_model // lanes, lanes)
    send = select_dot(pick.T, normed).astype(bf16).reshape(block)
    arrived = lax.all_to_all(send, "dp", split_axis=0, concat_axis=0, tiled=True)
    slots = lax.all_gather(arrived.reshape(n_rows, width_model), "expert", axis=0, tiled=True)

    width_e = expert_gate.shape[2]
    gate_up = jnp.dot(
        slots, jnp.concatenate([expert_gate[0], expert_up[0]], axis=1), preferred_element_type=f32
    )
    gate_e, up_e = gate_up[:, :width_e], gate_up[:, width_e:]
    hidden_e = (jax.nn.silu(gate_e) * up_e).astype(bf16)
    partial_out = jnp.dot(hidden_e, expert_down[0], preferred_element_type=f32).astype(bf16)
    summed = lax.psum_scatter(partial_out, "expert", scatter_dimension=0, tiled=True)
    returned = lax.all_to_all(
        summed.reshape(block), "dp", split_axis=0, concat_axis=0, tiled=True
    ).reshape(n_rows, width_model)

    weights_n = weights_f / jnp.sum(weights_f, axis=1, keepdims=True)
    coef = jnp.sum(jnp.where(hit, weights_n[:, :, None], 0.0), axis=1)
    coef_hi = coef.astype(bf16)
    coef_lo = (coef - coef_hi.astype(f32)).astype(bf16)
    terms = jnp.dot(
        jnp.concatenate([shared_hidden, coef_hi, coef_lo], axis=1),
        jnp.concatenate([shared_down, returned, returned], axis=0),
        preferred_element_type=f32,
    )
    return expert_reduce_scatter(
        terms.astype(bf16).reshape(n_group, tok_dev, width_model),
        4,
        bf16,
        embed_own.astype(bf16),
    )


def solution(mesh):
    return jax.shard_map(
        shards,
        mesh=mesh,
        in_specs=(
            P(("dp", "expert"), None),
            P(("dp", "expert"), None),
            P(("dp", "expert")),
            P(None, "expert"),
            P("expert", None),
            P(),
            P(None, "expert"),
            P(None, "expert"),
            P("expert", None),
            P("dp", None, "expert"),
            P("dp", None, "expert"),
            P("dp", "expert", None),
            P(("dp", "expert"), None),
            P(("dp", "expert"), None),
        ),
        out_specs=P(("dp", "expert"), None),
        check_vma=False,
    )
```

```python
import jax
import jax.numpy as jnp
from jax import lax
from jax.experimental import pallas as pl
from jax.experimental.pallas import tpu as pltpu
from jax.sharding import PartitionSpec as P


def dp_all_to_all(x, collective_id):
    n = x.shape[0]
    mesh_ids = pl.DeviceIdType.MESH

    def kernel(x_ref, y_ref, send_sem, recv_sem, local_sem):
        me = lax.axis_index("dp")
        j = lax.axis_index("expert")
        barrier = pltpu.get_barrier_semaphore()
        for k in range(1, n):
            pl.semaphore_signal(
                barrier, inc=1, device_id=(lax.rem(me + k, n), j), device_id_type=mesh_ids
            )
        pl.semaphore_wait(barrier, n - 1)
        local = pltpu.make_async_copy(x_ref.at[me], y_ref.at[me], local_sem)
        local.start()
        copies = []
        for k in range(1, n):
            peer = lax.rem(me + k, n)
            copy = pltpu.make_async_remote_copy(
                src_ref=x_ref.at[peer],
                dst_ref=y_ref.at[me],
                send_sem=send_sem.at[k],
                recv_sem=recv_sem.at[k],
                device_id=(peer, j),
                device_id_type=mesh_ids,
            )
            copy.start()
            copies.append(copy)
        local.wait()
        for copy in copies:
            copy.wait()

    return pl.pallas_call(
        kernel,
        out_shape=jax.ShapeDtypeStruct(x.shape, x.dtype),
        in_specs=[pl.BlockSpec(memory_space=pl.ANY)],
        out_specs=pl.BlockSpec(memory_space=pl.ANY),
        scratch_shapes=[
            pltpu.SemaphoreType.DMA((n,)),
            pltpu.SemaphoreType.DMA((n,)),
            pltpu.SemaphoreType.DMA,
        ],
        compiler_params=pltpu.CompilerParams(collective_id=collective_id, has_side_effects=True),
    )(x)


def expert_reduce_scatter(x, collective_id, out_dtype, base):
    n, rows, cols = x.shape
    chips = n // 2
    mesh_ids = pl.DeviceIdType.MESH

    def kernel(x_ref, b_ref, o_ref, pair_buf, part, far_buf, send1, recv1, send2, recv2):
        me = lax.axis_index("expert")
        row = lax.axis_index("dp")
        chip, core = me // 2, me % 2
        sibling = chip * 2 + 1 - core
        barrier = pltpu.get_barrier_semaphore()
        pl.semaphore_signal(barrier, inc=1, device_id=(row, sibling), device_id_type=mesh_ids)
        for k in range(1, chips):
            pl.semaphore_signal(
                barrier,
                inc=1,
                device_id=(row, lax.rem(chip + k, chips) * 2 + core),
                device_id_type=mesh_ids,
            )
        pl.semaphore_wait(barrier, chips)
        first = pltpu.make_async_remote_copy(
            src_ref=x_ref.at[:, 1 - core],
            dst_ref=pair_buf,
            send_sem=send1,
            recv_sem=recv1,
            device_id=(row, sibling),
            device_id_type=mesh_ids,
        )
        first.start()
        first.wait()
        copies = []
        for k in range(1, chips):
            dest = lax.rem(chip + k, chips)
            part[k] = (
                x_ref[dest, core].astype(jnp.float32) + pair_buf[dest].astype(jnp.float32)
            ).astype(part.dtype)
            copy = pltpu.make_async_remote_copy(
                src_ref=part.at[k],
                dst_ref=far_buf.at[k],
                send_sem=send2.at[k],
                recv_sem=recv2.at[k],
                device_id=(row, dest * 2 + core),
                device_id_type=mesh_ids,
            )
            copy.start()
            copies.append(copy)
        acc = x_ref[chip, core].astype(jnp.float32) + pair_buf[chip].astype(jnp.float32)
        acc = acc + b_ref[...].astype(jnp.float32)
        for k, copy in enumerate(copies, 1):
            copy.wait()
            acc = acc + far_buf[k].astype(jnp.float32)
        o_ref[...] = acc.astype(o_ref.dtype)

    return pl.pallas_call(
        kernel,
        out_shape=jax.ShapeDtypeStruct((rows, cols), out_dtype),
        in_specs=[pl.BlockSpec(memory_space=pltpu.VMEM)] * 2,
        out_specs=pl.BlockSpec(memory_space=pltpu.VMEM),
        scratch_shapes=[
            pltpu.VMEM((chips, rows, cols), x.dtype),
            pltpu.VMEM((chips, rows, cols), x.dtype),
            pltpu.VMEM((chips, rows, cols), x.dtype),
            pltpu.SemaphoreType.DMA,
            pltpu.SemaphoreType.DMA,
            pltpu.SemaphoreType.DMA((chips,)),
            pltpu.SemaphoreType.DMA((chips,)),
        ],
        compiler_params=pltpu.CompilerParams(collective_id=collective_id, has_side_effects=True),
    )(x.reshape(chips, 2, rows, cols), base)


def expert_all_gather(x, collective_id):
    rows, cols = x.shape
    n = lax.axis_size("expert")
    chips = n // 2
    mesh_ids = pl.DeviceIdType.MESH

    def kernel(x_ref, o_ref, send0, recv0, send1, recv1, send2, recv2):
        me = lax.axis_index("expert")
        row = lax.axis_index("dp")
        chip, core = me // 2, me % 2
        sibling = chip * 2 + 1 - core
        barrier = pltpu.get_barrier_semaphore()
        pl.semaphore_signal(barrier, inc=1, device_id=(row, sibling), device_id_type=mesh_ids)
        for k in range(1, chips):
            pl.semaphore_signal(
                barrier,
                inc=1,
                device_id=(row, lax.rem(chip + k, chips) * 2 + core),
                device_id_type=mesh_ids,
            )
        pl.semaphore_wait(barrier, chips)
        near = pltpu.make_async_remote_copy(
            src_ref=x_ref,
            dst_ref=o_ref.at[me],
            send_sem=send0,
            recv_sem=recv0,
            device_id=(row, sibling),
            device_id_type=mesh_ids,
        )
        near.start()
        far = []
        for k in range(1, chips):
            copy = pltpu.make_async_remote_copy(
                src_ref=x_ref,
                dst_ref=o_ref.at[me],
                send_sem=send1.at[k],
                recv_sem=recv1.at[k],
                device_id=(row, lax.rem(chip + k, chips) * 2 + core),
                device_id_type=mesh_ids,
            )
            copy.start()
            far.append(copy)
        o_ref[me] = x_ref[...]
        passed = []
        for k, copy in enumerate(far, 1):
            copy.wait_recv()
            source = lax.rem(chip - k + chips, chips) * 2 + core
            relay = pltpu.make_async_remote_copy(
                src_ref=o_ref.at[source],
                dst_ref=o_ref.at[source],
                send_sem=send2.at[k],
                recv_sem=recv2.at[k],
                device_id=(row, sibling),
                device_id_type=mesh_ids,
            )
            relay.start()
            passed.append(relay)
        near.wait()
        for copy in far:
            copy.wait_send()
        for relay in passed:
            relay.wait()

    return pl.pallas_call(
        kernel,
        out_shape=jax.ShapeDtypeStruct((n, rows, cols), x.dtype),
        in_specs=[pl.BlockSpec(memory_space=pltpu.VMEM)],
        out_specs=pl.BlockSpec(memory_space=pltpu.VMEM),
        scratch_shapes=[
            pltpu.SemaphoreType.DMA,
            pltpu.SemaphoreType.DMA,
            pltpu.SemaphoreType.DMA((chips,)),
            pltpu.SemaphoreType.DMA((chips,)),
            pltpu.SemaphoreType.DMA((chips,)),
            pltpu.SemaphoreType.DMA((chips,)),
        ],
        compiler_params=pltpu.CompilerParams(collective_id=collective_id, has_side_effects=True),
    )(x)


def fused_projector(feats, proj_in, proj_out, collective_id):
    rows, width_vis = feats.shape
    n = lax.axis_size("expert")
    chips = n // 2
    width_model = proj_out.shape[1]
    mesh_ids = pl.DeviceIdType.MESH
    f32, bf16 = jnp.float32, jnp.bfloat16

    def kernel(
        f_ref, wi_ref, wo_ref, o_ref, fbuf, psend, pbuf,
        send_n, recv_n, send_f, recv_f, send_r, recv_r, send_p, recv_p,
    ):
        me = lax.axis_index("expert")
        row = lax.axis_index("dp")
        chip, core = me // 2, me % 2
        sibling = chip * 2 + 1 - core
        barrier = pltpu.get_barrier_semaphore()
        for k in range(1, n):
            pl.semaphore_signal(
                barrier, inc=1, device_id=(row, lax.rem(me + k, n)), device_id_type=mesh_ids
            )
        pl.semaphore_wait(barrier, n - 1)
        near = pltpu.make_async_remote_copy(
            src_ref=f_ref,
            dst_ref=fbuf.at[me],
            send_sem=send_n,
            recv_sem=recv_n,
            device_id=(row, sibling),
            device_id_type=mesh_ids,
        )
        near.start()
        far = []
        for k in range(1, chips):
            copy = pltpu.make_async_remote_copy(
                src_ref=f_ref,
                dst_ref=fbuf.at[me],
                send_sem=send_f.at[k],
                recv_sem=recv_f.at[k],
                device_id=(row, lax.rem(chip + k, chips) * 2 + core),
                device_id_type=mesh_ids,
            )
            copy.start()
            far.append(copy)

        def partial(x):
            hidden = jnp.dot(x, wi_ref[...], preferred_element_type=f32)
            hidden = jax.nn.gelu(hidden, approximate=True).astype(bf16)
            return jnp.dot(hidden, wo_ref[...], preferred_element_type=f32)

        backs = []

        def answer(index, source):
            psend[index] = partial(fbuf[source]).astype(bf16)
            back = pltpu.make_async_remote_copy(
                src_ref=psend.at[index],
                dst_ref=pbuf.at[index],
                send_sem=send_p.at[index],
                recv_sem=recv_p.at[index],
                device_id=(row, source),
                device_id_type=mesh_ids,
            )
            back.start()
            backs.append(back)

        acc = partial(f_ref[...])
        near.wait_recv()
        answer(0, sibling)
        relays = []
        for k, copy in enumerate(far, 1):
            copy.wait_recv()
            source = lax.rem(chip - k + chips, chips) * 2 + core
            relay = pltpu.make_async_remote_copy(
                src_ref=fbuf.at[source],
                dst_ref=fbuf.at[source],
                send_sem=send_r.at[k],
                recv_sem=recv_r.at[k],
                device_id=(row, sibling),
                device_id_type=mesh_ids,
            )
            relay.start()
            relays.append(relay)
            answer(k, source)
        for k, relay in enumerate(relays, 1):
            relay.wait_recv()
            answer(chips - 1 + k, lax.rem(chip - k + chips, chips) * 2 + 1 - core)
        for index, back in enumerate(backs):
            back.wait_recv()
            acc = acc + pbuf[index].astype(f32)
        o_ref[...] = acc.astype(o_ref.dtype)
        near.wait_send()
        for copy in far:
            copy.wait_send()
        for relay in relays:
            relay.wait_send()
        for back in backs:
            back.wait_send()

    return pl.pallas_call(
        kernel,
        out_shape=jax.ShapeDtypeStruct((rows, width_model), bf16),
        in_specs=[pl.BlockSpec(memory_space=pltpu.VMEM)] * 3,
        out_specs=pl.BlockSpec(memory_space=pltpu.VMEM),
        scratch_shapes=[
            pltpu.VMEM((n, rows, width_vis), feats.dtype),
            pltpu.VMEM((n, rows, width_model), bf16),
            pltpu.VMEM((n, rows, width_model), bf16),
            pltpu.SemaphoreType.DMA,
            pltpu.SemaphoreType.DMA,
            pltpu.SemaphoreType.DMA((chips,)),
            pltpu.SemaphoreType.DMA((chips,)),
            pltpu.SemaphoreType.DMA((chips,)),
            pltpu.SemaphoreType.DMA((chips,)),
            pltpu.SemaphoreType.DMA((n,)),
            pltpu.SemaphoreType.DMA((n,)),
        ],
        compiler_params=pltpu.CompilerParams(
            collective_id=collective_id, has_side_effects=True, vmem_limit_bytes=48 * 1024 * 1024
        ),
    )(feats, proj_in, proj_out)


def normalize(rows, norm_gain):
    rows_f = rows.astype(jnp.float32)
    meansq = jnp.mean(rows_f * rows_f, axis=-1, keepdims=True) + 1e-06
    return (rows_f * lax.rsqrt(meansq) * norm_gain).astype(jnp.bfloat16)


def select_dot(sel, rows):
    return jnp.dot(sel, rows, preferred_element_type=jnp.float32)


def shards(
    text_embed,
    image_feats,
    tile_pos,
    proj_in,
    proj_out,
    norm_gain,
    shared_gate,
    shared_up,
    shared_down,
    expert_gate,
    expert_up,
    expert_down,
    route_ids,
    route_wts,
):
    bf16, f32 = jnp.bfloat16, jnp.float32
    tok_dev, width_model = text_embed.shape
    img_dev, width_vis = image_feats.shape
    n_data = lax.axis_size("dp")
    n_group = lax.axis_size("expert")
    peer = img_dev // n_data
    my_place = lax.axis_index("expert")

    route_cols = jnp.concatenate([route_ids, route_wts // 256, route_wts % 256], axis=1)
    route_cols = jnp.pad(route_cols, ((0, 0), (0, 128 - route_cols.shape[1])))

    dest_index = tile_pos // tok_dev // n_group
    img_iota = jnp.arange(img_dev, dtype=jnp.int32)
    same_before = (dest_index[None, :] == dest_index[:, None]) & (img_iota[None, :] < img_iota[:, None])
    send_slot = dest_index * peer + jnp.sum(same_before.astype(jnp.int32), axis=1)
    reorder = (send_slot[None, :] == img_iota[:, None]).astype(bf16)
    pad = 128
    unordered = jnp.concatenate(
        [image_feats, jnp.broadcast_to((tile_pos % tok_dev).astype(bf16)[:, None], (img_dev, pad))],
        axis=1,
    )
    packed = select_dot(reorder, unordered).astype(bf16).reshape(n_data, peer, width_vis + pad)
    moved = lax.all_to_all(packed, "dp", split_axis=0, concat_axis=0, tiled=True)
    moved = moved.reshape(img_dev, width_vis + pad)
    moved_feats = moved[:, :width_vis]
    moved_offs = moved[:, width_vis].astype(jnp.int32)

    projected = fused_projector(moved_feats, proj_in, proj_out, 5)

    place = (
        moved_offs[None, :] == jnp.arange(tok_dev, dtype=jnp.int32)[:, None]
    ).astype(bf16)
    placed = select_dot(place, projected)
    has_image = jnp.sum(place.astype(f32), axis=1, keepdims=True) > 0
    embed_own = jnp.where(has_image, placed, text_embed.astype(f32))
    normed_own = normalize(embed_own, norm_gain)

    gathered = expert_all_gather(
        jnp.concatenate([normed_own, route_cols.astype(bf16)], axis=1), 6
    ).reshape(n_group * tok_dev, width_model + route_cols.shape[1])
    normed = gathered[:, :width_model]
    routes = gathered[:, width_model:].astype(f32)
    top_count = route_ids.shape[1]
    ids = routes[:, :top_count].astype(jnp.int32)
    weights_f = routes[:, top_count : 2 * top_count] * 256.0 + routes[:, 2 * top_count : 3 * top_count]


    group_rows = normed.shape[0]
    n_pairs = group_rows * top_count
    capacity = 3 * group_rows * top_count // (2 * n_data)
    share = capacity // n_group
    flat_ids = ids.reshape(-1)
    onehot = (flat_ids[:, None] == jnp.arange(n_data, dtype=jnp.int32)[None, :]).astype(bf16)
    pair_iota = jnp.arange(n_pairs, dtype=jnp.int32)
    earlier = (pair_iota[None, :] < pair_iota[:, None]).astype(bf16)
    counts = select_dot(earlier, onehot)
    rank = jnp.sum(counts * onehot.astype(f32), axis=1).astype(jnp.int32)

    inside = rank // share == my_place
    row_of = jnp.where(inside, flat_ids * share + rank - my_place * share, -1)
    n_rows = n_data * share
    hit = (
        row_of.reshape(group_rows, top_count)[:, :, None]
        == jnp.arange(n_rows, dtype=jnp.int32)[None, None, :]
    )
    pick = jnp.sum(hit.astype(f32), axis=1).astype(bf16)
    lanes = 128
    block = (n_data, share * width_model // lanes, lanes)
    send = select_dot(pick.T, normed).astype(bf16).reshape(block)
    arrived = lax.all_to_all(send, "dp", split_axis=0, concat_axis=0, tiled=True)
    slots = lax.all_gather(arrived.reshape(n_rows, width_model), "expert", axis=0, tiled=True)

    width_e = expert_gate.shape[2]
    gate_up = jnp.dot(
        slots, jnp.concatenate([expert_gate[0], expert_up[0]], axis=1), preferred_element_type=f32
    )
    gate_e, up_e = gate_up[:, :width_e], gate_up[:, width_e:]
    hidden_e = (jax.nn.silu(gate_e) * up_e).astype(bf16)
    partial_out = jnp.dot(hidden_e, expert_down[0], preferred_element_type=f32).astype(bf16)
    summed = lax.psum_scatter(partial_out, "expert", scatter_dimension=0, tiled=True)
    summed, normed_late = lax.optimization_barrier((summed, normed))
    gate_s = jnp.dot(normed_late, shared_gate, preferred_element_type=f32)
    up_s = jnp.dot(normed_late, shared_up, preferred_element_type=f32)
    shared_hidden = (jax.nn.silu(gate_s) * up_s).astype(bf16)
    returned = lax.all_to_all(
        summed.reshape(block), "dp", split_axis=0, concat_axis=0, tiled=True
    ).reshape(n_rows, width_model)

    weights_n = weights_f / jnp.sum(weights_f, axis=1, keepdims=True)
    coef = jnp.sum(jnp.where(hit, weights_n[:, :, None], 0.0), axis=1)
    coef_hi = coef.astype(bf16)
    coef_lo = (coef - coef_hi.astype(f32)).astype(bf16)
    terms = jnp.dot(
        jnp.concatenate([shared_hidden, coef_hi, coef_lo], axis=1),
        jnp.concatenate([shared_down, returned, returned], axis=0),
        preferred_element_type=f32,
    )
    return expert_reduce_scatter(
        terms.astype(bf16).reshape(n_group, tok_dev, width_model),
        4,
        bf16,
        embed_own.astype(bf16),
    )


def solution(mesh):
    return jax.shard_map(
        shards,
        mesh=mesh,
        in_specs=(
            P(("dp", "expert"), None),
            P(("dp", "expert"), None),
            P(("dp", "expert")),
            P(None, "expert"),
            P("expert", None),
            P(),
            P(None, "expert"),
            P(None, "expert"),
            P("expert", None),
            P("dp", None, "expert"),
            P("dp", None, "expert"),
            P("dp", "expert", None),
            P(("dp", "expert"), None),
            P(("dp", "expert"), None),
        ),
        out_specs=P(("dp", "expert"), None),
        check_vma=False,
    )
```

```python
import jax
import jax.numpy as jnp
from jax import lax
from jax.experimental import pallas as pl
from jax.experimental.pallas import tpu as pltpu
from jax.sharding import PartitionSpec as P


def dp_all_to_all(x, collective_id):
    n = x.shape[0]
    mesh_ids = pl.DeviceIdType.MESH

    def kernel(x_ref, y_ref, send_sem, recv_sem, local_sem):
        me = lax.axis_index("dp")
        j = lax.axis_index("expert")
        barrier = pltpu.get_barrier_semaphore()
        for k in range(1, n):
            pl.semaphore_signal(
                barrier, inc=1, device_id=(lax.rem(me + k, n), j), device_id_type=mesh_ids
            )
        pl.semaphore_wait(barrier, n - 1)
        local = pltpu.make_async_copy(x_ref.at[me], y_ref.at[me], local_sem)
        local.start()
        copies = []
        for k in range(1, n):
            peer = lax.rem(me + k, n)
            copy = pltpu.make_async_remote_copy(
                src_ref=x_ref.at[peer],
                dst_ref=y_ref.at[me],
                send_sem=send_sem.at[k],
                recv_sem=recv_sem.at[k],
                device_id=(peer, j),
                device_id_type=mesh_ids,
            )
            copy.start()
            copies.append(copy)
        local.wait()
        for copy in copies:
            copy.wait()

    return pl.pallas_call(
        kernel,
        out_shape=jax.ShapeDtypeStruct(x.shape, x.dtype),
        in_specs=[pl.BlockSpec(memory_space=pl.ANY)],
        out_specs=pl.BlockSpec(memory_space=pl.ANY),
        scratch_shapes=[
            pltpu.SemaphoreType.DMA((n,)),
            pltpu.SemaphoreType.DMA((n,)),
            pltpu.SemaphoreType.DMA,
        ],
        compiler_params=pltpu.CompilerParams(collective_id=collective_id, has_side_effects=True),
    )(x)


def expert_reduce_scatter(x, collective_id, out_dtype, base):
    n, rows, cols = x.shape
    chips = n // 2
    mesh_ids = pl.DeviceIdType.MESH

    def kernel(x_ref, b_ref, o_ref, pair_buf, part, far_buf, send1, recv1, send2, recv2):
        me = lax.axis_index("expert")
        row = lax.axis_index("dp")
        chip, core = me // 2, me % 2
        sibling = chip * 2 + 1 - core
        barrier = pltpu.get_barrier_semaphore()
        pl.semaphore_signal(barrier, inc=1, device_id=(row, sibling), device_id_type=mesh_ids)
        for k in range(1, chips):
            pl.semaphore_signal(
                barrier,
                inc=1,
                device_id=(row, lax.rem(chip + k, chips) * 2 + core),
                device_id_type=mesh_ids,
            )
        pl.semaphore_wait(barrier, chips)
        first = pltpu.make_async_remote_copy(
            src_ref=x_ref.at[:, 1 - core],
            dst_ref=pair_buf,
            send_sem=send1,
            recv_sem=recv1,
            device_id=(row, sibling),
            device_id_type=mesh_ids,
        )
        first.start()
        first.wait()
        copies = []
        for k in range(1, chips):
            dest = lax.rem(chip + k, chips)
            part[k] = (
                x_ref[dest, core].astype(jnp.float32) + pair_buf[dest].astype(jnp.float32)
            ).astype(part.dtype)
            copy = pltpu.make_async_remote_copy(
                src_ref=part.at[k],
                dst_ref=far_buf.at[k],
                send_sem=send2.at[k],
                recv_sem=recv2.at[k],
                device_id=(row, dest * 2 + core),
                device_id_type=mesh_ids,
            )
            copy.start()
            copies.append(copy)
        acc = x_ref[chip, core].astype(jnp.float32) + pair_buf[chip].astype(jnp.float32)
        acc = acc + b_ref[...].astype(jnp.float32)
        for k, copy in enumerate(copies, 1):
            copy.wait()
            acc = acc + far_buf[k].astype(jnp.float32)
        o_ref[...] = acc.astype(o_ref.dtype)

    return pl.pallas_call(
        kernel,
        out_shape=jax.ShapeDtypeStruct((rows, cols), out_dtype),
        in_specs=[pl.BlockSpec(memory_space=pltpu.VMEM)] * 2,
        out_specs=pl.BlockSpec(memory_space=pltpu.VMEM),
        scratch_shapes=[
            pltpu.VMEM((chips, rows, cols), x.dtype),
            pltpu.VMEM((chips, rows, cols), x.dtype),
            pltpu.VMEM((chips, rows, cols), x.dtype),
            pltpu.SemaphoreType.DMA,
            pltpu.SemaphoreType.DMA,
            pltpu.SemaphoreType.DMA((chips,)),
            pltpu.SemaphoreType.DMA((chips,)),
        ],
        compiler_params=pltpu.CompilerParams(collective_id=collective_id, has_side_effects=True),
    )(x.reshape(chips, 2, rows, cols), base)


def expert_all_gather(x, collective_id):
    rows, cols = x.shape
    n = lax.axis_size("expert")
    chips = n // 2
    mesh_ids = pl.DeviceIdType.MESH

    def kernel(x_ref, o_ref, send0, recv0, send1, recv1, send2, recv2):
        me = lax.axis_index("expert")
        row = lax.axis_index("dp")
        chip, core = me // 2, me % 2
        sibling = chip * 2 + 1 - core
        barrier = pltpu.get_barrier_semaphore()
        pl.semaphore_signal(barrier, inc=1, device_id=(row, sibling), device_id_type=mesh_ids)
        for k in range(1, chips):
            pl.semaphore_signal(
                barrier,
                inc=1,
                device_id=(row, lax.rem(chip + k, chips) * 2 + core),
                device_id_type=mesh_ids,
            )
        pl.semaphore_wait(barrier, chips)
        near = pltpu.make_async_remote_copy(
            src_ref=x_ref,
            dst_ref=o_ref.at[me],
            send_sem=send0,
            recv_sem=recv0,
            device_id=(row, sibling),
            device_id_type=mesh_ids,
        )
        near.start()
        far = []
        for k in range(1, chips):
            copy = pltpu.make_async_remote_copy(
                src_ref=x_ref,
                dst_ref=o_ref.at[me],
                send_sem=send1.at[k],
                recv_sem=recv1.at[k],
                device_id=(row, lax.rem(chip + k, chips) * 2 + core),
                device_id_type=mesh_ids,
            )
            copy.start()
            far.append(copy)
        o_ref[me] = x_ref[...]
        passed = []
        for k, copy in enumerate(far, 1):
            copy.wait_recv()
            source = lax.rem(chip - k + chips, chips) * 2 + core
            relay = pltpu.make_async_remote_copy(
                src_ref=o_ref.at[source],
                dst_ref=o_ref.at[source],
                send_sem=send2.at[k],
                recv_sem=recv2.at[k],
                device_id=(row, sibling),
                device_id_type=mesh_ids,
            )
            relay.start()
            passed.append(relay)
        near.wait()
        for copy in far:
            copy.wait_send()
        for relay in passed:
            relay.wait()

    return pl.pallas_call(
        kernel,
        out_shape=jax.ShapeDtypeStruct((n, rows, cols), x.dtype),
        in_specs=[pl.BlockSpec(memory_space=pltpu.VMEM)],
        out_specs=pl.BlockSpec(memory_space=pltpu.VMEM),
        scratch_shapes=[
            pltpu.SemaphoreType.DMA,
            pltpu.SemaphoreType.DMA,
            pltpu.SemaphoreType.DMA((chips,)),
            pltpu.SemaphoreType.DMA((chips,)),
            pltpu.SemaphoreType.DMA((chips,)),
            pltpu.SemaphoreType.DMA((chips,)),
        ],
        compiler_params=pltpu.CompilerParams(collective_id=collective_id, has_side_effects=True),
    )(x)


def fused_projector(feats, proj_in, proj_out, collective_id):
    rows, width_vis = feats.shape
    n = lax.axis_size("expert")
    chips = n // 2
    width_model = proj_out.shape[1]
    mesh_ids = pl.DeviceIdType.MESH
    f32, bf16 = jnp.float32, jnp.bfloat16

    def kernel(
        f_ref, wi_ref, wo_ref, o_ref, fbuf, psend, pbuf,
        send_n, recv_n, send_f, recv_f, send_r, recv_r, send_p, recv_p,
    ):
        me = lax.axis_index("expert")
        row = lax.axis_index("dp")
        chip, core = me // 2, me % 2
        sibling = chip * 2 + 1 - core
        barrier = pltpu.get_barrier_semaphore()
        for k in range(1, n):
            pl.semaphore_signal(
                barrier, inc=1, device_id=(row, lax.rem(me + k, n)), device_id_type=mesh_ids
            )
        pl.semaphore_wait(barrier, n - 1)
        near = pltpu.make_async_remote_copy(
            src_ref=f_ref,
            dst_ref=fbuf.at[me],
            send_sem=send_n,
            recv_sem=recv_n,
            device_id=(row, sibling),
            device_id_type=mesh_ids,
        )
        near.start()
        far = []
        for k in range(1, chips):
            copy = pltpu.make_async_remote_copy(
                src_ref=f_ref,
                dst_ref=fbuf.at[me],
                send_sem=send_f.at[k],
                recv_sem=recv_f.at[k],
                device_id=(row, lax.rem(chip + k, chips) * 2 + core),
                device_id_type=mesh_ids,
            )
            copy.start()
            far.append(copy)

        def partial(x):
            hidden = jnp.dot(x, wi_ref[...], preferred_element_type=f32)
            hidden = jax.nn.gelu(hidden, approximate=True).astype(bf16)
            return jnp.dot(hidden, wo_ref[...], preferred_element_type=f32)

        backs = []

        def answer(index, source):
            psend[index] = partial(fbuf[source]).astype(bf16)
            back = pltpu.make_async_remote_copy(
                src_ref=psend.at[index],
                dst_ref=pbuf.at[index],
                send_sem=send_p.at[index],
                recv_sem=recv_p.at[index],
                device_id=(row, source),
                device_id_type=mesh_ids,
            )
            back.start()
            backs.append(back)

        acc = partial(f_ref[...])
        near.wait_recv()
        answer(0, sibling)
        relays = []
        for k, copy in enumerate(far, 1):
            copy.wait_recv()
            source = lax.rem(chip - k + chips, chips) * 2 + core
            relay = pltpu.make_async_remote_copy(
                src_ref=fbuf.at[source],
                dst_ref=fbuf.at[source],
                send_sem=send_r.at[k],
                recv_sem=recv_r.at[k],
                device_id=(row, sibling),
                device_id_type=mesh_ids,
            )
            relay.start()
            relays.append(relay)
            answer(k, source)
        for k, relay in enumerate(relays, 1):
            relay.wait_recv()
            answer(chips - 1 + k, lax.rem(chip - k + chips, chips) * 2 + 1 - core)
        for index, back in enumerate(backs):
            back.wait_recv()
            acc = acc + pbuf[index].astype(f32)
        o_ref[...] = acc.astype(o_ref.dtype)
        near.wait_send()
        for copy in far:
            copy.wait_send()
        for relay in relays:
            relay.wait_send()
        for back in backs:
            back.wait_send()

    return pl.pallas_call(
        kernel,
        out_shape=jax.ShapeDtypeStruct((rows, width_model), bf16),
        in_specs=[pl.BlockSpec(memory_space=pltpu.VMEM)] * 3,
        out_specs=pl.BlockSpec(memory_space=pltpu.VMEM),
        scratch_shapes=[
            pltpu.VMEM((n, rows, width_vis), feats.dtype),
            pltpu.VMEM((n, rows, width_model), bf16),
            pltpu.VMEM((n, rows, width_model), bf16),
            pltpu.SemaphoreType.DMA,
            pltpu.SemaphoreType.DMA,
            pltpu.SemaphoreType.DMA((chips,)),
            pltpu.SemaphoreType.DMA((chips,)),
            pltpu.SemaphoreType.DMA((chips,)),
            pltpu.SemaphoreType.DMA((chips,)),
            pltpu.SemaphoreType.DMA((n,)),
            pltpu.SemaphoreType.DMA((n,)),
        ],
        compiler_params=pltpu.CompilerParams(
            collective_id=collective_id, has_side_effects=True, vmem_limit_bytes=48 * 1024 * 1024
        ),
    )(feats, proj_in, proj_out)


def normalize(rows, norm_gain):
    rows_f = rows.astype(jnp.float32)
    meansq = jnp.mean(rows_f * rows_f, axis=-1, keepdims=True) + 1e-06
    return (rows_f * lax.rsqrt(meansq) * norm_gain).astype(jnp.bfloat16)


def select_dot(sel, rows):
    return jnp.dot(sel, rows, preferred_element_type=jnp.float32)


def shards(
    text_embed,
    image_feats,
    tile_pos,
    proj_in,
    proj_out,
    norm_gain,
    shared_gate,
    shared_up,
    shared_down,
    expert_gate,
    expert_up,
    expert_down,
    route_ids,
    route_wts,
):
    bf16, f32 = jnp.bfloat16, jnp.float32
    tok_dev, width_model = text_embed.shape
    img_dev, width_vis = image_feats.shape
    n_data = lax.axis_size("dp")
    n_group = lax.axis_size("expert")
    peer = img_dev // n_data
    my_place = lax.axis_index("expert")

    route_cols = jnp.concatenate([route_ids, route_wts // 256, route_wts % 256], axis=1)
    route_cols = jnp.pad(route_cols, ((0, 0), (0, 128 - route_cols.shape[1])))

    dest_index = tile_pos // tok_dev // n_group
    img_iota = jnp.arange(img_dev, dtype=jnp.int32)
    same_before = (dest_index[None, :] == dest_index[:, None]) & (img_iota[None, :] < img_iota[:, None])
    send_slot = dest_index * peer + jnp.sum(same_before.astype(jnp.int32), axis=1)
    reorder = (send_slot[None, :] == img_iota[:, None]).astype(bf16)
    pad = 128
    unordered = jnp.concatenate(
        [image_feats, jnp.broadcast_to((tile_pos % tok_dev).astype(bf16)[:, None], (img_dev, pad))],
        axis=1,
    )
    packed = select_dot(reorder, unordered).astype(bf16).reshape(n_data, peer, width_vis + pad)
    moved = lax.all_to_all(packed, "dp", split_axis=0, concat_axis=0, tiled=True)
    moved = moved.reshape(img_dev, width_vis + pad)
    moved_feats = moved[:, :width_vis]
    moved_offs = moved[:, width_vis].astype(jnp.int32)

    projected = fused_projector(moved_feats, proj_in, proj_out, 5)

    place = (
        moved_offs[None, :] == jnp.arange(tok_dev, dtype=jnp.int32)[:, None]
    ).astype(bf16)
    placed = select_dot(place, projected)
    has_image = jnp.sum(place.astype(f32), axis=1, keepdims=True) > 0
    embed_own = jnp.where(has_image, placed, text_embed.astype(f32))
    normed_own = normalize(embed_own, norm_gain)

    gathered = expert_all_gather(
        jnp.concatenate([normed_own, route_cols.astype(bf16)], axis=1), 6
    ).reshape(n_group * tok_dev, width_model + route_cols.shape[1])
    normed = gathered[:, :width_model]
    routes = gathered[:, width_model:].astype(f32)
    top_count = route_ids.shape[1]
    ids = routes[:, :top_count].astype(jnp.int32)
    weights_f = routes[:, top_count : 2 * top_count] * 256.0 + routes[:, 2 * top_count : 3 * top_count]


    group_rows = normed.shape[0]
    n_pairs = group_rows * top_count
    capacity = 3 * group_rows * top_count // (2 * n_data)
    share = capacity // n_group
    flat_ids = ids.reshape(-1)
    onehot = (flat_ids[:, None] == jnp.arange(n_data, dtype=jnp.int32)[None, :]).astype(bf16)
    pair_iota = jnp.arange(n_pairs, dtype=jnp.int32)
    earlier = (pair_iota[None, :] < pair_iota[:, None]).astype(bf16)
    counts = select_dot(earlier, onehot)
    rank = jnp.sum(counts * onehot.astype(f32), axis=1).astype(jnp.int32)

    inside = rank // share == my_place
    row_of = jnp.where(inside, flat_ids * share + rank - my_place * share, -1)
    n_rows = n_data * share
    hit = (
        row_of.reshape(group_rows, top_count)[:, :, None]
        == jnp.arange(n_rows, dtype=jnp.int32)[None, None, :]
    )
    pick = jnp.sum(hit.astype(f32), axis=1).astype(bf16)
    lanes = 128
    block = (n_data, share * width_model // lanes, lanes)
    send = select_dot(pick.T, normed).astype(bf16).reshape(block)
    arrived = lax.all_to_all(send, "dp", split_axis=0, concat_axis=0, tiled=True)
    slots = lax.all_gather(arrived.reshape(n_rows, width_model), "expert", axis=0, tiled=True)

    width_e = expert_gate.shape[2]
    gate_up = jnp.dot(
        slots, jnp.concatenate([expert_gate[0], expert_up[0]], axis=1), preferred_element_type=f32
    )
    gate_e, up_e = gate_up[:, :width_e], gate_up[:, width_e:]
    hidden_e = (jax.nn.silu(gate_e) * up_e).astype(bf16)
    partial_out = jnp.dot(hidden_e, expert_down[0], preferred_element_type=f32).astype(bf16)
    summed = lax.psum_scatter(partial_out, "expert", scatter_dimension=0, tiled=True)
    summed, normed_late = lax.optimization_barrier((summed, normed))
    gate_s = jnp.dot(normed_late, shared_gate, preferred_element_type=f32)
    up_s = jnp.dot(normed_late, shared_up, preferred_element_type=f32)
    shared_hidden = (jax.nn.silu(gate_s) * up_s).astype(bf16)
    returned = lax.all_to_all(
        summed.reshape(block), "dp", split_axis=0, concat_axis=0, tiled=True
    ).reshape(n_rows, width_model)

    weights_n = weights_f / jnp.sum(weights_f, axis=1, keepdims=True)
    coef = jnp.sum(jnp.where(hit, weights_n[:, :, None], 0.0), axis=1)
    coef_hi = coef.astype(bf16)
    coef_lo = (coef - coef_hi.astype(f32)).astype(bf16)
    terms = jnp.dot(shared_hidden, shared_down, preferred_element_type=f32) + jnp.dot(
        jnp.concatenate([coef_hi, coef_lo], axis=1),
        jnp.concatenate([returned, returned], axis=0),
        preferred_element_type=f32,
    )
    return expert_reduce_scatter(
        terms.astype(bf16).reshape(n_group, tok_dev, width_model),
        4,
        bf16,
        embed_own.astype(bf16),
    )


def solution(mesh):
    return jax.shard_map(
        shards,
        mesh=mesh,
        in_specs=(
            P(("dp", "expert"), None),
            P(("dp", "expert"), None),
            P(("dp", "expert")),
            P(None, "expert"),
            P("expert", None),
            P(),
            P(None, "expert"),
            P(None, "expert"),
            P("expert", None),
            P("dp", None, "expert"),
            P("dp", None, "expert"),
            P("dp", "expert", None),
            P(("dp", "expert"), None),
            P(("dp", "expert"), None),
        ),
        out_specs=P(("dp", "expert"), None),
        check_vma=False,
    )
```
